256 devices in a mesh: replica: 64 (over y, z, core), tensor: 4 (over x).
Axes of the slice: x: 4, y: 4, z: 8, core: 2. Of those that a mesh axis runs over, the one named last changes fastest.
Arguments:
- residual: bfloat16 [8192, 4, 5120], P('replica', None, 'tensor'), may hold values from -3 to 3
- queries: bfloat16 [8192, 4, 2560], P('replica', None, 'tensor'), may hold values from -144 to 144
- new_keys: bfloat16 [8192, 4, 512], P('replica', None, 'tensor'), may hold values from -6 to 6
- new_values: bfloat16 [8192, 4, 512], P('replica', None, 'tensor'), may hold values from -6 to 6
- cache_keys: bfloat16 [8192, 64, 512], P('replica', None, 'tensor'), may hold values from -7 to 7
- cache_values: bfloat16 [8192, 64, 512], P('replica', None, 'tensor'), may hold values from -6 to 6
- cache_lengths: int32 [8192], replicated, may hold values from 2 to 64
- finished: int32 [8192], replicated, may hold values 0 or 1
- partner: int32 [8192], P('replica'), may hold values from 0 to 8191, as said below
- row_slot: int32 [8192], replicated, may hold values from 0 to 3
- fork_table: int32 [64, 4], replicated, may hold values from 0 to 255, as said below
- prompt_keys: bfloat16 [256, 128, 512], P('replica', None, 'tensor'), may hold values from -6 to 6
- prompt_values: bfloat16 [256, 128, 512], P('replica', None, 'tensor'), may hold values from -6 to 6
- prompt_lengths: int32 [256], replicated, may hold values from 32 to 128
- out_proj: bfloat16 [2560, 5120], P('tensor'), may hold values from -0.125 to 0.125
Outputs:
- layer_out: bfloat16 [8192, 4, 5120], P('replica', None, 'tensor')
The draws below stay inside these ranges and needn't reach their ends.
Inputs may be any that keep to these rules, and one draw needn't show every extreme that they name: partner is an involution; each replica has exactly 32 rows paired with rows of 32 different other replicas, one of them the replica 64 / 2 away, and every other row is paired with itself. `fork_table`: the 4 entries of a replica name prompts of 4 different owners, prompt p being held by replica p // 4.
All inputs are finite; a program needn't handle non-finite values.
Results may differ from the reference program's by a relative error of at most 0.0034.
Values may be sent and summed in bfloat16 or wider, within the bound.
A program may use at most 128 MiB of HBM per device.

```python
import math
import jax
import jax.numpy as jnp
from jax import lax

D = 5120
HEADS = 20
KV_HEADS = 4
HEAD_DIM = 128
STEPS = 4
ROWS_DEV = 128
SUFFIX = 64
PREFIX = 128
OWN = 4
SLOTS = 4
ROWS = 8192
PROBS = 256
MOVE = 32
N_REPLICA = 64


def shuffle_rows(sub_key):
    return jax.random.permutation(sub_key, ROWS_DEV).astype(jnp.int32)


def pair_rows(key):
    first, second = jax.random.split(key)
    odd_pick = jax.random.permutation(first, N_REPLICA // 2)[:MOVE - 1].astype(jnp.int32)
    totals = 2 * odd_pick + 1
    orders = jax.vmap(shuffle_rows)(jax.random.split(second, N_REPLICA))
    replicas = jnp.arange(N_REPLICA, dtype=jnp.int32)
    half_peer = (replicas + N_REPLICA // 2) % N_REPLICA
    odd_peers = (totals[None, :] - replicas[:, None]) % N_REPLICA
    peers = jnp.concatenate([half_peer[:, None], odd_peers], axis=1).astype(jnp.int32)
    rounds = jnp.arange(MOVE, dtype=jnp.int32)
    own_rows = replicas[:, None] * ROWS_DEV + orders[:, :MOVE]
    peer_rows = peers * ROWS_DEV + orders[peers, rounds[None, :]]
    result = jnp.arange(ROWS, dtype=jnp.int32)
    return result.at[own_rows.reshape(-1)].set(peer_rows.reshape(-1))


def draw_partner(key, part):
    return pair_rows(jax.random.fold_in(key, 11))


def owner_pick(sub_key):
    return jax.random.permutation(sub_key, N_REPLICA)[:SLOTS].astype(jnp.int32)


def draw_fork_table(key, part):
    first, second, third = jax.random.split(jax.random.fold_in(key, 12), 3)
    owners = jax.vmap(owner_pick)(jax.random.split(first, N_REPLICA))
    pick_a = jax.random.randint(second, (N_REPLICA, SLOTS), 0, OWN, dtype=jnp.int32)
    pick_b = jax.random.randint(third, (N_REPLICA, SLOTS), 0, OWN, dtype=jnp.int32)
    return (owners * OWN + jnp.minimum(pick_a, pick_b)).astype(jnp.int32)


def draw_cache_lengths(key, part):
    first, second = jax.random.split(jax.random.fold_in(key, 13))
    lengths = jax.random.randint(first, (ROWS,), 2, SUFFIX + 1, dtype=jnp.int32)
    spot = jax.random.randint(second, (), 0, ROWS, dtype=jnp.int32)
    return lengths.at[spot].set(SUFFIX)


def draw_prompt_lengths(key, part):
    first, second = jax.random.split(jax.random.fold_in(key, 14))
    lengths = jax.random.randint(first, (PROBS,), PREFIX // 4, PREFIX + 1, dtype=jnp.int32)
    spot = jax.random.randint(second, (), 0, PROBS, dtype=jnp.int32)
    return lengths.at[spot].set(PREFIX)


def draw_cache_keys(key, part):
    values = jax.random.normal(jax.random.fold_in(key, 22), (ROWS, SUFFIX, KV_HEADS * HEAD_DIM), jnp.float32)
    values = jnp.clip(values, -6.0, 6.0)
    return values.astype(jnp.bfloat16)


def draw_queries(key, part):
    values = jax.random.normal(jax.random.fold_in(key, 24), (ROWS, STEPS, HEADS * HEAD_DIM), jnp.float32)
    values = jnp.clip(values, -6.0, 6.0)
    return values.astype(jnp.bfloat16)


def touch_ends(values, own_key, least, top_value):
    spot = [jax.random.randint(jax.random.fold_in(own_key, axis), (), 0, length) for axis, length in enumerate(values.shape)]
    widest = values.shape.index(max(values.shape))
    neighbour = spot[:widest] + [(spot[widest] + 1) % values.shape[widest]] + spot[widest + 1:]
    return values.at[tuple(spot)].set(least).at[tuple(neighbour)].set(top_value)


def levels(own_key, shape, pieces, smallest, top_value):
    level = 1.0
    for position, parts in pieces:
        heights = jax.random.uniform(jax.random.fold_in(jax.random.fold_in(own_key, 6), position), (parts,), jnp.float32, smallest / len(pieces), top_value / len(pieces))
        level = level * jnp.repeat(jnp.exp(heights), shape[position] // parts).reshape((-1,) + (1,) * (len(shape) - 1 - position))
    return level


def scatter_about(own_key, dims, scale, bound, cuts=(), kind=jnp.bfloat16):
    loudness = levels(own_key, dims, cuts, -0.22, 0.18) if cuts else 1.0
    values = jax.random.normal(own_key, dims, jnp.float32) * scale * loudness
    return jnp.minimum(jnp.maximum(values, -bound), bound).astype(kind)


def setup_inputs(seed: int = 0) -> dict:
    arg_keys = jax.random.split(jax.random.key(seed), 16)
    residual = scatter_about(arg_keys[0], (ROWS, STEPS, D), 0.5, 3.0, ((0, 64), (2, 4)))
    queries = draw_queries(jax.random.fold_in(arg_keys[15], 71), 0)
    new_keys = scatter_about(arg_keys[2], (ROWS, STEPS, KV_HEADS * HEAD_DIM), 1.0, 6.0, ((0, 64), (2, 4)))
    new_values = scatter_about(arg_keys[3], (ROWS, STEPS, KV_HEADS * HEAD_DIM), 1.0, 6.0, ((0, 64), (2, 4)))
    cache_keys = draw_cache_keys(jax.random.fold_in(arg_keys[15], 71), 0)
    cache_values = scatter_about(arg_keys[5], (ROWS, SUFFIX, KV_HEADS * HEAD_DIM), 1.0, 6.0, ((0, 64), (2, 4)))
    cache_lengths = draw_cache_lengths(jax.random.fold_in(arg_keys[15], 71), 0)
    finished = touch_ends((jax.random.randint(arg_keys[7], (ROWS,), 0, 4) < 1).astype(jnp.int32), jax.random.fold_in(arg_keys[7], 1), 0, 1)
    partner = draw_partner(jax.random.fold_in(arg_keys[15], 71), 0)
    row_slot = touch_ends(jax.random.randint(arg_keys[9], (ROWS,), 0, SLOTS), jax.random.fold_in(arg_keys[9], 1), 0, SLOTS - 1).astype(jnp.int32)
    fork_table = draw_fork_table(jax.random.fold_in(arg_keys[15], 71), 0)
    prompt_keys = scatter_about(arg_keys[11], (PROBS, PREFIX, KV_HEADS * HEAD_DIM), 1.0, 6.0, ((0, 64), (2, 4)))
    prompt_values = scatter_about(arg_keys[12], (PROBS, PREFIX, KV_HEADS * HEAD_DIM), 1.0, 6.0, ((0, 64), (2, 4)))
    prompt_lengths = draw_prompt_lengths(jax.random.fold_in(arg_keys[15], 71), 0)
    out_proj = scatter_about(arg_keys[14], (HEADS * HEAD_DIM, D), (HEADS * HEAD_DIM) ** -0.5, 0.125, ((0, 4),))
    return dict(residual=residual, queries=queries, new_keys=new_keys, new_values=new_values, cache_keys=cache_keys, cache_values=cache_values, cache_lengths=cache_lengths, finished=finished, partner=partner, row_slot=row_slot, fork_table=fork_table, prompt_keys=prompt_keys, prompt_values=prompt_values, prompt_lengths=prompt_lengths, out_proj=out_proj)


def split_heads(block, kv_heads):
    return block.astype(jnp.float32).reshape(block.shape[0], block.shape[1], kv_heads, HEAD_DIM)

def attend(queries, new_keys, new_values, pre_keys, pre_values, pre_len, old_keys, old_values, old_len):
    row_count, step_count = (queries.shape[0], queries.shape[1])
    kv_heads = new_keys.shape[2] // HEAD_DIM
    groups = queries.shape[2] // HEAD_DIM // kv_heads
    query_split = queries.astype(jnp.float32).reshape(row_count, step_count, kv_heads, groups, HEAD_DIM)
    score_scale = 1.0 / math.sqrt(HEAD_DIM)
    part_pre = jnp.einsum('bskgd,bpkd->bkgsp', query_split, split_heads(pre_keys, kv_heads)) * score_scale
    part_old = jnp.einsum('bskgd,bpkd->bkgsp', query_split, split_heads(old_keys, kv_heads)) * score_scale
    part_new = jnp.einsum('bskgd,btkd->bkgst', query_split, split_heads(new_keys, kv_heads)) * score_scale
    mask_pre = jnp.arange(pre_keys.shape[1], dtype=jnp.int32)[None, :] < pre_len[:, None]
    mask_old = jnp.arange(old_keys.shape[1], dtype=jnp.int32)[None, :] < old_len[:, None]
    steps_idx = jnp.arange(step_count, dtype=jnp.int32)
    mask_new = steps_idx[None, :] <= steps_idx[:, None]
    part_pre = jnp.where(mask_pre[:, None, None, None, :], part_pre, -jnp.inf)
    part_old = jnp.where(mask_old[:, None, None, None, :], part_old, -jnp.inf)
    part_new = jnp.where(mask_new[None, None, None, :, :], part_new, -jnp.inf)
    scores = jnp.concatenate([part_pre, part_old, part_new], axis=-1)
    row_top = lax.optimization_barrier(jnp.max(scores, axis=-1, keepdims=True))
    exp_scores = jnp.exp(scores - row_top)
    weights = (exp_scores / lax.optimization_barrier(jnp.sum(exp_scores, axis=-1, keepdims=True))).astype(jnp.bfloat16).astype(jnp.float32)
    len_pre = pre_keys.shape[1]
    len_old = old_keys.shape[1]
    mixed = jnp.einsum('bkgsp,bpkd->bskgd', weights[..., :len_pre], split_heads(pre_values, kv_heads))
    mixed = mixed + jnp.einsum('bkgsp,bpkd->bskgd', weights[..., len_pre:len_pre + len_old], split_heads(old_values, kv_heads))
    mixed = mixed + jnp.einsum('bkgst,btkd->bskgd', weights[..., len_pre + len_old:], split_heads(new_values, kv_heads))
    return mixed.reshape(row_count, step_count, -1)

def reference(residual, queries, new_keys, new_values, cache_keys, cache_values, cache_lengths, finished, partner, row_slot, fork_table, prompt_keys, prompt_values, prompt_lengths, out_proj):
    weight_f = out_proj.astype(jnp.float32)

    def one_block(block_id):
        first_id = block_id * ROWS_DEV
        source = lax.dynamic_slice_in_dim(partner, first_id, ROWS_DEV)
        problem = fork_table[source // ROWS_DEV, row_slot[source]]
        pre_len = prompt_lengths[problem]
        old_len = cache_lengths[source]
        alive = (1 - finished[source]).astype(jnp.float32)
        block_q = lax.dynamic_slice_in_dim(queries, first_id, ROWS_DEV)
        block_k = lax.dynamic_slice_in_dim(new_keys, first_id, ROWS_DEV)
        block_v = lax.dynamic_slice_in_dim(new_values, first_id, ROWS_DEV)
        heads_out = attend(block_q, block_k, block_v, prompt_keys[problem], prompt_values[problem], pre_len, cache_keys[source], cache_values[source], old_len)
        heads_out = (heads_out * alive[:, None, None]).astype(jnp.bfloat16)
        branch = jnp.einsum('bsh,hd->bsd', heads_out.astype(jnp.float32), weight_f)
        block_res = lax.dynamic_slice_in_dim(residual, first_id, ROWS_DEV).astype(jnp.float32)
        return (block_res + branch).astype(jnp.bfloat16)
    result = lax.map(one_block, jnp.arange(N_REPLICA, dtype=jnp.int32))
    return result.reshape(ROWS, STEPS, D)
```

```python
import math

import jax
import jax.numpy as jnp
from jax import lax
from jax.sharding import PartitionSpec as P

HEAD_DIM = 128


def attend_local(q, nk, nv, slot_keys, slot_values, slot_of_row, slot_len, old_keys, old_values, old_len):
    rows, steps = q.shape[0], q.shape[1]
    groups = q.shape[2] // HEAD_DIM
    n_slots, pre_len_max = slot_keys.shape[0], slot_keys.shape[1]
    qs = q.reshape(rows, steps * groups, HEAD_DIM)
    scale = 1.0 / math.sqrt(HEAD_DIM)
    flat_pk = slot_keys.reshape(n_slots * pre_len_max, HEAD_DIM)
    flat_pv = slot_values.reshape(n_slots * pre_len_max, HEAD_DIM)
    part_pre = (
        jnp.einsum("bqd,kd->bqk", qs, flat_pk, preferred_element_type=jnp.float32) * scale
    )
    part_old = (
        jnp.einsum("bqd,btd->bqt", qs, old_keys, preferred_element_type=jnp.float32) * scale
    )
    part_new = jnp.einsum("bqd,btd->bqt", qs, nk, preferred_element_type=jnp.float32) * scale
    key_slot = jnp.arange(n_slots * pre_len_max, dtype=jnp.int32) // pre_len_max
    key_pos = jnp.arange(n_slots * pre_len_max, dtype=jnp.int32) % pre_len_max
    mask_pre = (key_slot[None, :] == slot_of_row[:, None]) & (
        key_pos[None, :] < slot_len[key_slot][None, :]
    )
    mask_old = jnp.arange(old_keys.shape[1], dtype=jnp.int32)[None, :] < old_len[:, None]
    q_step = jnp.arange(steps * groups, dtype=jnp.int32) // groups
    mask_new = jnp.arange(steps, dtype=jnp.int32)[None, :] <= q_step[:, None]
    part_pre = jnp.where(mask_pre[:, None, :], part_pre, -jnp.inf)
    part_old = jnp.where(mask_old[:, None, :], part_old, -jnp.inf)
    part_new = jnp.where(mask_new[None, :, :], part_new, -jnp.inf)
    scores = jnp.concatenate([part_pre, part_old, part_new], axis=-1)
    row_top = jnp.max(scores, axis=-1, keepdims=True)
    exp_scores = jnp.exp(scores - row_top)
    weights = (exp_scores / jnp.sum(exp_scores, axis=-1, keepdims=True)).astype(jnp.bfloat16)
    n_pre = n_slots * pre_len_max
    n_old = old_keys.shape[1]
    mixed = jnp.einsum(
        "bqk,kd->bqd", weights[..., :n_pre], flat_pv, preferred_element_type=jnp.float32
    )
    mixed = mixed + jnp.einsum(
        "bqt,btd->bqd",
        weights[..., n_pre : n_pre + n_old],
        old_values,
        preferred_element_type=jnp.float32,
    )
    mixed = mixed + jnp.einsum(
        "bqt,btd->bqd", weights[..., n_pre + n_old :], nv, preferred_element_type=jnp.float32
    )
    return mixed.reshape(rows, steps, groups * HEAD_DIM)


def body(
    residual,
    queries,
    new_keys,
    new_values,
    cache_keys,
    cache_values,
    cache_lengths,
    finished,
    partner,
    row_slot,
    fork_table,
    prompt_keys,
    prompt_values,
    prompt_lengths,
    out_proj,
):
    local_rows = queries.shape[0]
    peer_count = lax.axis_size("replica")
    where_am = lax.axis_index("replica")
    first_id = where_am * local_rows
    held_count = prompt_keys.shape[0]

    owners = fork_table // held_count
    chosen = owners == where_am
    offsets = jnp.sum(jnp.where(chosen, fork_table % held_count, 0), axis=1)
    has_block = jnp.any(chosen, axis=1)[:, None, None]
    zero_value = jnp.zeros((), prompt_keys.dtype)
    out_keys = jnp.where(has_block, prompt_keys[offsets], zero_value)
    out_values = jnp.where(has_block, prompt_values[offsets], zero_value)
    got_keys = lax.all_to_all(out_keys, "replica", split_axis=0, concat_axis=0, tiled=True)
    got_values = lax.all_to_all(out_values, "replica", split_axis=0, concat_axis=0, tiled=True)
    my_owners = owners[where_am]
    slot_keys = got_keys[my_owners]
    slot_values = got_values[my_owners]
    slot_len = prompt_lengths[fork_table[where_am]]

    peer_of = partner // local_rows
    moved_row = peer_of != where_am
    pairing = (peer_of[None, :] == jnp.arange(peer_count, dtype=jnp.int32)[:, None]) & moved_row[
        None, :
    ]
    peer_row = jnp.sum(
        jnp.where(pairing, jnp.arange(local_rows, dtype=jnp.int32)[None, :], 0), axis=1
    )
    has_row = jnp.any(pairing, axis=1)[:, None, None]
    from_peer = jnp.where(moved_row, peer_of, 0)
    keep_mask = moved_row[:, None, None]
    packed = jnp.concatenate([queries, new_keys, new_values], axis=2)
    outgoing = jnp.where(has_row, packed[peer_row], jnp.zeros((), packed.dtype))
    received = lax.all_to_all(outgoing, "replica", split_axis=0, concat_axis=0, tiled=True)
    use_packed = jnp.where(keep_mask, received[from_peer], packed)
    q_width = queries.shape[2]
    kv_width = new_keys.shape[2]
    use_q = use_packed[..., :q_width]
    use_nk = use_packed[..., q_width : q_width + kv_width]
    use_nv = use_packed[..., q_width + kv_width :]

    own_ids = first_id + jnp.arange(local_rows, dtype=jnp.int32)
    slot_of_row = row_slot[own_ids]
    old_len = cache_lengths[own_ids]
    alive = (1 - finished[own_ids]).astype(jnp.float32)
    result = attend_local(
        use_q,
        use_nk,
        use_nv,
        slot_keys,
        slot_values,
        slot_of_row,
        slot_len,
        cache_keys,
        cache_values,
        old_len,
    )
    cache_side = (result * alive[:, None, None]).astype(jnp.bfloat16)

    back = jnp.where(has_row, cache_side[peer_row], jnp.zeros((), cache_side.dtype))
    returned = lax.all_to_all(back, "replica", split_axis=0, concat_axis=0, tiled=True)
    heads_out = jnp.where(keep_mask, returned[from_peer], cache_side)

    terms = jnp.einsum("bsh,hd->bsd", heads_out, out_proj, preferred_element_type=jnp.float32)
    summed = lax.psum_scatter(terms, "tensor", scatter_dimension=2, tiled=True)
    return (residual.astype(jnp.float32) + summed).astype(jnp.bfloat16)


def solution(mesh):
    in_specs = (
        P("replica", None, "tensor"),
        P("replica", None, "tensor"),
        P("replica", None, "tensor"),
        P("replica", None, "tensor"),
        P("replica", None, "tensor"),
        P("replica", None, "tensor"),
        P(),
        P(),
        P("replica"),
        P(),
        P(),
        P("replica", None, "tensor"),
        P("replica", None, "tensor"),
        P(),
        P("tensor", None),
    )
    out_specs = P("replica", None, "tensor")
    return jax.shard_map(body, mesh=mesh, in_specs=in_specs, out_specs=out_specs, check_vma=False)
```

```python
import math

import jax
import jax.numpy as jnp
from jax import lax
from jax.sharding import PartitionSpec as P

HEAD_DIM = 128


def attend_local(q, nk, nv, slot_keys, slot_values, slot_of_row, slot_len, old_keys, old_values, old_len):
    rows, steps = q.shape[0], q.shape[1]
    groups = q.shape[2] // HEAD_DIM
    n_slots, pre_len_max = slot_keys.shape[0], slot_keys.shape[1]
    qs = q.reshape(rows, steps * groups, HEAD_DIM)
    scale = 1.0 / math.sqrt(HEAD_DIM)
    flat_pk = slot_keys.reshape(n_slots * pre_len_max, HEAD_DIM)
    flat_pv = slot_values.reshape(n_slots * pre_len_max, HEAD_DIM)
    part_pre = (
        jnp.einsum("bqd,kd->bqk", qs, flat_pk, preferred_element_type=jnp.float32) * scale
    )
    part_old = (
        jnp.einsum("bqd,btd->bqt", qs, old_keys, preferred_element_type=jnp.float32) * scale
    )
    part_new = jnp.einsum("bqd,btd->bqt", qs, nk, preferred_element_type=jnp.float32) * scale
    key_slot = jnp.arange(n_slots * pre_len_max, dtype=jnp.int32) // pre_len_max
    key_pos = jnp.arange(n_slots * pre_len_max, dtype=jnp.int32) % pre_len_max
    mask_pre = (key_slot[None, :] == slot_of_row[:, None]) & (
        key_pos[None, :] < slot_len[key_slot][None, :]
    )
    mask_old = jnp.arange(old_keys.shape[1], dtype=jnp.int32)[None, :] < old_len[:, None]
    q_step = jnp.arange(steps * groups, dtype=jnp.int32) // groups
    mask_new = jnp.arange(steps, dtype=jnp.int32)[None, :] <= q_step[:, None]
    part_pre = jnp.where(mask_pre[:, None, :], part_pre, -jnp.inf)
    part_old = jnp.where(mask_old[:, None, :], part_old, -jnp.inf)
    part_new = jnp.where(mask_new[None, :, :], part_new, -jnp.inf)
    scores = jnp.concatenate([part_pre, part_old, part_new], axis=-1)
    row_top = jnp.max(scores, axis=-1, keepdims=True)
    exp_scores = jnp.exp(scores - row_top)
    weights = (exp_scores / jnp.sum(exp_scores, axis=-1, keepdims=True)).astype(jnp.bfloat16)
    n_pre = n_slots * pre_len_max
    n_old = old_keys.shape[1]
    mixed = jnp.einsum(
        "bqk,kd->bqd", weights[..., :n_pre], flat_pv, preferred_element_type=jnp.float32
    )
    mixed = mixed + jnp.einsum(
        "bqt,btd->bqd",
        weights[..., n_pre : n_pre + n_old],
        old_values,
        preferred_element_type=jnp.float32,
    )
    mixed = mixed + jnp.einsum(
        "bqt,btd->bqd", weights[..., n_pre + n_old :], nv, preferred_element_type=jnp.float32
    )
    return mixed.reshape(rows, steps, groups * HEAD_DIM)


def body(
    residual,
    queries,
    new_keys,
    new_values,
    cache_keys,
    cache_values,
    cache_lengths,
    finished,
    partner,
    row_slot,
    fork_table,
    prompt_keys,
    prompt_values,
    prompt_lengths,
    out_proj,
):
    local_rows = queries.shape[0]
    peer_count = lax.axis_size("replica")
    where_am = lax.axis_index("replica")
    first_id = where_am * local_rows
    held_count = prompt_keys.shape[0]

    owners = fork_table // held_count
    chosen = owners == where_am
    offsets = jnp.sum(jnp.where(chosen, fork_table % held_count, 0), axis=1)
    has_block = jnp.any(chosen, axis=1)[:, None, None]
    zero_value = jnp.zeros((), prompt_keys.dtype)
    both = jnp.concatenate([prompt_keys, prompt_values], axis=2)
    out_both = jnp.where(has_block, both[offsets], zero_value)
    got_both = lax.all_to_all(out_both, "replica", split_axis=0, concat_axis=0, tiled=True)
    my_owners = owners[where_am]
    slot_both = got_both[my_owners]
    slot_keys = slot_both[..., : prompt_keys.shape[2]]
    slot_values = slot_both[..., prompt_keys.shape[2] :]
    slot_len = prompt_lengths[fork_table[where_am]]

    peer_of = partner // local_rows
    moved_row = peer_of != where_am
    pairing = (peer_of[None, :] == jnp.arange(peer_count, dtype=jnp.int32)[:, None]) & moved_row[
        None, :
    ]
    peer_row = jnp.sum(
        jnp.where(pairing, jnp.arange(local_rows, dtype=jnp.int32)[None, :], 0), axis=1
    )
    has_row = jnp.any(pairing, axis=1)[:, None, None]
    from_peer = jnp.where(moved_row, peer_of, 0)
    keep_mask = moved_row[:, None, None]
    packed = jnp.concatenate([queries, new_keys, new_values], axis=2)
    outgoing = jnp.where(has_row, packed[peer_row], jnp.zeros((), packed.dtype))
    received = lax.all_to_all(outgoing, "replica", split_axis=0, concat_axis=0, tiled=True)
    use_packed = jnp.where(keep_mask, received[from_peer], packed)
    q_width = queries.shape[2]
    kv_width = new_keys.shape[2]
    use_q = use_packed[..., :q_width]
    use_nk = use_packed[..., q_width : q_width + kv_width]
    use_nv = use_packed[..., q_width + kv_width :]

    own_ids = first_id + jnp.arange(local_rows, dtype=jnp.int32)
    slot_of_row = row_slot[own_ids]
    old_len = cache_lengths[own_ids]
    alive = (1 - finished[own_ids]).astype(jnp.float32)
    result = attend_local(
        use_q,
        use_nk,
        use_nv,
        slot_keys,
        slot_values,
        slot_of_row,
        slot_len,
        cache_keys,
        cache_values,
        old_len,
    )
    cache_side = (result * alive[:, None, None]).astype(jnp.bfloat16)

    back = jnp.where(has_row, cache_side[peer_row], jnp.zeros((), cache_side.dtype))
    returned = lax.all_to_all(back, "replica", split_axis=0, concat_axis=0, tiled=True)
    heads_out = jnp.where(keep_mask, returned[from_peer], cache_side)

    terms = jnp.einsum("bsh,hd->bsd", heads_out, out_proj, preferred_element_type=jnp.float32)
    terms = terms.astype(jnp.bfloat16)
    summed = lax.psum_scatter(terms, "tensor", scatter_dimension=2, tiled=True)
    return (residual.astype(jnp.float32) + summed.astype(jnp.float32)).astype(jnp.bfloat16)


def solution(mesh):
    in_specs = (
        P("replica", None, "tensor"),
        P("replica", None, "tensor"),
        P("replica", None, "tensor"),
        P("replica", None, "tensor"),
        P("replica", None, "tensor"),
        P("replica", None, "tensor"),
        P(),
        P(),
        P("replica"),
        P(),
        P(),
        P("replica", None, "tensor"),
        P("replica", None, "tensor"),
        P(),
        P("tensor", None),
    )
    out_specs = P("replica", None, "tensor")
    return jax.shard_map(body, mesh=mesh, in_specs=in_specs, out_specs=out_specs, check_vma=False)
```

```python
import math

import jax
import jax.numpy as jnp
from jax import lax
import functools

from jax.experimental import pallas as pl
from jax.experimental.pallas import tpu as pltpu
from jax.sharding import PartitionSpec as P

HEAD_DIM = 128
MESH = pl.DeviceIdType.MESH


def exchange_kernel(
    n_rep, n_ten, p_send, q_send, w_ref, p_recv, q_recv, w_recv,
    p_ssem, p_rsem, q_ssem, q_rsem, w_ssem, w_rsem, l_sem,
):
    me = lax.axis_index("replica")
    mt = lax.axis_index("tensor")
    width = w_recv.shape[2]
    barrier = pltpu.get_barrier_semaphore()

    def greet_replica(k, carry):
        j = lax.rem(me + k, n_rep)
        pl.semaphore_signal(barrier, inc=1, device_id=(j, mt), device_id_type=MESH)
        return carry

    def greet_tensor(k, carry):
        t = lax.rem(mt + k, n_ten)
        pl.semaphore_signal(barrier, inc=1, device_id=(me, t), device_id_type=MESH)
        return carry

    lax.fori_loop(1, n_rep, greet_replica, 0)
    lax.fori_loop(1, n_ten, greet_tensor, 0)
    pl.semaphore_wait(barrier, n_rep - 1 + n_ten - 1)

    def w_cols(t):
        return w_ref.at[:, pl.ds(pl.multiple_of(t * width, width), width)]

    def w_out(t):
        return pltpu.make_async_remote_copy(
            src_ref=w_cols(t), dst_ref=w_recv.at[mt], send_sem=w_ssem.at[t],
            recv_sem=w_rsem.at[mt], device_id=(me, t), device_id_type=MESH)

    def w_in(t):
        return pltpu.make_async_remote_copy(
            src_ref=w_cols(t), dst_ref=w_recv.at[t], send_sem=w_ssem.at[t],
            recv_sem=w_rsem.at[t], device_id=(me, t), device_id_type=MESH)

    def p_out(j):
        return pltpu.make_async_remote_copy(
            src_ref=p_send.at[j], dst_ref=p_recv.at[me], send_sem=p_ssem.at[j],
            recv_sem=p_rsem.at[me], device_id=(j, mt), device_id_type=MESH)

    def p_in(j):
        return pltpu.make_async_remote_copy(
            src_ref=p_send.at[j], dst_ref=p_recv.at[j], send_sem=p_ssem.at[j],
            recv_sem=p_rsem.at[j], device_id=(j, mt), device_id_type=MESH)

    def q_out(j):
        return pltpu.make_async_remote_copy(
            src_ref=q_send.at[j], dst_ref=q_recv.at[me], send_sem=q_ssem.at[j],
            recv_sem=q_rsem.at[me], device_id=(j, mt), device_id_type=MESH)

    def q_in(j):
        return pltpu.make_async_remote_copy(
            src_ref=q_send.at[j], dst_ref=q_recv.at[j], send_sem=q_ssem.at[j],
            recv_sem=q_rsem.at[j], device_id=(j, mt), device_id_type=MESH)

    own_w = pltpu.make_async_copy(w_cols(mt), w_recv.at[mt], l_sem.at[0])
    own_q = pltpu.make_async_copy(q_send.at[me], q_recv.at[me], l_sem.at[1])
    own_p = pltpu.make_async_copy(p_send.at[me], p_recv.at[me], l_sem.at[2])
    own_w.start()
    own_q.start()
    own_p.start()

    def start_tensor(k, carry):
        w_out(lax.rem(mt + k, n_ten)).start()
        return carry

    def start_replica(k, carry):
        j = lax.rem(me + k, n_rep)
        q_out(j).start()
        p_out(j).start()
        return carry

    lax.fori_loop(1, n_ten, start_tensor, 0)
    lax.fori_loop(1, n_rep, start_replica, 0)

    def wait_replica(k, carry):
        j = lax.rem(me + k, n_rep)
        q_out(j).wait_send()
        q_in(j).wait_recv()
        p_out(j).wait_send()
        p_in(j).wait_recv()
        return carry

    def wait_tensor(k, carry):
        t = lax.rem(mt + k, n_ten)
        w_out(t).wait_send()
        w_in(t).wait_recv()
        return carry

    lax.fori_loop(1, n_rep, wait_replica, 0)
    lax.fori_loop(1, n_ten, wait_tensor, 0)
    own_w.wait()
    own_q.wait()
    own_p.wait()


def exchange(p_send, q_send, w, n_rep, n_ten):
    width = w.shape[1] // n_ten
    any_spec = pl.BlockSpec(memory_space=pl.ANY)
    return pl.pallas_call(
        functools.partial(exchange_kernel, n_rep, n_ten),
        out_shape=(
            jax.ShapeDtypeStruct(p_send.shape, p_send.dtype),
            jax.ShapeDtypeStruct(q_send.shape, q_send.dtype),
            jax.ShapeDtypeStruct((n_ten, w.shape[0], width), w.dtype),
        ),
        in_specs=[any_spec] * 3,
        out_specs=(any_spec, any_spec, any_spec),
        scratch_shapes=[
            pltpu.SemaphoreType.DMA((n_rep,)),
            pltpu.SemaphoreType.DMA((n_rep,)),
            pltpu.SemaphoreType.DMA((n_rep,)),
            pltpu.SemaphoreType.DMA((n_rep,)),
            pltpu.SemaphoreType.DMA((n_ten,)),
            pltpu.SemaphoreType.DMA((n_ten,)),
            pltpu.SemaphoreType.DMA((3,)),
        ],
        compiler_params=pltpu.CompilerParams(collective_id=0, has_side_effects=True),
    )(p_send, q_send, w)


def attend_local(q, nk, nv, slot_keys, slot_values, slot_of_row, slot_len, old_keys, old_values, old_len):
    rows, steps = q.shape[0], q.shape[1]
    groups = q.shape[2] // HEAD_DIM
    n_slots, pre_len_max = slot_keys.shape[0], slot_keys.shape[1]
    qs = q.reshape(rows, steps * groups, HEAD_DIM)
    scale = 1.0 / math.sqrt(HEAD_DIM)
    flat_pk = slot_keys.reshape(n_slots * pre_len_max, HEAD_DIM)
    flat_pv = slot_values.reshape(n_slots * pre_len_max, HEAD_DIM)
    part_pre = (
        jnp.einsum("bqd,kd->bqk", qs, flat_pk, preferred_element_type=jnp.float32) * scale
    )
    part_old = (
        jnp.einsum("bqd,btd->bqt", qs, old_keys, preferred_element_type=jnp.float32) * scale
    )
    part_new = jnp.einsum("bqd,btd->bqt", qs, nk, preferred_element_type=jnp.float32) * scale
    key_slot = jnp.arange(n_slots * pre_len_max, dtype=jnp.int32) // pre_len_max
    key_pos = jnp.arange(n_slots * pre_len_max, dtype=jnp.int32) % pre_len_max
    mask_pre = (key_slot[None, :] == slot_of_row[:, None]) & (
        key_pos[None, :] < slot_len[key_slot][None, :]
    )
    mask_old = jnp.arange(old_keys.shape[1], dtype=jnp.int32)[None, :] < old_len[:, None]
    q_step = jnp.arange(steps * groups, dtype=jnp.int32) // groups
    mask_new = jnp.arange(steps, dtype=jnp.int32)[None, :] <= q_step[:, None]
    part_pre = jnp.where(mask_pre[:, None, :], part_pre, -jnp.inf)
    part_old = jnp.where(mask_old[:, None, :], part_old, -jnp.inf)
    part_new = jnp.where(mask_new[None, :, :], part_new, -jnp.inf)
    scores = jnp.concatenate([part_pre, part_old, part_new], axis=-1)
    row_top = jnp.max(scores, axis=-1, keepdims=True)
    exp_scores = jnp.exp(scores - row_top)
    weights = (exp_scores / jnp.sum(exp_scores, axis=-1, keepdims=True)).astype(jnp.bfloat16)
    n_pre = n_slots * pre_len_max
    n_old = old_keys.shape[1]
    mixed = jnp.einsum(
        "bqk,kd->bqd", weights[..., :n_pre], flat_pv, preferred_element_type=jnp.float32
    )
    mixed = mixed + jnp.einsum(
        "bqt,btd->bqd",
        weights[..., n_pre : n_pre + n_old],
        old_values,
        preferred_element_type=jnp.float32,
    )
    mixed = mixed + jnp.einsum(
        "bqt,btd->bqd", weights[..., n_pre + n_old :], nv, preferred_element_type=jnp.float32
    )
    return mixed.reshape(rows, steps, groups * HEAD_DIM)


def body(
    residual,
    queries,
    new_keys,
    new_values,
    cache_keys,
    cache_values,
    cache_lengths,
    finished,
    partner,
    row_slot,
    fork_table,
    prompt_keys,
    prompt_values,
    prompt_lengths,
    out_proj,
):
    local_rows = queries.shape[0]
    peer_count = lax.axis_size("replica")
    where_am = lax.axis_index("replica")
    first_id = where_am * local_rows
    held_count = prompt_keys.shape[0]

    owners = fork_table // held_count
    chosen = owners == where_am
    offsets = jnp.sum(jnp.where(chosen, fork_table % held_count, 0), axis=1)
    has_block = jnp.any(chosen, axis=1)[:, None, None]
    zero_value = jnp.zeros((), prompt_keys.dtype)
    both = jnp.concatenate([prompt_keys, prompt_values], axis=2)
    out_both = jnp.where(has_block, both[offsets], zero_value)

    peer_of = partner // local_rows
    moved_row = peer_of != where_am
    pairing = (peer_of[None, :] == jnp.arange(peer_count, dtype=jnp.int32)[:, None]) & moved_row[
        None, :
    ]
    peer_row = jnp.sum(
        jnp.where(pairing, jnp.arange(local_rows, dtype=jnp.int32)[None, :], 0), axis=1
    )
    has_row = jnp.any(pairing, axis=1)[:, None, None]
    from_peer = jnp.where(moved_row, peer_of, 0)
    keep_mask = moved_row[:, None, None]
    packed = jnp.concatenate([queries, new_keys, new_values], axis=2)
    outgoing = jnp.where(has_row, packed[peer_row], jnp.zeros((), packed.dtype))
    got_both, received, proj_blocks = exchange(
        out_both, outgoing, out_proj, peer_count, lax.axis_size("tensor")
    )
    proj_cols = proj_blocks.reshape(-1, proj_blocks.shape[2])
    my_owners = owners[where_am]
    slot_both = got_both[my_owners]
    slot_keys = slot_both[..., : prompt_keys.shape[2]]
    slot_values = slot_both[..., prompt_keys.shape[2] :]
    slot_len = prompt_lengths[fork_table[where_am]]
    use_packed = jnp.where(keep_mask, received[from_peer], packed)
    q_width = queries.shape[2]
    kv_width = new_keys.shape[2]
    use_q = use_packed[..., :q_width]
    use_nk = use_packed[..., q_width : q_width + kv_width]
    use_nv = use_packed[..., q_width + kv_width :]

    own_ids = first_id + jnp.arange(local_rows, dtype=jnp.int32)
    slot_of_row = row_slot[own_ids]
    old_len = cache_lengths[own_ids]
    alive = (1 - finished[own_ids]).astype(jnp.float32)
    result = attend_local(
        use_q,
        use_nk,
        use_nv,
        slot_keys,
        slot_values,
        slot_of_row,
        slot_len,
        cache_keys,
        cache_values,
        old_len,
    )
    cache_side = (result * alive[:, None, None]).astype(jnp.bfloat16)

    back = jnp.where(has_row, cache_side[peer_row], jnp.zeros((), cache_side.dtype))
    returned = lax.all_to_all(back, "replica", split_axis=0, concat_axis=0, tiled=True)
    heads_out = jnp.where(keep_mask, returned[from_peer], cache_side)

    all_heads = lax.all_gather(heads_out, "tensor", axis=2, tiled=True)
    summed = jnp.einsum("bsh,hd->bsd", all_heads, proj_cols, preferred_element_type=jnp.float32)
    return (residual.astype(jnp.float32) + summed).astype(jnp.bfloat16)


def solution(mesh):
    in_specs = (
        P("replica", None, "tensor"),
        P("replica", None, "tensor"),
        P("replica", None, "tensor"),
        P("replica", None, "tensor"),
        P("replica", None, "tensor"),
        P("replica", None, "tensor"),
        P(),
        P(),
        P("replica"),
        P(),
        P(),
        P("replica", None, "tensor"),
        P("replica", None, "tensor"),
        P(),
        P("tensor", None),
    )
    out_specs = P("replica", None, "tensor")
    return jax.shard_map(body, mesh=mesh, in_specs=in_specs, out_specs=out_specs, check_vma=False)
```

```python
import math

import jax
import jax.numpy as jnp
from jax import lax
import functools

from jax.experimental import pallas as pl
from jax.experimental.pallas import tpu as pltpu
from jax.sharding import PartitionSpec as P

HEAD_DIM = 128
MESH = pl.DeviceIdType.MESH


def exchange_kernel(
    n_rep, n_ten, p_send, q_send, w_ref, p_recv, q_recv, w_recv,
    p_ssem, p_rsem, q_ssem, q_rsem, w_ssem, w_rsem, l_sem,
):
    me = lax.axis_index("replica")
    mt = lax.axis_index("tensor")
    width = w_recv.shape[2]
    barrier = pltpu.get_barrier_semaphore()

    def greet_replica(k, carry):
        j = lax.rem(me + k, n_rep)
        pl.semaphore_signal(barrier, inc=1, device_id=(j, mt), device_id_type=MESH)
        return carry

    def greet_tensor(k, carry):
        t = lax.rem(mt + k, n_ten)
        pl.semaphore_signal(barrier, inc=1, device_id=(me, t), device_id_type=MESH)
        return carry

    lax.fori_loop(1, n_rep, greet_replica, 0)
    lax.fori_loop(1, n_ten, greet_tensor, 0)
    pl.semaphore_wait(barrier, n_rep - 1 + n_ten - 1)

    def w_cols(t):
        return w_ref.at[t]

    def w_out(t):
        return pltpu.make_async_remote_copy(
            src_ref=w_cols(t), dst_ref=w_recv.at[mt], send_sem=w_ssem.at[t],
            recv_sem=w_rsem.at[mt], device_id=(me, t), device_id_type=MESH)

    def w_in(t):
        return pltpu.make_async_remote_copy(
            src_ref=w_cols(t), dst_ref=w_recv.at[t], send_sem=w_ssem.at[t],
            recv_sem=w_rsem.at[t], device_id=(me, t), device_id_type=MESH)

    def p_out(j):
        return pltpu.make_async_remote_copy(
            src_ref=p_send.at[j], dst_ref=p_recv.at[me], send_sem=p_ssem.at[j],
            recv_sem=p_rsem.at[me], device_id=(j, mt), device_id_type=MESH)

    def p_in(j):
        return pltpu.make_async_remote_copy(
            src_ref=p_send.at[j], dst_ref=p_recv.at[j], send_sem=p_ssem.at[j],
            recv_sem=p_rsem.at[j], device_id=(j, mt), device_id_type=MESH)

    def q_out(j):
        return pltpu.make_async_remote_copy(
            src_ref=q_send.at[j], dst_ref=q_recv.at[me], send_sem=q_ssem.at[j],
            recv_sem=q_rsem.at[me], device_id=(j, mt), device_id_type=MESH)

    def q_in(j):
        return pltpu.make_async_remote_copy(
            src_ref=q_send.at[j], dst_ref=q_recv.at[j], send_sem=q_ssem.at[j],
            recv_sem=q_rsem.at[j], device_id=(j, mt), device_id_type=MESH)

    own_w = pltpu.make_async_copy(w_cols(mt), w_recv.at[mt], l_sem.at[0])
    own_q = pltpu.make_async_copy(q_send.at[me], q_recv.at[me], l_sem.at[1])
    own_p = pltpu.make_async_copy(p_send.at[me], p_recv.at[me], l_sem.at[2])
    own_q.start()
    own_p.start()
    own_w.start()

    def start_tensor(k, carry):
        w_out(lax.rem(mt + k, n_ten)).start()
        return carry

    def start_replica(k, carry):
        j = lax.rem(me + k, n_rep)
        q_out(j).start()
        p_out(j).start()
        return carry

    lax.fori_loop(1, n_rep, start_replica, 0)
    lax.fori_loop(1, n_ten, start_tensor, 0)

    def wait_replica(k, carry):
        j = lax.rem(me + k, n_rep)
        q_out(j).wait_send()
        q_in(j).wait_recv()
        p_out(j).wait_send()
        p_in(j).wait_recv()
        return carry

    def wait_tensor(k, carry):
        t = lax.rem(mt + k, n_ten)
        w_out(t).wait_send()
        w_in(t).wait_recv()
        return carry

    lax.fori_loop(1, n_rep, wait_replica, 0)
    lax.fori_loop(1, n_ten, wait_tensor, 0)
    own_w.wait()
    own_q.wait()
    own_p.wait()


def exchange(p_send, q_send, w, n_rep, n_ten):
    width = w.shape[2]
    any_spec = pl.BlockSpec(memory_space=pl.ANY)
    return pl.pallas_call(
        functools.partial(exchange_kernel, n_rep, n_ten),
        out_shape=(
            jax.ShapeDtypeStruct(p_send.shape, p_send.dtype),
            jax.ShapeDtypeStruct(q_send.shape, q_send.dtype),
            jax.ShapeDtypeStruct(w.shape, w.dtype),
        ),
        in_specs=[any_spec] * 3,
        out_specs=(any_spec, any_spec, any_spec),
        scratch_shapes=[
            pltpu.SemaphoreType.DMA((n_rep,)),
            pltpu.SemaphoreType.DMA((n_rep,)),
            pltpu.SemaphoreType.DMA((n_rep,)),
            pltpu.SemaphoreType.DMA((n_rep,)),
            pltpu.SemaphoreType.DMA((n_ten,)),
            pltpu.SemaphoreType.DMA((n_ten,)),
            pltpu.SemaphoreType.DMA((3,)),
        ],
        compiler_params=pltpu.CompilerParams(collective_id=0, has_side_effects=True),
    )(p_send, q_send, w)


def attend_local(q, nk, nv, slot_keys, slot_values, slot_of_row, slot_len, old_keys, old_values, old_len):
    rows, steps = q.shape[0], q.shape[1]
    groups = q.shape[2] // HEAD_DIM
    n_slots, pre_len_max = slot_keys.shape[0], slot_keys.shape[1]
    qs = q.reshape(rows, steps * groups, HEAD_DIM)
    scale = 1.0 / math.sqrt(HEAD_DIM)
    flat_pk = slot_keys.reshape(n_slots * pre_len_max, HEAD_DIM)
    flat_pv = slot_values.reshape(n_slots * pre_len_max, HEAD_DIM)
    part_pre = (
        jnp.einsum("bqd,kd->bqk", qs, flat_pk, preferred_element_type=jnp.float32) * scale
    )
    part_old = (
        jnp.einsum("bqd,btd->bqt", qs, old_keys, preferred_element_type=jnp.float32) * scale
    )
    part_new = jnp.einsum("bqd,btd->bqt", qs, nk, preferred_element_type=jnp.float32) * scale
    key_slot = jnp.arange(n_slots * pre_len_max, dtype=jnp.int32) // pre_len_max
    key_pos = jnp.arange(n_slots * pre_len_max, dtype=jnp.int32) % pre_len_max
    mask_pre = (key_slot[None, :] == slot_of_row[:, None]) & (
        key_pos[None, :] < slot_len[key_slot][None, :]
    )
    mask_old = jnp.arange(old_keys.shape[1], dtype=jnp.int32)[None, :] < old_len[:, None]
    q_step = jnp.arange(steps * groups, dtype=jnp.int32) // groups
    mask_new = jnp.arange(steps, dtype=jnp.int32)[None, :] <= q_step[:, None]
    part_pre = jnp.where(mask_pre[:, None, :], part_pre, -jnp.inf)
    part_old = jnp.where(mask_old[:, None, :], part_old, -jnp.inf)
    part_new = jnp.where(mask_new[None, :, :], part_new, -jnp.inf)
    scores = jnp.concatenate([part_pre, part_old, part_new], axis=-1)
    row_top = jnp.max(scores, axis=-1, keepdims=True)
    exp_scores = jnp.exp(scores - row_top)
    weights = (exp_scores / jnp.sum(exp_scores, axis=-1, keepdims=True)).astype(jnp.bfloat16)
    n_pre = n_slots * pre_len_max
    n_old = old_keys.shape[1]
    mixed = jnp.einsum(
        "bqk,kd->bqd", weights[..., :n_pre], flat_pv, preferred_element_type=jnp.float32
    )
    mixed = mixed + jnp.einsum(
        "bqt,btd->bqd",
        weights[..., n_pre : n_pre + n_old],
        old_values,
        preferred_element_type=jnp.float32,
    )
    mixed = mixed + jnp.einsum(
        "bqt,btd->bqd", weights[..., n_pre + n_old :], nv, preferred_element_type=jnp.float32
    )
    return mixed.reshape(rows, steps, groups * HEAD_DIM)


def gather_kernel(n_ten, h_ref, h_all, s_sem, r_sem, l_sem):
    mt = lax.axis_index("tensor")
    me = lax.axis_index("replica")
    barrier = pltpu.get_barrier_semaphore()

    def greet(k, carry):
        t = lax.rem(mt + k, n_ten)
        pl.semaphore_signal(barrier, inc=1, device_id=(me, t), device_id_type=MESH)
        return carry

    lax.fori_loop(1, n_ten, greet, 0)
    pl.semaphore_wait(barrier, n_ten - 1)

    def h_out(t):
        return pltpu.make_async_remote_copy(
            src_ref=h_ref, dst_ref=h_all.at[mt], send_sem=s_sem.at[t],
            recv_sem=r_sem.at[mt], device_id=(me, t), device_id_type=MESH)

    def h_in(t):
        return pltpu.make_async_remote_copy(
            src_ref=h_ref, dst_ref=h_all.at[t], send_sem=s_sem.at[t],
            recv_sem=r_sem.at[t], device_id=(me, t), device_id_type=MESH)

    own = pltpu.make_async_copy(h_ref, h_all.at[mt], l_sem.at[0])
    own.start()

    def start(k, carry):
        h_out(lax.rem(mt + k, n_ten)).start()
        return carry

    def wait(k, carry):
        t = lax.rem(mt + k, n_ten)
        h_out(t).wait_send()
        h_in(t).wait_recv()
        return carry

    lax.fori_loop(1, n_ten, start, 0)
    lax.fori_loop(1, n_ten, wait, 0)
    own.wait()


def gather_heads(h, n_ten):
    any_spec = pl.BlockSpec(memory_space=pl.ANY)
    return pl.pallas_call(
        functools.partial(gather_kernel, n_ten),
        out_shape=jax.ShapeDtypeStruct((n_ten,) + h.shape, h.dtype),
        in_specs=[any_spec],
        out_specs=any_spec,
        scratch_shapes=[
            pltpu.SemaphoreType.DMA((n_ten,)),
            pltpu.SemaphoreType.DMA((n_ten,)),
            pltpu.SemaphoreType.DMA((1,)),
        ],
        compiler_params=pltpu.CompilerParams(collective_id=1, has_side_effects=True),
    )(h)


def body(
    residual,
    queries,
    new_keys,
    new_values,
    cache_keys,
    cache_values,
    cache_lengths,
    finished,
    partner,
    row_slot,
    fork_table,
    prompt_keys,
    prompt_values,
    prompt_lengths,
    out_proj,
):
    local_rows = queries.shape[0]
    peer_count = lax.axis_size("replica")
    where_am = lax.axis_index("replica")
    first_id = where_am * local_rows
    held_count = prompt_keys.shape[0]

    owners = fork_table // held_count
    chosen = owners == where_am
    offsets = jnp.sum(jnp.where(chosen, fork_table % held_count, 0), axis=1)
    has_block = jnp.any(chosen, axis=1)[:, None, None]
    zero_value = jnp.zeros((), prompt_keys.dtype)
    both = jnp.concatenate([prompt_keys, prompt_values], axis=2)
    out_both = jnp.where(has_block, both[offsets], zero_value)

    peer_of = partner // local_rows
    moved_row = peer_of != where_am
    pairing = (peer_of[None, :] == jnp.arange(peer_count, dtype=jnp.int32)[:, None]) & moved_row[
        None, :
    ]
    peer_row = jnp.sum(
        jnp.where(pairing, jnp.arange(local_rows, dtype=jnp.int32)[None, :], 0), axis=1
    )
    has_row = jnp.any(pairing, axis=1)[:, None, None]
    from_peer = jnp.where(moved_row, peer_of, 0)
    keep_mask = moved_row[:, None, None]
    packed = jnp.concatenate([queries, new_keys, new_values], axis=2)
    outgoing = jnp.where(has_row, packed[peer_row], jnp.zeros((), packed.dtype))
    n_ten = lax.axis_size("tensor")
    w_blocks = out_proj.reshape(out_proj.shape[0], n_ten, -1).transpose(1, 0, 2)
    got_both, received, proj_blocks = exchange(out_both, outgoing, w_blocks, peer_count, n_ten)
    my_owners = owners[where_am]
    slot_both = got_both[my_owners]
    slot_keys = slot_both[..., : prompt_keys.shape[2]]
    slot_values = slot_both[..., prompt_keys.shape[2] :]
    slot_len = prompt_lengths[fork_table[where_am]]
    use_packed = jnp.where(keep_mask, received[from_peer], packed)
    q_width = queries.shape[2]
    kv_width = new_keys.shape[2]
    use_q = use_packed[..., :q_width]
    use_nk = use_packed[..., q_width : q_width + kv_width]
    use_nv = use_packed[..., q_width + kv_width :]

    own_ids = first_id + jnp.arange(local_rows, dtype=jnp.int32)
    slot_of_row = row_slot[own_ids]
    old_len = cache_lengths[own_ids]
    alive = (1 - finished[own_ids]).astype(jnp.float32)
    result = attend_local(
        use_q,
        use_nk,
        use_nv,
        slot_keys,
        slot_values,
        slot_of_row,
        slot_len,
        cache_keys,
        cache_values,
        old_len,
    )
    cache_side = (result * alive[:, None, None]).astype(jnp.bfloat16)

    back = jnp.where(has_row, cache_side[peer_row], jnp.zeros((), cache_side.dtype))
    returned = lax.all_to_all(back, "replica", split_axis=0, concat_axis=0, tiled=True)
    heads_out = jnp.where(keep_mask, returned[from_peer], cache_side)

    all_heads = gather_heads(heads_out, n_ten)
    summed = jnp.einsum(
        "tbsh,thd->bsd", all_heads, proj_blocks, preferred_element_type=jnp.float32
    )
    return (residual.astype(jnp.float32) + summed).astype(jnp.bfloat16)


def solution(mesh):
    in_specs = (
        P("replica", None, "tensor"),
        P("replica", None, "tensor"),
        P("replica", None, "tensor"),
        P("replica", None, "tensor"),
        P("replica", None, "tensor"),
        P("replica", None, "tensor"),
        P(),
        P(),
        P("replica"),
        P(),
        P(),
        P("replica", None, "tensor"),
        P("replica", None, "tensor"),
        P(),
        P("tensor", None),
    )
    out_specs = P("replica", None, "tensor")
    return jax.shard_map(body, mesh=mesh, in_specs=in_specs, out_specs=out_specs, check_vma=False)
```

```python
import math

import jax
import jax.numpy as jnp
from jax import lax
import functools

from jax.experimental import pallas as pl
from jax.experimental.pallas import tpu as pltpu
from jax.sharding import PartitionSpec as P

HEAD_DIM = 128
MESH = pl.DeviceIdType.MESH


def exchange_kernel(n_rep, p_send, q_send, p_recv, q_recv, p_ssem, p_rsem, q_ssem, q_rsem, l_sem):
    me = lax.axis_index("replica")
    mt = lax.axis_index("tensor")
    barrier = pltpu.get_barrier_semaphore()

    def greet_replica(k, carry):
        j = lax.rem(me + k, n_rep)
        pl.semaphore_signal(barrier, inc=1, device_id=(j, mt), device_id_type=MESH)
        return carry

    lax.fori_loop(1, n_rep, greet_replica, 0)
    pl.semaphore_wait(barrier, n_rep - 1)

    def p_out(j):
        return pltpu.make_async_remote_copy(
            src_ref=p_send.at[j], dst_ref=p_recv.at[me], send_sem=p_ssem.at[j],
            recv_sem=p_rsem.at[me], device_id=(j, mt), device_id_type=MESH)

    def p_in(j):
        return pltpu.make_async_remote_copy(
            src_ref=p_send.at[j], dst_ref=p_recv.at[j], send_sem=p_ssem.at[j],
            recv_sem=p_rsem.at[j], device_id=(j, mt), device_id_type=MESH)

    def q_out(j):
        return pltpu.make_async_remote_copy(
            src_ref=q_send.at[j], dst_ref=q_recv.at[me], send_sem=q_ssem.at[j],
            recv_sem=q_rsem.at[me], device_id=(j, mt), device_id_type=MESH)

    def q_in(j):
        return pltpu.make_async_remote_copy(
            src_ref=q_send.at[j], dst_ref=q_recv.at[j], send_sem=q_ssem.at[j],
            recv_sem=q_rsem.at[j], device_id=(j, mt), device_id_type=MESH)

    own_q = pltpu.make_async_copy(q_send.at[me], q_recv.at[me], l_sem.at[0])
    own_p = pltpu.make_async_copy(p_send.at[me], p_recv.at[me], l_sem.at[1])
    own_q.start()
    own_p.start()

    def start_replica(k, carry):
        j = lax.rem(me + k, n_rep)
        q_out(j).start()
        p_out(j).start()
        return carry

    def wait_replica(k, carry):
        j = lax.rem(me + k, n_rep)
        q_out(j).wait_send()
        q_in(j).wait_recv()
        p_out(j).wait_send()
        p_in(j).wait_recv()
        return carry

    lax.fori_loop(1, n_rep, start_replica, 0)
    lax.fori_loop(1, n_rep, wait_replica, 0)
    own_q.wait()
    own_p.wait()


def exchange(p_send, q_send, n_rep):
    any_spec = pl.BlockSpec(memory_space=pl.ANY)
    return pl.pallas_call(
        functools.partial(exchange_kernel, n_rep),
        out_shape=(
            jax.ShapeDtypeStruct(p_send.shape, p_send.dtype),
            jax.ShapeDtypeStruct(q_send.shape, q_send.dtype),
        ),
        in_specs=[any_spec] * 2,
        out_specs=(any_spec, any_spec),
        scratch_shapes=[
            pltpu.SemaphoreType.DMA((n_rep,)),
            pltpu.SemaphoreType.DMA((n_rep,)),
            pltpu.SemaphoreType.DMA((n_rep,)),
            pltpu.SemaphoreType.DMA((n_rep,)),
            pltpu.SemaphoreType.DMA((2,)),
        ],
        compiler_params=pltpu.CompilerParams(collective_id=0, has_side_effects=True),
    )(p_send, q_send)


def attend_local(q, nk, nv, slot_keys, slot_values, slot_of_row, slot_len, old_keys, old_values, old_len):
    rows, steps = q.shape[0], q.shape[1]
    groups = q.shape[2] // HEAD_DIM
    n_slots, pre_len_max = slot_keys.shape[0], slot_keys.shape[1]
    qs = q.reshape(rows, steps * groups, HEAD_DIM)
    scale = 1.0 / math.sqrt(HEAD_DIM)
    flat_pk = slot_keys.reshape(n_slots * pre_len_max, HEAD_DIM)
    flat_pv = slot_values.reshape(n_slots * pre_len_max, HEAD_DIM)
    part_pre = (
        jnp.einsum("bqd,kd->bqk", qs, flat_pk, preferred_element_type=jnp.float32) * scale
    )
    part_old = (
        jnp.einsum("bqd,btd->bqt", qs, old_keys, preferred_element_type=jnp.float32) * scale
    )
    part_new = jnp.einsum("bqd,btd->bqt", qs, nk, preferred_element_type=jnp.float32) * scale
    key_slot = jnp.arange(n_slots * pre_len_max, dtype=jnp.int32) // pre_len_max
    key_pos = jnp.arange(n_slots * pre_len_max, dtype=jnp.int32) % pre_len_max
    mask_pre = (key_slot[None, :] == slot_of_row[:, None]) & (
        key_pos[None, :] < slot_len[key_slot][None, :]
    )
    mask_old = jnp.arange(old_keys.shape[1], dtype=jnp.int32)[None, :] < old_len[:, None]
    q_step = jnp.arange(steps * groups, dtype=jnp.int32) // groups
    mask_new = jnp.arange(steps, dtype=jnp.int32)[None, :] <= q_step[:, None]
    part_pre = jnp.where(mask_pre[:, None, :], part_pre, -jnp.inf)
    part_old = jnp.where(mask_old[:, None, :], part_old, -jnp.inf)
    part_new = jnp.where(mask_new[None, :, :], part_new, -jnp.inf)
    scores = jnp.concatenate([part_pre, part_old, part_new], axis=-1)
    row_top = jnp.max(scores, axis=-1, keepdims=True)
    exp_scores = jnp.exp(scores - row_top)
    weights = (exp_scores / jnp.sum(exp_scores, axis=-1, keepdims=True)).astype(jnp.bfloat16)
    n_pre = n_slots * pre_len_max
    n_old = old_keys.shape[1]
    mixed = jnp.einsum(
        "bqk,kd->bqd", weights[..., :n_pre], flat_pv, preferred_element_type=jnp.float32
    )
    mixed = mixed + jnp.einsum(
        "bqt,btd->bqd",
        weights[..., n_pre : n_pre + n_old],
        old_values,
        preferred_element_type=jnp.float32,
    )
    mixed = mixed + jnp.einsum(
        "bqt,btd->bqd", weights[..., n_pre + n_old :], nv, preferred_element_type=jnp.float32
    )
    return mixed.reshape(rows, steps, groups * HEAD_DIM)


def body(
    residual,
    queries,
    new_keys,
    new_values,
    cache_keys,
    cache_values,
    cache_lengths,
    finished,
    partner,
    row_slot,
    fork_table,
    prompt_keys,
    prompt_values,
    prompt_lengths,
    out_proj,
):
    local_rows = queries.shape[0]
    peer_count = lax.axis_size("replica")
    where_am = lax.axis_index("replica")
    first_id = where_am * local_rows
    held_count = prompt_keys.shape[0]

    owners = fork_table // held_count
    chosen = owners == where_am
    offsets = jnp.sum(jnp.where(chosen, fork_table % held_count, 0), axis=1)
    has_block = jnp.any(chosen, axis=1)[:, None, None]
    zero_value = jnp.zeros((), prompt_keys.dtype)
    both = jnp.concatenate([prompt_keys, prompt_values], axis=2)
    out_both = jnp.where(has_block, both[offsets], zero_value)

    peer_of = partner // local_rows
    moved_row = peer_of != where_am
    pairing = (peer_of[None, :] == jnp.arange(peer_count, dtype=jnp.int32)[:, None]) & moved_row[
        None, :
    ]
    peer_row = jnp.sum(
        jnp.where(pairing, jnp.arange(local_rows, dtype=jnp.int32)[None, :], 0), axis=1
    )
    has_row = jnp.any(pairing, axis=1)[:, None, None]
    from_peer = jnp.where(moved_row, peer_of, 0)
    keep_mask = moved_row[:, None, None]
    packed = jnp.concatenate([queries, new_keys, new_values], axis=2)
    outgoing = jnp.where(has_row, packed[peer_row], jnp.zeros((), packed.dtype))
    got_both, received = exchange(out_both, outgoing, peer_count)
    my_owners = owners[where_am]
    slot_both = got_both[my_owners]
    slot_keys = slot_both[..., : prompt_keys.shape[2]]
    slot_values = slot_both[..., prompt_keys.shape[2] :]
    slot_len = prompt_lengths[fork_table[where_am]]
    use_packed = jnp.where(keep_mask, received[from_peer], packed)
    q_width = queries.shape[2]
    kv_width = new_keys.shape[2]
    use_q = use_packed[..., :q_width]
    use_nk = use_packed[..., q_width : q_width + kv_width]
    use_nv = use_packed[..., q_width + kv_width :]

    own_ids = first_id + jnp.arange(local_rows, dtype=jnp.int32)
    slot_of_row = row_slot[own_ids]
    old_len = cache_lengths[own_ids]
    alive = (1 - finished[own_ids]).astype(jnp.float32)
    result = attend_local(
        use_q,
        use_nk,
        use_nv,
        slot_keys,
        slot_values,
        slot_of_row,
        slot_len,
        cache_keys,
        cache_values,
        old_len,
    )
    cache_side = (result * alive[:, None, None]).astype(jnp.bfloat16)

    back = jnp.where(has_row, cache_side[peer_row], jnp.zeros((), cache_side.dtype))
    returned = lax.all_to_all(back, "replica", split_axis=0, concat_axis=0, tiled=True)
    heads_out = jnp.where(keep_mask, returned[from_peer], cache_side)

    terms = jnp.einsum("bsh,hd->bsd", heads_out, out_proj, preferred_element_type=jnp.float32)
    terms = terms.astype(jnp.bfloat16)
    summed = lax.psum_scatter(terms, "tensor", scatter_dimension=2, tiled=True)
    return (residual.astype(jnp.float32) + summed.astype(jnp.float32)).astype(jnp.bfloat16)


def solution(mesh):
    in_specs = (
        P("replica", None, "tensor"),
        P("replica", None, "tensor"),
        P("replica", None, "tensor"),
        P("replica", None, "tensor"),
        P("replica", None, "tensor"),
        P("replica", None, "tensor"),
        P(),
        P(),
        P("replica"),
        P(),
        P(),
        P("replica", None, "tensor"),
        P("replica", None, "tensor"),
        P(),
        P("tensor", None),
    )
    out_specs = P("replica", None, "tensor")
    return jax.shard_map(body, mesh=mesh, in_specs=in_specs, out_specs=out_specs, check_vma=False)
```

```python
import math

import jax
import jax.numpy as jnp
from jax import lax
from jax.sharding import PartitionSpec as P

HEAD_DIM = 128


def attend_local(q, nk, nv, slot_keys, slot_values, slot_of_row, slot_len, old_keys, old_values, old_len):
    rows, steps = q.shape[0], q.shape[1]
    groups = q.shape[2] // HEAD_DIM
    n_slots, pre_len_max = slot_keys.shape[0], slot_keys.shape[1]
    qs = q.reshape(rows, steps * groups, HEAD_DIM)
    scale = 1.0 / math.sqrt(HEAD_DIM)
    flat_pk = slot_keys.reshape(n_slots * pre_len_max, HEAD_DIM)
    flat_pv = slot_values.reshape(n_slots * pre_len_max, HEAD_DIM)
    part_pre = (
        jnp.einsum("bqd,kd->bqk", qs, flat_pk, preferred_element_type=jnp.float32) * scale
    )
    part_old = (
        jnp.einsum("bqd,btd->bqt", qs, old_keys, preferred_element_type=jnp.float32) * scale
    )
    part_new = jnp.einsum("bqd,btd->bqt", qs, nk, preferred_element_type=jnp.float32) * scale
    key_slot = jnp.arange(n_slots * pre_len_max, dtype=jnp.int32) // pre_len_max
    key_pos = jnp.arange(n_slots * pre_len_max, dtype=jnp.int32) % pre_len_max
    mask_pre = (key_slot[None, :] == slot_of_row[:, None]) & (
        key_pos[None, :] < slot_len[key_slot][None, :]
    )
    mask_old = jnp.arange(old_keys.shape[1], dtype=jnp.int32)[None, :] < old_len[:, None]
    q_step = jnp.arange(steps * groups, dtype=jnp.int32) // groups
    mask_new = jnp.arange(steps, dtype=jnp.int32)[None, :] <= q_step[:, None]
    part_pre = jnp.where(mask_pre[:, None, :], part_pre, -jnp.inf)
    part_old = jnp.where(mask_old[:, None, :], part_old, -jnp.inf)
    part_new = jnp.where(mask_new[None, :, :], part_new, -jnp.inf)
    scores = jnp.concatenate([part_pre, part_old, part_new], axis=-1)
    row_top = jnp.max(scores, axis=-1, keepdims=True)
    exp_scores = jnp.exp(scores - row_top)
    weights = (exp_scores / jnp.sum(exp_scores, axis=-1, keepdims=True)).astype(jnp.bfloat16)
    n_pre = n_slots * pre_len_max
    n_old = old_keys.shape[1]
    mixed = jnp.einsum(
        "bqk,kd->bqd", weights[..., :n_pre], flat_pv, preferred_element_type=jnp.float32
    )
    mixed = mixed + jnp.einsum(
        "bqt,btd->bqd",
        weights[..., n_pre : n_pre + n_old],
        old_values,
        preferred_element_type=jnp.float32,
    )
    mixed = mixed + jnp.einsum(
        "bqt,btd->bqd", weights[..., n_pre + n_old :], nv, preferred_element_type=jnp.float32
    )
    return mixed.reshape(rows, steps, groups * HEAD_DIM)


def body(
    residual,
    queries,
    new_keys,
    new_values,
    cache_keys,
    cache_values,
    cache_lengths,
    finished,
    partner,
    row_slot,
    fork_table,
    prompt_keys,
    prompt_values,
    prompt_lengths,
    out_proj,
):
    local_rows = queries.shape[0]
    peer_count = lax.axis_size("replica")
    where_am = lax.axis_index("replica")
    first_id = where_am * local_rows
    held_count = prompt_keys.shape[0]

    owners = fork_table // held_count
    chosen = owners == where_am
    offsets = jnp.sum(jnp.where(chosen, fork_table % held_count, 0), axis=1)
    has_block = jnp.any(chosen, axis=1)[:, None, None]
    zero_value = jnp.zeros((), prompt_keys.dtype)
    both = jnp.concatenate([prompt_keys, prompt_values], axis=2)
    out_both = jnp.where(has_block, both[offsets], zero_value)

    peer_of = partner // local_rows
    moved_row = peer_of != where_am
    pairing = (peer_of[None, :] == jnp.arange(peer_count, dtype=jnp.int32)[:, None]) & moved_row[
        None, :
    ]
    peer_row = jnp.sum(
        jnp.where(pairing, jnp.arange(local_rows, dtype=jnp.int32)[None, :], 0), axis=1
    )
    has_row = jnp.any(pairing, axis=1)[:, None, None]
    from_peer = jnp.where(moved_row, peer_of, 0)
    keep_mask = moved_row[:, None, None]
    packed = jnp.concatenate([queries, new_keys, new_values], axis=2)
    outgoing = jnp.where(has_row, packed[peer_row], jnp.zeros((), packed.dtype))
    prompt_size = out_both[0].size
    joined = jnp.concatenate(
        [out_both.reshape(peer_count, -1), outgoing.reshape(peer_count, -1)], axis=1
    )
    arrived = lax.all_to_all(joined, "replica", split_axis=0, concat_axis=0, tiled=True)
    got_both = arrived[:, :prompt_size].reshape(out_both.shape)
    received = arrived[:, prompt_size:].reshape(outgoing.shape)
    my_owners = owners[where_am]
    slot_both = got_both[my_owners]
    slot_keys = slot_both[..., : prompt_keys.shape[2]]
    slot_values = slot_both[..., prompt_keys.shape[2] :]
    slot_len = prompt_lengths[fork_table[where_am]]
    use_packed = jnp.where(keep_mask, received[from_peer], packed)
    q_width = queries.shape[2]
    kv_width = new_keys.shape[2]
    use_q = use_packed[..., :q_width]
    use_nk = use_packed[..., q_width : q_width + kv_width]
    use_nv = use_packed[..., q_width + kv_width :]

    own_ids = first_id + jnp.arange(local_rows, dtype=jnp.int32)
    slot_of_row = row_slot[own_ids]
    old_len = cache_lengths[own_ids]
    alive = (1 - finished[own_ids]).astype(jnp.float32)
    result = attend_local(
        use_q,
        use_nk,
        use_nv,
        slot_keys,
        slot_values,
        slot_of_row,
        slot_len,
        cache_keys,
        cache_values,
        old_len,
    )
    cache_side = (result * alive[:, None, None]).astype(jnp.bfloat16)

    back = jnp.where(has_row, cache_side[peer_row], jnp.zeros((), cache_side.dtype))
    returned = lax.all_to_all(back, "replica", split_axis=0, concat_axis=0, tiled=True)
    heads_out = jnp.where(keep_mask, returned[from_peer], cache_side)

    terms = jnp.einsum("bsh,hd->bsd", heads_out, out_proj, preferred_element_type=jnp.float32)
    terms = terms.astype(jnp.bfloat16)
    summed = lax.psum_scatter(terms, "tensor", scatter_dimension=2, tiled=True)
    return (residual.astype(jnp.float32) + summed.astype(jnp.float32)).astype(jnp.bfloat16)


def solution(mesh):
    in_specs = (
        P("replica", None, "tensor"),
        P("replica", None, "tensor"),
        P("replica", None, "tensor"),
        P("replica", None, "tensor"),
        P("replica", None, "tensor"),
        P("replica", None, "tensor"),
        P(),
        P(),
        P("replica"),
        P(),
        P(),
        P("replica", None, "tensor"),
        P("replica", None, "tensor"),
        P(),
        P("tensor", None),
    )
    out_specs = P("replica", None, "tensor")
    return jax.shard_map(body, mesh=mesh, in_specs=in_specs, out_specs=out_specs, check_vma=False)
```

```python
import math

import jax
import jax.numpy as jnp
from jax import lax
import functools

from jax.experimental import pallas as pl
from jax.sharding import PartitionSpec as P

HEAD_DIM = 128


def attend_local(q, nk, nv, slot_keys, slot_values, slot_of_row, slot_len, old_keys, old_values, old_len):
    rows, steps = q.shape[0], q.shape[1]
    groups = q.shape[2] // HEAD_DIM
    n_slots, pre_len_max = slot_keys.shape[0], slot_keys.shape[1]
    qs = q.reshape(rows, steps * groups, HEAD_DIM)
    scale = 1.0 / math.sqrt(HEAD_DIM)
    flat_pk = slot_keys.reshape(n_slots * pre_len_max, HEAD_DIM)
    flat_pv = slot_values.reshape(n_slots * pre_len_max, HEAD_DIM)
    part_pre = (
        jnp.einsum("bqd,kd->bqk", qs, flat_pk, preferred_element_type=jnp.float32) * scale
    )
    part_old = (
        jnp.einsum("bqd,btd->bqt", qs, old_keys, preferred_element_type=jnp.float32) * scale
    )
    part_new = jnp.einsum("bqd,btd->bqt", qs, nk, preferred_element_type=jnp.float32) * scale
    key_slot = jnp.arange(n_slots * pre_len_max, dtype=jnp.int32) // pre_len_max
    key_pos = jnp.arange(n_slots * pre_len_max, dtype=jnp.int32) % pre_len_max
    mask_pre = (key_slot[None, :] == slot_of_row[:, None]) & (
        key_pos[None, :] < slot_len[key_slot][None, :]
    )
    mask_old = jnp.arange(old_keys.shape[1], dtype=jnp.int32)[None, :] < old_len[:, None]
    q_step = jnp.arange(steps * groups, dtype=jnp.int32) // groups
    mask_new = jnp.arange(steps, dtype=jnp.int32)[None, :] <= q_step[:, None]
    part_pre = jnp.where(mask_pre[:, None, :], part_pre, -jnp.inf)
    part_old = jnp.where(mask_old[:, None, :], part_old, -jnp.inf)
    part_new = jnp.where(mask_new[None, :, :], part_new, -jnp.inf)
    scores = jnp.concatenate([part_pre, part_old, part_new], axis=-1)
    row_top = jnp.max(scores, axis=-1, keepdims=True)
    exp_scores = jnp.exp(scores - row_top)
    weights = (exp_scores / jnp.sum(exp_scores, axis=-1, keepdims=True)).astype(jnp.bfloat16)
    n_pre = n_slots * pre_len_max
    n_old = old_keys.shape[1]
    mixed = jnp.einsum(
        "bqk,kd->bqd", weights[..., :n_pre], flat_pv, preferred_element_type=jnp.float32
    )
    mixed = mixed + jnp.einsum(
        "bqt,btd->bqd",
        weights[..., n_pre : n_pre + n_old],
        old_values,
        preferred_element_type=jnp.float32,
    )
    mixed = mixed + jnp.einsum(
        "bqt,btd->bqd", weights[..., n_pre + n_old :], nv, preferred_element_type=jnp.float32
    )
    return mixed.reshape(rows, steps, groups * HEAD_DIM)


def attn_kernel(scale, q_ref, meta_ref, pk_ref, pv_ref, ck_ref, cv_ref, nk_ref, nv_ref, o_ref):
    q = q_ref[...]
    meta = meta_ref[...]
    dims = (((1,), (1,)), ((), ()))

    def masked(keys, lo, hi):
        s = lax.dot_general(q, keys, dims, preferred_element_type=jnp.float32) * scale
        k = lax.broadcasted_iota(jnp.int32, s.shape, 1)
        return jnp.where((k >= lo) & (k < hi), s, -jnp.inf)

    s_pre = masked(pk_ref[...], meta[:, 0:1], meta[:, 1:2])
    s_old = masked(ck_ref[...], meta[:, 2:3], meta[:, 3:4])
    s_new = masked(nk_ref[...], meta[:, 4:5], meta[:, 5:6])
    top = jnp.maximum(
        jnp.maximum(jnp.max(s_pre, axis=1, keepdims=True), jnp.max(s_old, axis=1, keepdims=True)),
        jnp.max(s_new, axis=1, keepdims=True),
    )
    e_pre = jnp.exp(s_pre - top)
    e_old = jnp.exp(s_old - top)
    e_new = jnp.exp(s_new - top)
    total = (
        jnp.sum(e_pre, axis=1, keepdims=True)
        + jnp.sum(e_old, axis=1, keepdims=True)
        + jnp.sum(e_new, axis=1, keepdims=True)
    )
    w_pre = (e_pre / total).astype(jnp.bfloat16)
    w_old = (e_old / total).astype(jnp.bfloat16)
    w_new = (e_new / total).astype(jnp.bfloat16)
    out = jnp.dot(w_pre, pv_ref[...], preferred_element_type=jnp.float32)
    out = out + jnp.dot(w_old, cv_ref[...], preferred_element_type=jnp.float32)
    out = out + jnp.dot(w_new, nv_ref[...], preferred_element_type=jnp.float32)
    alive = meta[:, 6:7].astype(jnp.float32)
    o_ref[...] = (out * alive).astype(o_ref.dtype)


def attend_kernel_call(q2, meta, pk, pv, ck2, cv2, nk2, nv2, rows_per_block, q_per_row, old_per_row, new_per_row):
    n_q, width = q2.shape
    qb = rows_per_block * q_per_row
    ob = rows_per_block * old_per_row
    nb = rows_per_block * new_per_row
    full = lambda i: (0, 0)
    return pl.pallas_call(
        functools.partial(attn_kernel, 1.0 / math.sqrt(HEAD_DIM)),
        out_shape=jax.ShapeDtypeStruct((n_q, width), jnp.bfloat16),
        grid=(n_q // qb,),
        in_specs=[
            pl.BlockSpec((qb, width), lambda i: (i, 0)),
            pl.BlockSpec((qb, meta.shape[1]), lambda i: (i, 0)),
            pl.BlockSpec(pk.shape, full),
            pl.BlockSpec(pv.shape, full),
            pl.BlockSpec((ob, width), lambda i: (i, 0)),
            pl.BlockSpec((ob, width), lambda i: (i, 0)),
            pl.BlockSpec((nb, width), lambda i: (i, 0)),
            pl.BlockSpec((nb, width), lambda i: (i, 0)),
        ],
        out_specs=pl.BlockSpec((qb, width), lambda i: (i, 0)),
    )(q2, meta, pk, pv, ck2, cv2, nk2, nv2)


def attend_fused(q, nk, nv, slot_keys, slot_values, slot_of_row, slot_len, old_keys, old_values, old_len, alive, rows_per_block=8):
    rows, steps = q.shape[0], q.shape[1]
    groups = q.shape[2] // HEAD_DIM
    n_slots, pre_max = slot_keys.shape[0], slot_keys.shape[1]
    old_max = old_keys.shape[1]
    local = jnp.arange(rows, dtype=jnp.int32) % rows_per_block
    lo_pre = slot_of_row * pre_max
    hi_pre = lo_pre + slot_len[slot_of_row]
    lo_old = local * old_max
    hi_old = lo_old + old_len
    lo_new = local * steps
    step_id = jnp.arange(steps * groups, dtype=jnp.int32) // groups
    per_row = jnp.stack([lo_pre, hi_pre, lo_old, hi_old, lo_new, alive, alive, alive], axis=1)
    meta = jnp.broadcast_to(per_row[:, None, :], (rows, steps * groups, 8))
    hi_new = lo_new[:, None] + step_id[None, :] + 1
    meta = meta.at[:, :, 5].set(hi_new)
    meta = meta.reshape(rows * steps * groups, 8)
    out = attend_kernel_call(
        q.reshape(rows * steps * groups, HEAD_DIM),
        meta,
        slot_keys.reshape(n_slots * pre_max, HEAD_DIM),
        slot_values.reshape(n_slots * pre_max, HEAD_DIM),
        old_keys.reshape(rows * old_max, HEAD_DIM),
        old_values.reshape(rows * old_max, HEAD_DIM),
        nk.reshape(rows * steps, HEAD_DIM),
        nv.reshape(rows * steps, HEAD_DIM),
        rows_per_block, steps * groups, old_max, steps,
    )
    return out.reshape(rows, steps, groups * HEAD_DIM)


def body(
    residual,
    queries,
    new_keys,
    new_values,
    cache_keys,
    cache_values,
    cache_lengths,
    finished,
    partner,
    row_slot,
    fork_table,
    prompt_keys,
    prompt_values,
    prompt_lengths,
    out_proj,
):
    local_rows = queries.shape[0]
    peer_count = lax.axis_size("replica")
    where_am = lax.axis_index("replica")
    first_id = where_am * local_rows
    held_count = prompt_keys.shape[0]

    owners = fork_table // held_count
    chosen = owners == where_am
    offsets = jnp.sum(jnp.where(chosen, fork_table % held_count, 0), axis=1)
    has_block = jnp.any(chosen, axis=1)[:, None, None]
    zero_value = jnp.zeros((), prompt_keys.dtype)
    both = jnp.concatenate([prompt_keys, prompt_values], axis=2)
    out_both = jnp.where(has_block, both[offsets], zero_value)
    got_both = lax.all_to_all(out_both, "replica", split_axis=0, concat_axis=0, tiled=True)
    my_owners = owners[where_am]
    slot_both = got_both[my_owners]
    slot_keys = slot_both[..., : prompt_keys.shape[2]]
    slot_values = slot_both[..., prompt_keys.shape[2] :]
    slot_len = prompt_lengths[fork_table[where_am]]

    peer_of = partner // local_rows
    moved_row = peer_of != where_am
    pairing = (peer_of[None, :] == jnp.arange(peer_count, dtype=jnp.int32)[:, None]) & moved_row[
        None, :
    ]
    peer_row = jnp.sum(
        jnp.where(pairing, jnp.arange(local_rows, dtype=jnp.int32)[None, :], 0), axis=1
    )
    has_row = jnp.any(pairing, axis=1)[:, None, None]
    from_peer = jnp.where(moved_row, peer_of, 0)
    keep_mask = moved_row[:, None, None]
    packed = jnp.concatenate([queries, new_keys, new_values], axis=2)
    outgoing = jnp.where(has_row, packed[peer_row], jnp.zeros((), packed.dtype))
    received = lax.all_to_all(outgoing, "replica", split_axis=0, concat_axis=0, tiled=True)
    use_packed = jnp.where(keep_mask, received[from_peer], packed)
    q_width = queries.shape[2]
    kv_width = new_keys.shape[2]
    use_q = use_packed[..., :q_width]
    use_nk = use_packed[..., q_width : q_width + kv_width]
    use_nv = use_packed[..., q_width + kv_width :]

    own_ids = first_id + jnp.arange(local_rows, dtype=jnp.int32)
    slot_of_row = row_slot[own_ids]
    old_len = cache_lengths[own_ids]
    alive = 1 - finished[own_ids]
    cache_side = attend_fused(
        use_q,
        use_nk,
        use_nv,
        slot_keys,
        slot_values,
        slot_of_row,
        slot_len,
        cache_keys,
        cache_values,
        old_len,
        alive,
    )

    back = jnp.where(has_row, cache_side[peer_row], jnp.zeros((), cache_side.dtype))
    returned = lax.all_to_all(back, "replica", split_axis=0, concat_axis=0, tiled=True)
    heads_out = jnp.where(keep_mask, returned[from_peer], cache_side)

    terms = jnp.einsum("bsh,hd->bsd", heads_out, out_proj, preferred_element_type=jnp.float32)
    terms = terms.astype(jnp.bfloat16)
    summed = lax.psum_scatter(terms, "tensor", scatter_dimension=2, tiled=True)
    return (residual.astype(jnp.float32) + summed.astype(jnp.float32)).astype(jnp.bfloat16)


def solution(mesh):
    in_specs = (
        P("replica", None, "tensor"),
        P("replica", None, "tensor"),
        P("replica", None, "tensor"),
        P("replica", None, "tensor"),
        P("replica", None, "tensor"),
        P("replica", None, "tensor"),
        P(),
        P(),
        P("replica"),
        P(),
        P(),
        P("replica", None, "tensor"),
        P("replica", None, "tensor"),
        P(),
        P("tensor", None),
    )
    out_specs = P("replica", None, "tensor")
    return jax.shard_map(body, mesh=mesh, in_specs=in_specs, out_specs=out_specs, check_vma=False)
```

```python
import math

import jax
import jax.numpy as jnp
from jax import lax
import functools

from jax.experimental import pallas as pl
from jax.experimental.pallas import tpu as pltpu
from jax.sharding import PartitionSpec as P

HEAD_DIM = 128
MESH = pl.DeviceIdType.MESH


def attend_local(q, nk, nv, slot_keys, slot_values, slot_of_row, slot_len, old_keys, old_values, old_len):
    rows, steps = q.shape[0], q.shape[1]
    groups = q.shape[2] // HEAD_DIM
    n_slots, pre_len_max = slot_keys.shape[0], slot_keys.shape[1]
    qs = q.reshape(rows, steps * groups, HEAD_DIM)
    scale = 1.0 / math.sqrt(HEAD_DIM)
    flat_pk = slot_keys.reshape(n_slots * pre_len_max, HEAD_DIM)
    flat_pv = slot_values.reshape(n_slots * pre_len_max, HEAD_DIM)
    part_pre = (
        jnp.einsum("bqd,kd->bqk", qs, flat_pk, preferred_element_type=jnp.float32) * scale
    )
    part_old = (
        jnp.einsum("bqd,btd->bqt", qs, old_keys, preferred_element_type=jnp.float32) * scale
    )
    part_new = jnp.einsum("bqd,btd->bqt", qs, nk, preferred_element_type=jnp.float32) * scale
    key_slot = jnp.arange(n_slots * pre_len_max, dtype=jnp.int32) // pre_len_max
    key_pos = jnp.arange(n_slots * pre_len_max, dtype=jnp.int32) % pre_len_max
    mask_pre = (key_slot[None, :] == slot_of_row[:, None]) & (
        key_pos[None, :] < slot_len[key_slot][None, :]
    )
    mask_old = jnp.arange(old_keys.shape[1], dtype=jnp.int32)[None, :] < old_len[:, None]
    q_step = jnp.arange(steps * groups, dtype=jnp.int32) // groups
    mask_new = jnp.arange(steps, dtype=jnp.int32)[None, :] <= q_step[:, None]
    part_pre = jnp.where(mask_pre[:, None, :], part_pre, -jnp.inf)
    part_old = jnp.where(mask_old[:, None, :], part_old, -jnp.inf)
    part_new = jnp.where(mask_new[None, :, :], part_new, -jnp.inf)
    scores = jnp.concatenate([part_pre, part_old, part_new], axis=-1)
    row_top = jnp.max(scores, axis=-1, keepdims=True)
    exp_scores = jnp.exp(scores - row_top)
    weights = (exp_scores / jnp.sum(exp_scores, axis=-1, keepdims=True)).astype(jnp.bfloat16)
    n_pre = n_slots * pre_len_max
    n_old = old_keys.shape[1]
    mixed = jnp.einsum(
        "bqk,kd->bqd", weights[..., :n_pre], flat_pv, preferred_element_type=jnp.float32
    )
    mixed = mixed + jnp.einsum(
        "bqt,btd->bqd",
        weights[..., n_pre : n_pre + n_old],
        old_values,
        preferred_element_type=jnp.float32,
    )
    mixed = mixed + jnp.einsum(
        "bqt,btd->bqd", weights[..., n_pre + n_old :], nv, preferred_element_type=jnp.float32
    )
    return mixed.reshape(rows, steps, groups * HEAD_DIM)


def swap_kernel(n_rep, send, recv, s_sem, r_sem, l_sem):
    me = lax.axis_index("replica")
    mt = lax.axis_index("tensor")
    barrier = pltpu.get_barrier_semaphore()

    def greet(k, carry):
        j = lax.rem(me + k, n_rep)
        pl.semaphore_signal(barrier, inc=1, device_id=(j, mt), device_id_type=MESH)
        return carry

    lax.fori_loop(1, n_rep, greet, 0)
    pl.semaphore_wait(barrier, n_rep - 1)

    def out_copy(j):
        return pltpu.make_async_remote_copy(
            src_ref=send.at[j], dst_ref=recv.at[me], send_sem=s_sem.at[j],
            recv_sem=r_sem.at[me], device_id=(j, mt), device_id_type=MESH)

    def in_copy(j):
        return pltpu.make_async_remote_copy(
            src_ref=send.at[j], dst_ref=recv.at[j], send_sem=s_sem.at[j],
            recv_sem=r_sem.at[j], device_id=(j, mt), device_id_type=MESH)

    own = pltpu.make_async_copy(send.at[me], recv.at[me], l_sem.at[0])
    own.start()

    def start(k, carry):
        out_copy(lax.rem(me + k, n_rep)).start()
        return carry

    def wait(k, carry):
        j = lax.rem(me + k, n_rep)
        out_copy(j).wait_send()
        in_copy(j).wait_recv()
        return carry

    lax.fori_loop(1, n_rep, start, 0)
    lax.fori_loop(1, n_rep, wait, 0)
    own.wait()


def swap_rows(send, n_rep, cid):
    any_spec = pl.BlockSpec(memory_space=pl.ANY)
    return pl.pallas_call(
        functools.partial(swap_kernel, n_rep),
        out_shape=jax.ShapeDtypeStruct(send.shape, send.dtype),
        in_specs=[any_spec],
        out_specs=any_spec,
        scratch_shapes=[
            pltpu.SemaphoreType.DMA((n_rep,)),
            pltpu.SemaphoreType.DMA((n_rep,)),
            pltpu.SemaphoreType.DMA((1,)),
        ],
        compiler_params=pltpu.CompilerParams(collective_id=cid, has_side_effects=True),
    )(send)


def attn_kernel(scale, q_ref, meta_ref, pk_ref, pv_ref, ck_ref, cv_ref, nk_ref, nv_ref, o_ref):
    q = q_ref[...]
    meta = meta_ref[...]
    dims = (((1,), (1,)), ((), ()))

    def masked(keys, lo, hi):
        s = lax.dot_general(q, keys, dims, preferred_element_type=jnp.float32) * scale
        k = lax.broadcasted_iota(jnp.int32, s.shape, 1)
        return jnp.where((k >= lo) & (k < hi), s, -jnp.inf)

    s_pre = masked(pk_ref[...], meta[:, 0:1], meta[:, 1:2])
    s_old = masked(ck_ref[...], meta[:, 2:3], meta[:, 3:4])
    s_new = masked(nk_ref[...], meta[:, 4:5], meta[:, 5:6])
    top = jnp.maximum(
        jnp.maximum(jnp.max(s_pre, axis=1, keepdims=True), jnp.max(s_old, axis=1, keepdims=True)),
        jnp.max(s_new, axis=1, keepdims=True),
    )
    e_pre = jnp.exp(s_pre - top)
    e_old = jnp.exp(s_old - top)
    e_new = jnp.exp(s_new - top)
    total = (
        jnp.sum(e_pre, axis=1, keepdims=True)
        + jnp.sum(e_old, axis=1, keepdims=True)
        + jnp.sum(e_new, axis=1, keepdims=True)
    )
    w_pre = (e_pre / total).astype(jnp.bfloat16)
    w_old = (e_old / total).astype(jnp.bfloat16)
    w_new = (e_new / total).astype(jnp.bfloat16)
    out = jnp.dot(w_pre, pv_ref[...], preferred_element_type=jnp.float32)
    out = out + jnp.dot(w_old, cv_ref[...], preferred_element_type=jnp.float32)
    out = out + jnp.dot(w_new, nv_ref[...], preferred_element_type=jnp.float32)
    alive = meta[:, 6:7].astype(jnp.float32)
    o_ref[...] = (out * alive).astype(o_ref.dtype)


def attend_kernel_call(q2, meta, pk, pv, ck2, cv2, nk2, nv2, rows_per_block, q_per_row, old_per_row, new_per_row):
    n_q, width = q2.shape
    qb = rows_per_block * q_per_row
    ob = rows_per_block * old_per_row
    nb = rows_per_block * new_per_row
    full = lambda i: (0, 0)
    return pl.pallas_call(
        functools.partial(attn_kernel, 1.0 / math.sqrt(HEAD_DIM)),
        out_shape=jax.ShapeDtypeStruct((n_q, width), jnp.bfloat16),
        grid=(n_q // qb,),
        in_specs=[
            pl.BlockSpec((qb, width), lambda i: (i, 0)),
            pl.BlockSpec((qb, meta.shape[1]), lambda i: (i, 0)),
            pl.BlockSpec(pk.shape, full),
            pl.BlockSpec(pv.shape, full),
            pl.BlockSpec((ob, width), lambda i: (i, 0)),
            pl.BlockSpec((ob, width), lambda i: (i, 0)),
            pl.BlockSpec((nb, width), lambda i: (i, 0)),
            pl.BlockSpec((nb, width), lambda i: (i, 0)),
        ],
        out_specs=pl.BlockSpec((qb, width), lambda i: (i, 0)),
    )(q2, meta, pk, pv, ck2, cv2, nk2, nv2)


def attend_fused(q, nk, nv, slot_keys, slot_values, slot_of_row, slot_len, old_keys, old_values, old_len, alive, rows_per_block=8):
    rows, steps = q.shape[0], q.shape[1]
    groups = q.shape[2] // HEAD_DIM
    n_slots, pre_max = slot_keys.shape[0], slot_keys.shape[1]
    old_max = old_keys.shape[1]
    local = jnp.arange(rows, dtype=jnp.int32) % rows_per_block
    lo_pre = slot_of_row * pre_max
    hi_pre = lo_pre + slot_len[slot_of_row]
    lo_old = local * old_max
    hi_old = lo_old + old_len
    lo_new = local * steps
    step_id = jnp.arange(steps * groups, dtype=jnp.int32) // groups
    per_row = jnp.stack([lo_pre, hi_pre, lo_old, hi_old, lo_new, alive, alive, alive], axis=1)
    meta = jnp.broadcast_to(per_row[:, None, :], (rows, steps * groups, 8))
    hi_new = lo_new[:, None] + step_id[None, :] + 1
    meta = meta.at[:, :, 5].set(hi_new)
    meta = meta.reshape(rows * steps * groups, 8)
    out = attend_kernel_call(
        q.reshape(rows * steps * groups, HEAD_DIM),
        meta,
        slot_keys.reshape(n_slots * pre_max, HEAD_DIM),
        slot_values.reshape(n_slots * pre_max, HEAD_DIM),
        old_keys.reshape(rows * old_max, HEAD_DIM),
        old_values.reshape(rows * old_max, HEAD_DIM),
        nk.reshape(rows * steps, HEAD_DIM),
        nv.reshape(rows * steps, HEAD_DIM),
        rows_per_block, steps * groups, old_max, steps,
    )
    return out.reshape(rows, steps, groups * HEAD_DIM)


def body(
    residual,
    queries,
    new_keys,
    new_values,
    cache_keys,
    cache_values,
    cache_lengths,
    finished,
    partner,
    row_slot,
    fork_table,
    prompt_keys,
    prompt_values,
    prompt_lengths,
    out_proj,
):
    local_rows = queries.shape[0]
    peer_count = lax.axis_size("replica")
    where_am = lax.axis_index("replica")
    first_id = where_am * local_rows
    held_count = prompt_keys.shape[0]

    owners = fork_table // held_count
    chosen = owners == where_am
    offsets = jnp.sum(jnp.where(chosen, fork_table % held_count, 0), axis=1)
    has_block = jnp.any(chosen, axis=1)[:, None, None]
    zero_value = jnp.zeros((), prompt_keys.dtype)
    both = jnp.concatenate([prompt_keys, prompt_values], axis=2)
    out_both = jnp.where(has_block, both[offsets], zero_value)
    got_both = lax.all_to_all(out_both, "replica", split_axis=0, concat_axis=0, tiled=True)
    my_owners = owners[where_am]
    slot_both = got_both[my_owners]
    slot_keys = slot_both[..., : prompt_keys.shape[2]]
    slot_values = slot_both[..., prompt_keys.shape[2] :]
    slot_len = prompt_lengths[fork_table[where_am]]

    peer_of = partner // local_rows
    moved_row = peer_of != where_am
    pairing = (peer_of[None, :] == jnp.arange(peer_count, dtype=jnp.int32)[:, None]) & moved_row[
        None, :
    ]
    peer_row = jnp.sum(
        jnp.where(pairing, jnp.arange(local_rows, dtype=jnp.int32)[None, :], 0), axis=1
    )
    has_row = jnp.any(pairing, axis=1)[:, None, None]
    from_peer = jnp.where(moved_row, peer_of, 0)
    keep_mask = moved_row[:, None, None]
    packed = jnp.concatenate([queries, new_keys, new_values], axis=2)
    outgoing = jnp.where(has_row, packed[peer_row], jnp.zeros((), packed.dtype))
    received = swap_rows(outgoing, peer_count, 0)
    use_packed = jnp.where(keep_mask, received[from_peer], packed)
    q_width = queries.shape[2]
    kv_width = new_keys.shape[2]
    use_q = use_packed[..., :q_width]
    use_nk = use_packed[..., q_width : q_width + kv_width]
    use_nv = use_packed[..., q_width + kv_width :]

    own_ids = first_id + jnp.arange(local_rows, dtype=jnp.int32)
    slot_of_row = row_slot[own_ids]
    old_len = cache_lengths[own_ids]
    alive = 1 - finished[own_ids]
    cache_side = attend_fused(
        use_q,
        use_nk,
        use_nv,
        slot_keys,
        slot_values,
        slot_of_row,
        slot_len,
        cache_keys,
        cache_values,
        old_len,
        alive,
    )

    back = jnp.where(has_row, cache_side[peer_row], jnp.zeros((), cache_side.dtype))
    returned = swap_rows(back, peer_count, 1)
    heads_out = jnp.where(keep_mask, returned[from_peer], cache_side)

    terms = jnp.einsum("bsh,hd->bsd", heads_out, out_proj, preferred_element_type=jnp.float32)
    terms = terms.astype(jnp.bfloat16)
    summed = lax.psum_scatter(terms, "tensor", scatter_dimension=2, tiled=True)
    return (residual.astype(jnp.float32) + summed.astype(jnp.float32)).astype(jnp.bfloat16)


def solution(mesh):
    in_specs = (
        P("replica", None, "tensor"),
        P("replica", None, "tensor"),
        P("replica", None, "tensor"),
        P("replica", None, "tensor"),
        P("replica", None, "tensor"),
        P("replica", None, "tensor"),
        P(),
        P(),
        P("replica"),
        P(),
        P(),
        P("replica", None, "tensor"),
        P("replica", None, "tensor"),
        P(),
        P("tensor", None),
    )
    out_specs = P("replica", None, "tensor")
    return jax.shard_map(body, mesh=mesh, in_specs=in_specs, out_specs=out_specs, check_vma=False)
```

```python
import math

import jax
import jax.numpy as jnp
from jax import lax
import functools

from jax.experimental import pallas as pl
from jax.experimental.pallas import tpu as pltpu
from jax.sharding import PartitionSpec as P

HEAD_DIM = 128
MESH = pl.DeviceIdType.MESH


def attend_local(q, nk, nv, slot_keys, slot_values, slot_of_row, slot_len, old_keys, old_values, old_len):
    rows, steps = q.shape[0], q.shape[1]
    groups = q.shape[2] // HEAD_DIM
    n_slots, pre_len_max = slot_keys.shape[0], slot_keys.shape[1]
    qs = q.reshape(rows, steps * groups, HEAD_DIM)
    scale = 1.0 / math.sqrt(HEAD_DIM)
    flat_pk = slot_keys.reshape(n_slots * pre_len_max, HEAD_DIM)
    flat_pv = slot_values.reshape(n_slots * pre_len_max, HEAD_DIM)
    part_pre = (
        jnp.einsum("bqd,kd->bqk", qs, flat_pk, preferred_element_type=jnp.float32) * scale
    )
    part_old = (
        jnp.einsum("bqd,btd->bqt", qs, old_keys, preferred_element_type=jnp.float32) * scale
    )
    part_new = jnp.einsum("bqd,btd->bqt", qs, nk, preferred_element_type=jnp.float32) * scale
    key_slot = jnp.arange(n_slots * pre_len_max, dtype=jnp.int32) // pre_len_max
    key_pos = jnp.arange(n_slots * pre_len_max, dtype=jnp.int32) % pre_len_max
    mask_pre = (key_slot[None, :] == slot_of_row[:, None]) & (
        key_pos[None, :] < slot_len[key_slot][None, :]
    )
    mask_old = jnp.arange(old_keys.shape[1], dtype=jnp.int32)[None, :] < old_len[:, None]
    q_step = jnp.arange(steps * groups, dtype=jnp.int32) // groups
    mask_new = jnp.arange(steps, dtype=jnp.int32)[None, :] <= q_step[:, None]
    part_pre = jnp.where(mask_pre[:, None, :], part_pre, -jnp.inf)
    part_old = jnp.where(mask_old[:, None, :], part_old, -jnp.inf)
    part_new = jnp.where(mask_new[None, :, :], part_new, -jnp.inf)
    scores = jnp.concatenate([part_pre, part_old, part_new], axis=-1)
    row_top = jnp.max(scores, axis=-1, keepdims=True)
    exp_scores = jnp.exp(scores - row_top)
    weights = (exp_scores / jnp.sum(exp_scores, axis=-1, keepdims=True)).astype(jnp.bfloat16)
    n_pre = n_slots * pre_len_max
    n_old = old_keys.shape[1]
    mixed = jnp.einsum(
        "bqk,kd->bqd", weights[..., :n_pre], flat_pv, preferred_element_type=jnp.float32
    )
    mixed = mixed + jnp.einsum(
        "bqt,btd->bqd",
        weights[..., n_pre : n_pre + n_old],
        old_values,
        preferred_element_type=jnp.float32,
    )
    mixed = mixed + jnp.einsum(
        "bqt,btd->bqd", weights[..., n_pre + n_old :], nv, preferred_element_type=jnp.float32
    )
    return mixed.reshape(rows, steps, groups * HEAD_DIM)


def swap_kernel(n_rep, send, recv, s_sem, r_sem, l_sem):
    me = lax.axis_index("replica")
    mt = lax.axis_index("tensor")
    barrier = pltpu.get_barrier_semaphore()

    def greet(k, carry):
        j = lax.rem(me + k, n_rep)
        pl.semaphore_signal(barrier, inc=1, device_id=(j, mt), device_id_type=MESH)
        return carry

    lax.fori_loop(1, n_rep, greet, 0)
    pl.semaphore_wait(barrier, n_rep - 1)

    def out_copy(j):
        return pltpu.make_async_remote_copy(
            src_ref=send.at[j], dst_ref=recv.at[me], send_sem=s_sem.at[j],
            recv_sem=r_sem.at[me], device_id=(j, mt), device_id_type=MESH)

    def in_copy(j):
        return pltpu.make_async_remote_copy(
            src_ref=send.at[j], dst_ref=recv.at[j], send_sem=s_sem.at[j],
            recv_sem=r_sem.at[j], device_id=(j, mt), device_id_type=MESH)

    own = pltpu.make_async_copy(send.at[me], recv.at[me], l_sem.at[0])
    own.start()

    def start(k, carry):
        out_copy(lax.rem(me + k, n_rep)).start()
        return carry

    def wait(k, carry):
        j = lax.rem(me + k, n_rep)
        out_copy(j).wait_send()
        in_copy(j).wait_recv()
        return carry

    lax.fori_loop(1, n_rep, start, 0)
    lax.fori_loop(1, n_rep, wait, 0)
    own.wait()


def swap_rows(send, n_rep, cid):
    any_spec = pl.BlockSpec(memory_space=pl.ANY)
    return pl.pallas_call(
        functools.partial(swap_kernel, n_rep),
        out_shape=jax.ShapeDtypeStruct(send.shape, send.dtype),
        in_specs=[any_spec],
        out_specs=any_spec,
        scratch_shapes=[
            pltpu.SemaphoreType.DMA((n_rep,)),
            pltpu.SemaphoreType.DMA((n_rep,)),
            pltpu.SemaphoreType.DMA((1,)),
        ],
        compiler_params=pltpu.CompilerParams(collective_id=cid, has_side_effects=True),
    )(send)


def attn_kernel(scale, q_ref, meta_ref, pk_ref, pv_ref, ck_ref, cv_ref, nk_ref, nv_ref, o_ref):
    q = q_ref[...]
    meta = meta_ref[...]
    dims = (((1,), (1,)), ((), ()))

    def masked(keys, lo, hi):
        s = lax.dot_general(q, keys, dims, preferred_element_type=jnp.float32) * scale
        k = lax.broadcasted_iota(jnp.int32, s.shape, 1)
        return jnp.where((k >= lo) & (k < hi), s, -jnp.inf)

    s_pre = masked(pk_ref[...], meta[:, 0:1], meta[:, 1:2])
    s_old = masked(ck_ref[...], meta[:, 2:3], meta[:, 3:4])
    s_new = masked(nk_ref[...], meta[:, 4:5], meta[:, 5:6])
    top = jnp.maximum(
        jnp.maximum(jnp.max(s_pre, axis=1, keepdims=True), jnp.max(s_old, axis=1, keepdims=True)),
        jnp.max(s_new, axis=1, keepdims=True),
    )
    e_pre = jnp.exp(s_pre - top)
    e_old = jnp.exp(s_old - top)
    e_new = jnp.exp(s_new - top)
    total = (
        jnp.sum(e_pre, axis=1, keepdims=True)
        + jnp.sum(e_old, axis=1, keepdims=True)
        + jnp.sum(e_new, axis=1, keepdims=True)
    )
    w_pre = (e_pre / total).astype(jnp.bfloat16)
    w_old = (e_old / total).astype(jnp.bfloat16)
    w_new = (e_new / total).astype(jnp.bfloat16)
    out = jnp.dot(w_pre, pv_ref[...], preferred_element_type=jnp.float32)
    out = out + jnp.dot(w_old, cv_ref[...], preferred_element_type=jnp.float32)
    out = out + jnp.dot(w_new, nv_ref[...], preferred_element_type=jnp.float32)
    alive = meta[:, 6:7].astype(jnp.float32)
    o_ref[...] = (out * alive).astype(o_ref.dtype)


def attend_kernel_call(q2, meta, pk, pv, ck2, cv2, nk2, nv2, rows_per_block, q_per_row, old_per_row, new_per_row):
    n_q, width = q2.shape
    qb = rows_per_block * q_per_row
    ob = rows_per_block * old_per_row
    nb = rows_per_block * new_per_row
    full = lambda i: (0, 0)
    return pl.pallas_call(
        functools.partial(attn_kernel, 1.0 / math.sqrt(HEAD_DIM)),
        out_shape=jax.ShapeDtypeStruct((n_q, width), jnp.bfloat16),
        grid=(n_q // qb,),
        in_specs=[
            pl.BlockSpec((qb, width), lambda i: (i, 0)),
            pl.BlockSpec((qb, meta.shape[1]), lambda i: (i, 0)),
            pl.BlockSpec(pk.shape, full),
            pl.BlockSpec(pv.shape, full),
            pl.BlockSpec((ob, width), lambda i: (i, 0)),
            pl.BlockSpec((ob, width), lambda i: (i, 0)),
            pl.BlockSpec((nb, width), lambda i: (i, 0)),
            pl.BlockSpec((nb, width), lambda i: (i, 0)),
        ],
        out_specs=pl.BlockSpec((qb, width), lambda i: (i, 0)),
    )(q2, meta, pk, pv, ck2, cv2, nk2, nv2)


def attend_fused(q, nk, nv, slot_keys, slot_values, slot_of_row, slot_len, old_keys, old_values, old_len, alive, rows_per_block=8):
    rows, steps = q.shape[0], q.shape[1]
    groups = q.shape[2] // HEAD_DIM
    n_slots, pre_max = slot_keys.shape[0], slot_keys.shape[1]
    old_max = old_keys.shape[1]
    local = jnp.arange(rows, dtype=jnp.int32) % rows_per_block
    lo_pre = slot_of_row * pre_max
    hi_pre = lo_pre + slot_len[slot_of_row]
    lo_old = local * old_max
    hi_old = lo_old + old_len
    lo_new = local * steps
    step_id = jnp.arange(steps * groups, dtype=jnp.int32) // groups
    per_row = jnp.stack([lo_pre, hi_pre, lo_old, hi_old, lo_new, alive, alive, alive], axis=1)
    meta = jnp.broadcast_to(per_row[:, None, :], (rows, steps * groups, 8))
    hi_new = lo_new[:, None] + step_id[None, :] + 1
    meta = meta.at[:, :, 5].set(hi_new)
    meta = meta.reshape(rows * steps * groups, 8)
    out = attend_kernel_call(
        q.reshape(rows * steps * groups, HEAD_DIM),
        meta,
        slot_keys.reshape(n_slots * pre_max, HEAD_DIM),
        slot_values.reshape(n_slots * pre_max, HEAD_DIM),
        old_keys.reshape(rows * old_max, HEAD_DIM),
        old_values.reshape(rows * old_max, HEAD_DIM),
        nk.reshape(rows * steps, HEAD_DIM),
        nv.reshape(rows * steps, HEAD_DIM),
        rows_per_block, steps * groups, old_max, steps,
    )
    return out.reshape(rows, steps, groups * HEAD_DIM)


def body(
    residual,
    queries,
    new_keys,
    new_values,
    cache_keys,
    cache_values,
    cache_lengths,
    finished,
    partner,
    row_slot,
    fork_table,
    prompt_keys,
    prompt_values,
    prompt_lengths,
    out_proj,
):
    local_rows = queries.shape[0]
    peer_count = lax.axis_size("replica")
    where_am = lax.axis_index("replica")
    first_id = where_am * local_rows
    held_count = prompt_keys.shape[0]

    owners = fork_table // held_count
    chosen = owners == where_am
    offsets = jnp.sum(jnp.where(chosen, fork_table % held_count, 0), axis=1)
    has_block = jnp.any(chosen, axis=1)[:, None, None]
    zero_value = jnp.zeros((), prompt_keys.dtype)
    both = jnp.concatenate([prompt_keys, prompt_values], axis=2)
    out_both = jnp.where(has_block, both[offsets], zero_value)
    got_both = lax.all_to_all(out_both, "replica", split_axis=0, concat_axis=0, tiled=True)
    my_owners = owners[where_am]
    slot_both = got_both[my_owners]
    slot_keys = slot_both[..., : prompt_keys.shape[2]]
    slot_values = slot_both[..., prompt_keys.shape[2] :]
    slot_len = prompt_lengths[fork_table[where_am]]

    peer_of = partner // local_rows
    moved_row = peer_of != where_am
    pairing = (peer_of[None, :] == jnp.arange(peer_count, dtype=jnp.int32)[:, None]) & moved_row[
        None, :
    ]
    peer_row = jnp.sum(
        jnp.where(pairing, jnp.arange(local_rows, dtype=jnp.int32)[None, :], 0), axis=1
    )
    has_row = jnp.any(pairing, axis=1)[:, None, None]
    from_peer = jnp.where(moved_row, peer_of, 0)
    keep_mask = moved_row[:, None, None]
    packed = jnp.concatenate([queries, new_keys, new_values], axis=2)
    outgoing = jnp.where(has_row, packed[peer_row], jnp.zeros((), packed.dtype))
    received = swap_rows(outgoing, peer_count, 0)
    use_packed = jnp.where(keep_mask, received[from_peer], packed)
    q_width = queries.shape[2]
    kv_width = new_keys.shape[2]
    use_q = use_packed[..., :q_width]
    use_nk = use_packed[..., q_width : q_width + kv_width]
    use_nv = use_packed[..., q_width + kv_width :]

    own_ids = first_id + jnp.arange(local_rows, dtype=jnp.int32)
    slot_of_row = row_slot[own_ids]
    old_len = cache_lengths[own_ids]
    alive = 1 - finished[own_ids]
    cache_side = attend_fused(
        use_q,
        use_nk,
        use_nv,
        slot_keys,
        slot_values,
        slot_of_row,
        slot_len,
        cache_keys,
        cache_values,
        old_len,
        alive,
    )

    back = jnp.where(has_row, cache_side[peer_row], jnp.zeros((), cache_side.dtype))
    stayed = jnp.where(keep_mask, jnp.zeros((), cache_side.dtype), cache_side)
    terms = jnp.einsum("bsh,hd->bsd", stayed, out_proj, preferred_element_type=jnp.float32)
    terms, back = lax.optimization_barrier((terms.astype(jnp.bfloat16), back))
    summed = lax.psum_scatter(terms, "tensor", scatter_dimension=2, tiled=True)
    returned = lax.all_to_all(back, "replica", split_axis=0, concat_axis=0, tiled=True)
    move_count = peer_count // 2
    moved_ids = jnp.nonzero(moved_row, size=move_count, fill_value=0)[0]
    valid = (jnp.arange(move_count) < jnp.sum(moved_row)).astype(jnp.float32)
    moved_heads = returned[peer_of[moved_ids]]
    moved_heads, summed = lax.optimization_barrier((moved_heads, summed))
    moved_terms = jnp.einsum(
        "bsh,hd->bsd", moved_heads, out_proj, preferred_element_type=jnp.float32
    )
    moved_sum = lax.psum_scatter(
        moved_terms.astype(jnp.bfloat16), "tensor", scatter_dimension=2, tiled=True
    )
    moved_part = jnp.zeros(summed.shape, jnp.float32).at[moved_ids].add(
        moved_sum.astype(jnp.float32) * valid[:, None, None]
    )
    total = residual.astype(jnp.float32) + summed.astype(jnp.float32) + moved_part
    return total.astype(jnp.bfloat16)


def solution(mesh):
    in_specs = (
        P("replica", None, "tensor"),
        P("replica", None, "tensor"),
        P("replica", None, "tensor"),
        P("replica", None, "tensor"),
        P("replica", None, "tensor"),
        P("replica", None, "tensor"),
        P(),
        P(),
        P("replica"),
        P(),
        P(),
        P("replica", None, "tensor"),
        P("replica", None, "tensor"),
        P(),
        P("tensor", None),
    )
    out_specs = P("replica", None, "tensor")
    return jax.shard_map(body, mesh=mesh, in_specs=in_specs, out_specs=out_specs, check_vma=False)
```

```python
import math

import jax
import jax.numpy as jnp
from jax import lax
import functools

from jax.experimental import pallas as pl
from jax.sharding import PartitionSpec as P

HEAD_DIM = 128


def attend_local(q, nk, nv, slot_keys, slot_values, slot_of_row, slot_len, old_keys, old_values, old_len):
    rows, steps = q.shape[0], q.shape[1]
    groups = q.shape[2] // HEAD_DIM
    n_slots, pre_len_max = slot_keys.shape[0], slot_keys.shape[1]
    qs = q.reshape(rows, steps * groups, HEAD_DIM)
    scale = 1.0 / math.sqrt(HEAD_DIM)
    flat_pk = slot_keys.reshape(n_slots * pre_len_max, HEAD_DIM)
    flat_pv = slot_values.reshape(n_slots * pre_len_max, HEAD_DIM)
    part_pre = (
        jnp.einsum("bqd,kd->bqk", qs, flat_pk, preferred_element_type=jnp.float32) * scale
    )
    part_old = (
        jnp.einsum("bqd,btd->bqt", qs, old_keys, preferred_element_type=jnp.float32) * scale
    )
    part_new = jnp.einsum("bqd,btd->bqt", qs, nk, preferred_element_type=jnp.float32) * scale
    key_slot = jnp.arange(n_slots * pre_len_max, dtype=jnp.int32) // pre_len_max
    key_pos = jnp.arange(n_slots * pre_len_max, dtype=jnp.int32) % pre_len_max
    mask_pre = (key_slot[None, :] == slot_of_row[:, None]) & (
        key_pos[None, :] < slot_len[key_slot][None, :]
    )
    mask_old = jnp.arange(old_keys.shape[1], dtype=jnp.int32)[None, :] < old_len[:, None]
    q_step = jnp.arange(steps * groups, dtype=jnp.int32) // groups
    mask_new = jnp.arange(steps, dtype=jnp.int32)[None, :] <= q_step[:, None]
    part_pre = jnp.where(mask_pre[:, None, :], part_pre, -jnp.inf)
    part_old = jnp.where(mask_old[:, None, :], part_old, -jnp.inf)
    part_new = jnp.where(mask_new[None, :, :], part_new, -jnp.inf)
    scores = jnp.concatenate([part_pre, part_old, part_new], axis=-1)
    row_top = jnp.max(scores, axis=-1, keepdims=True)
    exp_scores = jnp.exp(scores - row_top)
    weights = (exp_scores / jnp.sum(exp_scores, axis=-1, keepdims=True)).astype(jnp.bfloat16)
    n_pre = n_slots * pre_len_max
    n_old = old_keys.shape[1]
    mixed = jnp.einsum(
        "bqk,kd->bqd", weights[..., :n_pre], flat_pv, preferred_element_type=jnp.float32
    )
    mixed = mixed + jnp.einsum(
        "bqt,btd->bqd",
        weights[..., n_pre : n_pre + n_old],
        old_values,
        preferred_element_type=jnp.float32,
    )
    mixed = mixed + jnp.einsum(
        "bqt,btd->bqd", weights[..., n_pre + n_old :], nv, preferred_element_type=jnp.float32
    )
    return mixed.reshape(rows, steps, groups * HEAD_DIM)


def attn_kernel(scale, q_ref, meta_ref, pk_ref, pv_ref, ck_ref, cv_ref, nk_ref, nv_ref, o_ref):
    q = q_ref[...]
    meta = meta_ref[...]
    dims = (((1,), (1,)), ((), ()))

    def masked(keys, lo, hi):
        s = lax.dot_general(q, keys, dims, preferred_element_type=jnp.float32) * scale
        k = lax.broadcasted_iota(jnp.int32, s.shape, 1)
        return jnp.where((k >= lo) & (k < hi), s, -jnp.inf)

    s_pre = masked(pk_ref[...], meta[:, 0:1], meta[:, 1:2])
    s_old = masked(ck_ref[...], meta[:, 2:3], meta[:, 3:4])
    s_new = masked(nk_ref[...], meta[:, 4:5], meta[:, 5:6])
    top = jnp.maximum(
        jnp.maximum(jnp.max(s_pre, axis=1, keepdims=True), jnp.max(s_old, axis=1, keepdims=True)),
        jnp.max(s_new, axis=1, keepdims=True),
    )
    e_pre = jnp.exp(s_pre - top)
    e_old = jnp.exp(s_old - top)
    e_new = jnp.exp(s_new - top)
    total = (
        jnp.sum(e_pre, axis=1, keepdims=True)
        + jnp.sum(e_old, axis=1, keepdims=True)
        + jnp.sum(e_new, axis=1, keepdims=True)
    )
    w_pre = (e_pre / total).astype(jnp.bfloat16)
    w_old = (e_old / total).astype(jnp.bfloat16)
    w_new = (e_new / total).astype(jnp.bfloat16)
    out = jnp.dot(w_pre, pv_ref[...], preferred_element_type=jnp.float32)
    out = out + jnp.dot(w_old, cv_ref[...], preferred_element_type=jnp.float32)
    out = out + jnp.dot(w_new, nv_ref[...], preferred_element_type=jnp.float32)
    alive = meta[:, 6:7].astype(jnp.float32)
    o_ref[...] = (out * alive).astype(o_ref.dtype)


def attend_kernel_call(q2, meta, pk, pv, ck2, cv2, nk2, nv2, rows_per_block, q_per_row, old_per_row, new_per_row):
    n_q, width = q2.shape
    qb = rows_per_block * q_per_row
    ob = rows_per_block * old_per_row
    nb = rows_per_block * new_per_row
    full = lambda i: (0, 0)
    return pl.pallas_call(
        functools.partial(attn_kernel, 1.0 / math.sqrt(HEAD_DIM)),
        out_shape=jax.ShapeDtypeStruct((n_q, width), jnp.bfloat16),
        grid=(n_q // qb,),
        in_specs=[
            pl.BlockSpec((qb, width), lambda i: (i, 0)),
            pl.BlockSpec((qb, meta.shape[1]), lambda i: (i, 0)),
            pl.BlockSpec(pk.shape, full),
            pl.BlockSpec(pv.shape, full),
            pl.BlockSpec((ob, width), lambda i: (i, 0)),
            pl.BlockSpec((ob, width), lambda i: (i, 0)),
            pl.BlockSpec((nb, width), lambda i: (i, 0)),
            pl.BlockSpec((nb, width), lambda i: (i, 0)),
        ],
        out_specs=pl.BlockSpec((qb, width), lambda i: (i, 0)),
    )(q2, meta, pk, pv, ck2, cv2, nk2, nv2)


def attend_fused(q, nk, nv, slot_keys, slot_values, slot_of_row, slot_len, old_keys, old_values, old_len, alive, rows_per_block=8):
    rows, steps = q.shape[0], q.shape[1]
    groups = q.shape[2] // HEAD_DIM
    n_slots, pre_max = slot_keys.shape[0], slot_keys.shape[1]
    old_max = old_keys.shape[1]
    local = jnp.arange(rows, dtype=jnp.int32) % rows_per_block
    lo_pre = slot_of_row * pre_max
    hi_pre = lo_pre + slot_len[slot_of_row]
    lo_old = local * old_max
    hi_old = lo_old + old_len
    lo_new = local * steps
    step_id = jnp.arange(steps * groups, dtype=jnp.int32) // groups
    per_row = jnp.stack([lo_pre, hi_pre, lo_old, hi_old, lo_new, alive, alive, alive], axis=1)
    meta = jnp.broadcast_to(per_row[:, None, :], (rows, steps * groups, 8))
    hi_new = lo_new[:, None] + step_id[None, :] + 1
    meta = meta.at[:, :, 5].set(hi_new)
    meta = meta.reshape(rows * steps * groups, 8)
    out = attend_kernel_call(
        q.reshape(rows * steps * groups, HEAD_DIM),
        meta,
        slot_keys.reshape(n_slots * pre_max, HEAD_DIM),
        slot_values.reshape(n_slots * pre_max, HEAD_DIM),
        old_keys.reshape(rows * old_max, HEAD_DIM),
        old_values.reshape(rows * old_max, HEAD_DIM),
        nk.reshape(rows * steps, HEAD_DIM),
        nv.reshape(rows * steps, HEAD_DIM),
        rows_per_block, steps * groups, old_max, steps,
    )
    return out.reshape(rows, steps, groups * HEAD_DIM)


def body(
    residual,
    queries,
    new_keys,
    new_values,
    cache_keys,
    cache_values,
    cache_lengths,
    finished,
    partner,
    row_slot,
    fork_table,
    prompt_keys,
    prompt_values,
    prompt_lengths,
    out_proj,
):
    local_rows = queries.shape[0]
    peer_count = lax.axis_size("replica")
    where_am = lax.axis_index("replica")
    first_id = where_am * local_rows
    held_count = prompt_keys.shape[0]

    owners = fork_table // held_count
    chosen = owners == where_am
    offsets = jnp.sum(jnp.where(chosen, fork_table % held_count, 0), axis=1)
    has_block = jnp.any(chosen, axis=1)[:, None, None]
    zero_value = jnp.zeros((), prompt_keys.dtype)
    both = jnp.concatenate([prompt_keys, prompt_values], axis=2)
    out_both = jnp.where(has_block, both[offsets], zero_value)

    peer_of = partner // local_rows
    moved_row = peer_of != where_am
    pairing = (peer_of[None, :] == jnp.arange(peer_count, dtype=jnp.int32)[:, None]) & moved_row[
        None, :
    ]
    peer_row = jnp.sum(
        jnp.where(pairing, jnp.arange(local_rows, dtype=jnp.int32)[None, :], 0), axis=1
    )
    has_row = jnp.any(pairing, axis=1)[:, None, None]
    from_peer = jnp.where(moved_row, peer_of, 0)
    keep_mask = moved_row[:, None, None]
    packed = jnp.concatenate([queries, new_keys, new_values], axis=2)
    outgoing = jnp.where(has_row, packed[peer_row], jnp.zeros((), packed.dtype))
    lane = out_both.shape[2]
    q_rows = outgoing[0].size // lane
    q_pad = -q_rows % 16
    q_block = jnp.pad(outgoing.reshape(peer_count, q_rows, lane), ((0, 0), (0, q_pad), (0, 0)))
    joined = jnp.concatenate([out_both, q_block], axis=1)
    arrived = lax.all_to_all(joined, "replica", split_axis=0, concat_axis=0, tiled=True)
    prompt_rows = out_both.shape[1]
    got_both = arrived[:, :prompt_rows]
    received = arrived[:, prompt_rows : prompt_rows + q_rows].reshape(outgoing.shape)
    my_owners = owners[where_am]
    slot_both = got_both[my_owners]
    slot_keys = slot_both[..., : prompt_keys.shape[2]]
    slot_values = slot_both[..., prompt_keys.shape[2] :]
    slot_len = prompt_lengths[fork_table[where_am]]
    use_packed = jnp.where(keep_mask, received[from_peer], packed)
    q_width = queries.shape[2]
    kv_width = new_keys.shape[2]
    use_q = use_packed[..., :q_width]
    use_nk = use_packed[..., q_width : q_width + kv_width]
    use_nv = use_packed[..., q_width + kv_width :]

    own_ids = first_id + jnp.arange(local_rows, dtype=jnp.int32)
    slot_of_row = row_slot[own_ids]
    old_len = cache_lengths[own_ids]
    alive = 1 - finished[own_ids]
    cache_side = attend_fused(
        use_q,
        use_nk,
        use_nv,
        slot_keys,
        slot_values,
        slot_of_row,
        slot_len,
        cache_keys,
        cache_values,
        old_len,
        alive,
    )

    back = jnp.where(has_row, cache_side[peer_row], jnp.zeros((), cache_side.dtype))
    returned = lax.all_to_all(back, "replica", split_axis=0, concat_axis=0, tiled=True)
    heads_out = jnp.where(keep_mask, returned[from_peer], cache_side)

    terms = jnp.einsum("bsh,hd->bsd", heads_out, out_proj, preferred_element_type=jnp.float32)
    terms = terms.astype(jnp.bfloat16)
    summed = lax.psum_scatter(terms, "tensor", scatter_dimension=2, tiled=True)
    return (residual.astype(jnp.float32) + summed.astype(jnp.float32)).astype(jnp.bfloat16)


def solution(mesh):
    in_specs = (
        P("replica", None, "tensor"),
        P("replica", None, "tensor"),
        P("replica", None, "tensor"),
        P("replica", None, "tensor"),
        P("replica", None, "tensor"),
        P("replica", None, "tensor"),
        P(),
        P(),
        P("replica"),
        P(),
        P(),
        P("replica", None, "tensor"),
        P("replica", None, "tensor"),
        P(),
        P("tensor", None),
    )
    out_specs = P("replica", None, "tensor")
    return jax.shard_map(body, mesh=mesh, in_specs=in_specs, out_specs=out_specs, check_vma=False)
```

```python
import math

import jax
import jax.numpy as jnp
from jax import lax
import functools

from jax.experimental import pallas as pl
from jax.experimental.pallas import tpu as pltpu
from jax.sharding import PartitionSpec as P

HEAD_DIM = 128
MESH = pl.DeviceIdType.MESH


def attend_local(q, nk, nv, slot_keys, slot_values, slot_of_row, slot_len, old_keys, old_values, old_len):
    rows, steps = q.shape[0], q.shape[1]
    groups = q.shape[2] // HEAD_DIM
    n_slots, pre_len_max = slot_keys.shape[0], slot_keys.shape[1]
    qs = q.reshape(rows, steps * groups, HEAD_DIM)
    scale = 1.0 / math.sqrt(HEAD_DIM)
    flat_pk = slot_keys.reshape(n_slots * pre_len_max, HEAD_DIM)
    flat_pv = slot_values.reshape(n_slots * pre_len_max, HEAD_DIM)
    part_pre = (
        jnp.einsum("bqd,kd->bqk", qs, flat_pk, preferred_element_type=jnp.float32) * scale
    )
    part_old = (
        jnp.einsum("bqd,btd->bqt", qs, old_keys, preferred_element_type=jnp.float32) * scale
    )
    part_new = jnp.einsum("bqd,btd->bqt", qs, nk, preferred_element_type=jnp.float32) * scale
    key_slot = jnp.arange(n_slots * pre_len_max, dtype=jnp.int32) // pre_len_max
    key_pos = jnp.arange(n_slots * pre_len_max, dtype=jnp.int32) % pre_len_max
    mask_pre = (key_slot[None, :] == slot_of_row[:, None]) & (
        key_pos[None, :] < slot_len[key_slot][None, :]
    )
    mask_old = jnp.arange(old_keys.shape[1], dtype=jnp.int32)[None, :] < old_len[:, None]
    q_step = jnp.arange(steps * groups, dtype=jnp.int32) // groups
    mask_new = jnp.arange(steps, dtype=jnp.int32)[None, :] <= q_step[:, None]
    part_pre = jnp.where(mask_pre[:, None, :], part_pre, -jnp.inf)
    part_old = jnp.where(mask_old[:, None, :], part_old, -jnp.inf)
    part_new = jnp.where(mask_new[None, :, :], part_new, -jnp.inf)
    scores = jnp.concatenate([part_pre, part_old, part_new], axis=-1)
    row_top = jnp.max(scores, axis=-1, keepdims=True)
    exp_scores = jnp.exp(scores - row_top)
    weights = (exp_scores / jnp.sum(exp_scores, axis=-1, keepdims=True)).astype(jnp.bfloat16)
    n_pre = n_slots * pre_len_max
    n_old = old_keys.shape[1]
    mixed = jnp.einsum(
        "bqk,kd->bqd", weights[..., :n_pre], flat_pv, preferred_element_type=jnp.float32
    )
    mixed = mixed + jnp.einsum(
        "bqt,btd->bqd",
        weights[..., n_pre : n_pre + n_old],
        old_values,
        preferred_element_type=jnp.float32,
    )
    mixed = mixed + jnp.einsum(
        "bqt,btd->bqd", weights[..., n_pre + n_old :], nv, preferred_element_type=jnp.float32
    )
    return mixed.reshape(rows, steps, groups * HEAD_DIM)


def weight_kernel(n_ten, w_ref, w_recv, s_sem, r_sem, l_sem):
    me = lax.axis_index("replica")
    mt = lax.axis_index("tensor")
    width = w_recv.shape[2]
    barrier = pltpu.get_barrier_semaphore()

    def greet(k, carry):
        t = lax.rem(mt + k, n_ten)
        pl.semaphore_signal(barrier, inc=1, device_id=(me, t), device_id_type=MESH)
        return carry

    lax.fori_loop(1, n_ten, greet, 0)
    pl.semaphore_wait(barrier, n_ten - 1)

    def w_cols(t):
        return w_ref.at[:, pl.ds(pl.multiple_of(t * width, width), width)]

    def w_out(t):
        return pltpu.make_async_remote_copy(
            src_ref=w_cols(t), dst_ref=w_recv.at[mt], send_sem=s_sem.at[t],
            recv_sem=r_sem.at[mt], device_id=(me, t), device_id_type=MESH)

    def w_in(t):
        return pltpu.make_async_remote_copy(
            src_ref=w_cols(t), dst_ref=w_recv.at[t], send_sem=s_sem.at[t],
            recv_sem=r_sem.at[t], device_id=(me, t), device_id_type=MESH)

    own = pltpu.make_async_copy(w_cols(mt), w_recv.at[mt], l_sem.at[0])
    own.start()

    def start(k, carry):
        w_out(lax.rem(mt + k, n_ten)).start()
        return carry

    def wait(k, carry):
        t = lax.rem(mt + k, n_ten)
        w_out(t).wait_send()
        w_in(t).wait_recv()
        return carry

    lax.fori_loop(1, n_ten, start, 0)
    lax.fori_loop(1, n_ten, wait, 0)
    own.wait()


def exchange_weights(w, n_ten):
    any_spec = pl.BlockSpec(memory_space=pl.ANY)
    width = w.shape[1] // n_ten
    return pl.pallas_call(
        functools.partial(weight_kernel, n_ten),
        out_shape=jax.ShapeDtypeStruct((n_ten, w.shape[0], width), w.dtype),
        in_specs=[any_spec],
        out_specs=any_spec,
        scratch_shapes=[
            pltpu.SemaphoreType.DMA((n_ten,)),
            pltpu.SemaphoreType.DMA((n_ten,)),
            pltpu.SemaphoreType.DMA((1,)),
        ],
        compiler_params=pltpu.CompilerParams(collective_id=2, has_side_effects=True),
    )(w)


def attn_kernel(scale, q_ref, meta_ref, pk_ref, pv_ref, ck_ref, cv_ref, nk_ref, nv_ref, o_ref):
    q = q_ref[...]
    meta = meta_ref[...]
    dims = (((1,), (1,)), ((), ()))

    def masked(keys, lo, hi):
        s = lax.dot_general(q, keys, dims, preferred_element_type=jnp.float32) * scale
        k = lax.broadcasted_iota(jnp.int32, s.shape, 1)
        return jnp.where((k >= lo) & (k < hi), s, -jnp.inf)

    s_pre = masked(pk_ref[...], meta[:, 0:1], meta[:, 1:2])
    s_old = masked(ck_ref[...], meta[:, 2:3], meta[:, 3:4])
    s_new = masked(nk_ref[...], meta[:, 4:5], meta[:, 5:6])
    top = jnp.maximum(
        jnp.maximum(jnp.max(s_pre, axis=1, keepdims=True), jnp.max(s_old, axis=1, keepdims=True)),
        jnp.max(s_new, axis=1, keepdims=True),
    )
    e_pre = jnp.exp(s_pre - top)
    e_old = jnp.exp(s_old - top)
    e_new = jnp.exp(s_new - top)
    total = (
        jnp.sum(e_pre, axis=1, keepdims=True)
        + jnp.sum(e_old, axis=1, keepdims=True)
        + jnp.sum(e_new, axis=1, keepdims=True)
    )
    w_pre = (e_pre / total).astype(jnp.bfloat16)
    w_old = (e_old / total).astype(jnp.bfloat16)
    w_new = (e_new / total).astype(jnp.bfloat16)
    out = jnp.dot(w_pre, pv_ref[...], preferred_element_type=jnp.float32)
    out = out + jnp.dot(w_old, cv_ref[...], preferred_element_type=jnp.float32)
    out = out + jnp.dot(w_new, nv_ref[...], preferred_element_type=jnp.float32)
    alive = meta[:, 6:7].astype(jnp.float32)
    o_ref[...] = (out * alive).astype(o_ref.dtype)


def attend_kernel_call(q2, meta, pk, pv, ck2, cv2, nk2, nv2, rows_per_block, q_per_row, old_per_row, new_per_row):
    n_q, width = q2.shape
    qb = rows_per_block * q_per_row
    ob = rows_per_block * old_per_row
    nb = rows_per_block * new_per_row
    full = lambda i: (0, 0)
    return pl.pallas_call(
        functools.partial(attn_kernel, 1.0 / math.sqrt(HEAD_DIM)),
        out_shape=jax.ShapeDtypeStruct((n_q, width), jnp.bfloat16),
        grid=(n_q // qb,),
        in_specs=[
            pl.BlockSpec((qb, width), lambda i: (i, 0)),
            pl.BlockSpec((qb, meta.shape[1]), lambda i: (i, 0)),
            pl.BlockSpec(pk.shape, full),
            pl.BlockSpec(pv.shape, full),
            pl.BlockSpec((ob, width), lambda i: (i, 0)),
            pl.BlockSpec((ob, width), lambda i: (i, 0)),
            pl.BlockSpec((nb, width), lambda i: (i, 0)),
            pl.BlockSpec((nb, width), lambda i: (i, 0)),
        ],
        out_specs=pl.BlockSpec((qb, width), lambda i: (i, 0)),
    )(q2, meta, pk, pv, ck2, cv2, nk2, nv2)


def attend_fused(q, nk, nv, slot_keys, slot_values, slot_of_row, slot_len, old_keys, old_values, old_len, alive, rows_per_block=8):
    rows, steps = q.shape[0], q.shape[1]
    groups = q.shape[2] // HEAD_DIM
    n_slots, pre_max = slot_keys.shape[0], slot_keys.shape[1]
    old_max = old_keys.shape[1]
    local = jnp.arange(rows, dtype=jnp.int32) % rows_per_block
    lo_pre = slot_of_row * pre_max
    hi_pre = lo_pre + slot_len[slot_of_row]
    lo_old = local * old_max
    hi_old = lo_old + old_len
    lo_new = local * steps
    step_id = jnp.arange(steps * groups, dtype=jnp.int32) // groups
    per_row = jnp.stack([lo_pre, hi_pre, lo_old, hi_old, lo_new, alive, alive, alive], axis=1)
    meta = jnp.broadcast_to(per_row[:, None, :], (rows, steps * groups, 8))
    hi_new = lo_new[:, None] + step_id[None, :] + 1
    meta = meta.at[:, :, 5].set(hi_new)
    meta = meta.reshape(rows * steps * groups, 8)
    out = attend_kernel_call(
        q.reshape(rows * steps * groups, HEAD_DIM),
        meta,
        slot_keys.reshape(n_slots * pre_max, HEAD_DIM),
        slot_values.reshape(n_slots * pre_max, HEAD_DIM),
        old_keys.reshape(rows * old_max, HEAD_DIM),
        old_values.reshape(rows * old_max, HEAD_DIM),
        nk.reshape(rows * steps, HEAD_DIM),
        nv.reshape(rows * steps, HEAD_DIM),
        rows_per_block, steps * groups, old_max, steps,
    )
    return out.reshape(rows, steps, groups * HEAD_DIM)


def body(
    residual,
    queries,
    new_keys,
    new_values,
    cache_keys,
    cache_values,
    cache_lengths,
    finished,
    partner,
    row_slot,
    fork_table,
    prompt_keys,
    prompt_values,
    prompt_lengths,
    out_proj,
):
    local_rows = queries.shape[0]
    peer_count = lax.axis_size("replica")
    where_am = lax.axis_index("replica")
    first_id = where_am * local_rows
    held_count = prompt_keys.shape[0]

    owners = fork_table // held_count
    chosen = owners == where_am
    offsets = jnp.sum(jnp.where(chosen, fork_table % held_count, 0), axis=1)
    has_block = jnp.any(chosen, axis=1)[:, None, None]
    zero_value = jnp.zeros((), prompt_keys.dtype)
    both = jnp.concatenate([prompt_keys, prompt_values], axis=2)
    out_both = jnp.where(has_block, both[offsets], zero_value)
    got_both = lax.all_to_all(out_both, "replica", split_axis=0, concat_axis=0, tiled=True)
    n_ten = lax.axis_size("tensor")
    proj_blocks = exchange_weights(out_proj, n_ten)
    got_both, proj_blocks = lax.optimization_barrier((got_both, proj_blocks))
    my_owners = owners[where_am]
    slot_both = got_both[my_owners]
    slot_keys = slot_both[..., : prompt_keys.shape[2]]
    slot_values = slot_both[..., prompt_keys.shape[2] :]
    slot_len = prompt_lengths[fork_table[where_am]]

    peer_of = partner // local_rows
    moved_row = peer_of != where_am
    pairing = (peer_of[None, :] == jnp.arange(peer_count, dtype=jnp.int32)[:, None]) & moved_row[
        None, :
    ]
    peer_row = jnp.sum(
        jnp.where(pairing, jnp.arange(local_rows, dtype=jnp.int32)[None, :], 0), axis=1
    )
    has_row = jnp.any(pairing, axis=1)[:, None, None]
    from_peer = jnp.where(moved_row, peer_of, 0)
    keep_mask = moved_row[:, None, None]
    packed = jnp.concatenate([queries, new_keys, new_values], axis=2)
    outgoing = jnp.where(has_row, packed[peer_row], jnp.zeros((), packed.dtype))
    received = lax.all_to_all(outgoing, "replica", split_axis=0, concat_axis=0, tiled=True)
    use_packed = jnp.where(keep_mask, received[from_peer], packed)
    q_width = queries.shape[2]
    kv_width = new_keys.shape[2]
    use_q = use_packed[..., :q_width]
    use_nk = use_packed[..., q_width : q_width + kv_width]
    use_nv = use_packed[..., q_width + kv_width :]

    own_ids = first_id + jnp.arange(local_rows, dtype=jnp.int32)
    slot_of_row = row_slot[own_ids]
    old_len = cache_lengths[own_ids]
    alive = 1 - finished[own_ids]
    cache_side = attend_fused(
        use_q,
        use_nk,
        use_nv,
        slot_keys,
        slot_values,
        slot_of_row,
        slot_len,
        cache_keys,
        cache_values,
        old_len,
        alive,
    )

    back = jnp.where(has_row, cache_side[peer_row], jnp.zeros((), cache_side.dtype))
    returned = lax.all_to_all(back, "replica", split_axis=0, concat_axis=0, tiled=True)
    heads_out = jnp.where(keep_mask, returned[from_peer], cache_side)

    all_heads = lax.all_gather(heads_out, "tensor", axis=0, tiled=False)
    summed = jnp.einsum(
        "tbsh,thd->bsd", all_heads, proj_blocks, preferred_element_type=jnp.float32
    )
    return (residual.astype(jnp.float32) + summed).astype(jnp.bfloat16)


def solution(mesh):
    in_specs = (
        P("replica", None, "tensor"),
        P("replica", None, "tensor"),
        P("replica", None, "tensor"),
        P("replica", None, "tensor"),
        P("replica", None, "tensor"),
        P("replica", None, "tensor"),
        P(),
        P(),
        P("replica"),
        P(),
        P(),
        P("replica", None, "tensor"),
        P("replica", None, "tensor"),
        P(),
        P("tensor", None),
    )
    out_specs = P("replica", None, "tensor")
    return jax.shard_map(body, mesh=mesh, in_specs=in_specs, out_specs=out_specs, check_vma=False)
```

```python
import math

import jax
import jax.numpy as jnp
from jax import lax
import functools

from jax.experimental import pallas as pl
from jax.experimental.pallas import tpu as pltpu
from jax.sharding import PartitionSpec as P

HEAD_DIM = 128
MESH = pl.DeviceIdType.MESH


def attend_local(q, nk, nv, slot_keys, slot_values, slot_of_row, slot_len, old_keys, old_values, old_len):
    rows, steps = q.shape[0], q.shape[1]
    groups = q.shape[2] // HEAD_DIM
    n_slots, pre_len_max = slot_keys.shape[0], slot_keys.shape[1]
    qs = q.reshape(rows, steps * groups, HEAD_DIM)
    scale = 1.0 / math.sqrt(HEAD_DIM)
    flat_pk = slot_keys.reshape(n_slots * pre_len_max, HEAD_DIM)
    flat_pv = slot_values.reshape(n_slots * pre_len_max, HEAD_DIM)
    part_pre = (
        jnp.einsum("bqd,kd->bqk", qs, flat_pk, preferred_element_type=jnp.float32) * scale
    )
    part_old = (
        jnp.einsum("bqd,btd->bqt", qs, old_keys, preferred_element_type=jnp.float32) * scale
    )
    part_new = jnp.einsum("bqd,btd->bqt", qs, nk, preferred_element_type=jnp.float32) * scale
    key_slot = jnp.arange(n_slots * pre_len_max, dtype=jnp.int32) // pre_len_max
    key_pos = jnp.arange(n_slots * pre_len_max, dtype=jnp.int32) % pre_len_max
    mask_pre = (key_slot[None, :] == slot_of_row[:, None]) & (
        key_pos[None, :] < slot_len[key_slot][None, :]
    )
    mask_old = jnp.arange(old_keys.shape[1], dtype=jnp.int32)[None, :] < old_len[:, None]
    q_step = jnp.arange(steps * groups, dtype=jnp.int32) // groups
    mask_new = jnp.arange(steps, dtype=jnp.int32)[None, :] <= q_step[:, None]
    part_pre = jnp.where(mask_pre[:, None, :], part_pre, -jnp.inf)
    part_old = jnp.where(mask_old[:, None, :], part_old, -jnp.inf)
    part_new = jnp.where(mask_new[None, :, :], part_new, -jnp.inf)
    scores = jnp.concatenate([part_pre, part_old, part_new], axis=-1)
    row_top = jnp.max(scores, axis=-1, keepdims=True)
    exp_scores = jnp.exp(scores - row_top)
    weights = (exp_scores / jnp.sum(exp_scores, axis=-1, keepdims=True)).astype(jnp.bfloat16)
    n_pre = n_slots * pre_len_max
    n_old = old_keys.shape[1]
    mixed = jnp.einsum(
        "bqk,kd->bqd", weights[..., :n_pre], flat_pv, preferred_element_type=jnp.float32
    )
    mixed = mixed + jnp.einsum(
        "bqt,btd->bqd",
        weights[..., n_pre : n_pre + n_old],
        old_values,
        preferred_element_type=jnp.float32,
    )
    mixed = mixed + jnp.einsum(
        "bqt,btd->bqd", weights[..., n_pre + n_old :], nv, preferred_element_type=jnp.float32
    )
    return mixed.reshape(rows, steps, groups * HEAD_DIM)


def weight_kernel(n_ten, w_ref, w_recv, s_sem, r_sem, l_sem):
    me = lax.axis_index("replica")
    mt = lax.axis_index("tensor")
    width = w_recv.shape[2]
    barrier = pltpu.get_barrier_semaphore()

    def greet(k, carry):
        t = lax.rem(mt + k, n_ten)
        pl.semaphore_signal(barrier, inc=1, device_id=(me, t), device_id_type=MESH)
        return carry

    lax.fori_loop(1, n_ten, greet, 0)
    pl.semaphore_wait(barrier, n_ten - 1)

    def w_cols(t):
        return w_ref.at[:, pl.ds(pl.multiple_of(t * width, width), width)]

    def w_out(t):
        return pltpu.make_async_remote_copy(
            src_ref=w_cols(t), dst_ref=w_recv.at[mt], send_sem=s_sem.at[t],
            recv_sem=r_sem.at[mt], device_id=(me, t), device_id_type=MESH)

    def w_in(t):
        return pltpu.make_async_remote_copy(
            src_ref=w_cols(t), dst_ref=w_recv.at[t], send_sem=s_sem.at[t],
            recv_sem=r_sem.at[t], device_id=(me, t), device_id_type=MESH)

    own = pltpu.make_async_copy(w_cols(mt), w_recv.at[mt], l_sem.at[0])
    own.start()

    def start(k, carry):
        w_out(lax.rem(mt + k, n_ten)).start()
        return carry

    def wait(k, carry):
        t = lax.rem(mt + k, n_ten)
        w_out(t).wait_send()
        w_in(t).wait_recv()
        return carry

    lax.fori_loop(1, n_ten, start, 0)
    lax.fori_loop(1, n_ten, wait, 0)
    own.wait()


def exchange_weights(w, n_ten):
    any_spec = pl.BlockSpec(memory_space=pl.ANY)
    width = w.shape[1] // n_ten
    return pl.pallas_call(
        functools.partial(weight_kernel, n_ten),
        out_shape=jax.ShapeDtypeStruct((n_ten, w.shape[0], width), w.dtype),
        in_specs=[any_spec],
        out_specs=any_spec,
        scratch_shapes=[
            pltpu.SemaphoreType.DMA((n_ten,)),
            pltpu.SemaphoreType.DMA((n_ten,)),
            pltpu.SemaphoreType.DMA((1,)),
        ],
        compiler_params=pltpu.CompilerParams(collective_id=2, has_side_effects=True),
    )(w)


def attn_kernel(scale, q_ref, meta_ref, pk_ref, pv_ref, ck_ref, cv_ref, nk_ref, nv_ref, o_ref):
    q = q_ref[...]
    meta = meta_ref[...]
    dims = (((1,), (1,)), ((), ()))

    def masked(keys, lo, hi):
        s = lax.dot_general(q, keys, dims, preferred_element_type=jnp.float32) * scale
        k = lax.broadcasted_iota(jnp.int32, s.shape, 1)
        return jnp.where((k >= lo) & (k < hi), s, -jnp.inf)

    s_pre = masked(pk_ref[...], meta[:, 0:1], meta[:, 1:2])
    s_old = masked(ck_ref[...], meta[:, 2:3], meta[:, 3:4])
    s_new = masked(nk_ref[...], meta[:, 4:5], meta[:, 5:6])
    top = jnp.maximum(
        jnp.maximum(jnp.max(s_pre, axis=1, keepdims=True), jnp.max(s_old, axis=1, keepdims=True)),
        jnp.max(s_new, axis=1, keepdims=True),
    )
    e_pre = jnp.exp(s_pre - top)
    e_old = jnp.exp(s_old - top)
    e_new = jnp.exp(s_new - top)
    total = (
        jnp.sum(e_pre, axis=1, keepdims=True)
        + jnp.sum(e_old, axis=1, keepdims=True)
        + jnp.sum(e_new, axis=1, keepdims=True)
    )
    w_pre = (e_pre / total).astype(jnp.bfloat16)
    w_old = (e_old / total).astype(jnp.bfloat16)
    w_new = (e_new / total).astype(jnp.bfloat16)
    out = jnp.dot(w_pre, pv_ref[...], preferred_element_type=jnp.float32)
    out = out + jnp.dot(w_old, cv_ref[...], preferred_element_type=jnp.float32)
    out = out + jnp.dot(w_new, nv_ref[...], preferred_element_type=jnp.float32)
    alive = meta[:, 6:7].astype(jnp.float32)
    o_ref[...] = (out * alive).astype(o_ref.dtype)


def attend_kernel_call(q2, meta, pk, pv, ck2, cv2, nk2, nv2, rows_per_block, q_per_row, old_per_row, new_per_row):
    n_q, width = q2.shape
    qb = rows_per_block * q_per_row
    ob = rows_per_block * old_per_row
    nb = rows_per_block * new_per_row
    full = lambda i: (0, 0)
    return pl.pallas_call(
        functools.partial(attn_kernel, 1.0 / math.sqrt(HEAD_DIM)),
        out_shape=jax.ShapeDtypeStruct((n_q, width), jnp.bfloat16),
        grid=(n_q // qb,),
        in_specs=[
            pl.BlockSpec((qb, width), lambda i: (i, 0)),
            pl.BlockSpec((qb, meta.shape[1]), lambda i: (i, 0)),
            pl.BlockSpec(pk.shape, full),
            pl.BlockSpec(pv.shape, full),
            pl.BlockSpec((ob, width), lambda i: (i, 0)),
            pl.BlockSpec((ob, width), lambda i: (i, 0)),
            pl.BlockSpec((nb, width), lambda i: (i, 0)),
            pl.BlockSpec((nb, width), lambda i: (i, 0)),
        ],
        out_specs=pl.BlockSpec((qb, width), lambda i: (i, 0)),
    )(q2, meta, pk, pv, ck2, cv2, nk2, nv2)


def attend_fused(q, nk, nv, slot_keys, slot_values, slot_of_row, slot_len, old_keys, old_values, old_len, alive, rows_per_block=16):
    rows, steps = q.shape[0], q.shape[1]
    groups = q.shape[2] // HEAD_DIM
    n_slots, pre_max = slot_keys.shape[0], slot_keys.shape[1]
    old_max = old_keys.shape[1]
    local = jnp.arange(rows, dtype=jnp.int32) % rows_per_block
    lo_pre = slot_of_row * pre_max
    hi_pre = lo_pre + slot_len[slot_of_row]
    lo_old = local * old_max
    hi_old = lo_old + old_len
    lo_new = local * steps
    step_id = jnp.arange(steps * groups, dtype=jnp.int32) // groups
    per_row = jnp.stack([lo_pre, hi_pre, lo_old, hi_old, lo_new, alive, alive, alive], axis=1)
    meta = jnp.broadcast_to(per_row[:, None, :], (rows, steps * groups, 8))
    hi_new = lo_new[:, None] + step_id[None, :] + 1
    meta = meta.at[:, :, 5].set(hi_new)
    meta = meta.reshape(rows * steps * groups, 8)
    out = attend_kernel_call(
        q.reshape(rows * steps * groups, HEAD_DIM),
        meta,
        slot_keys.reshape(n_slots * pre_max, HEAD_DIM),
        slot_values.reshape(n_slots * pre_max, HEAD_DIM),
        old_keys.reshape(rows * old_max, HEAD_DIM),
        old_values.reshape(rows * old_max, HEAD_DIM),
        nk.reshape(rows * steps, HEAD_DIM),
        nv.reshape(rows * steps, HEAD_DIM),
        rows_per_block, steps * groups, old_max, steps,
    )
    return out.reshape(rows, steps, groups * HEAD_DIM)


def body(
    residual,
    queries,
    new_keys,
    new_values,
    cache_keys,
    cache_values,
    cache_lengths,
    finished,
    partner,
    row_slot,
    fork_table,
    prompt_keys,
    prompt_values,
    prompt_lengths,
    out_proj,
):
    local_rows = queries.shape[0]
    peer_count = lax.axis_size("replica")
    where_am = lax.axis_index("replica")
    first_id = where_am * local_rows
    held_count = prompt_keys.shape[0]

    owners = fork_table // held_count
    chosen = owners == where_am
    offsets = jnp.sum(jnp.where(chosen, fork_table % held_count, 0), axis=1)
    has_block = jnp.any(chosen, axis=1)[:, None, None]
    zero_value = jnp.zeros((), prompt_keys.dtype)
    both = jnp.concatenate([prompt_keys, prompt_values], axis=2)
    out_both = jnp.where(has_block, both[offsets], zero_value)
    got_both = lax.all_to_all(out_both, "replica", split_axis=0, concat_axis=0, tiled=True)
    n_ten = lax.axis_size("tensor")
    proj_blocks = exchange_weights(out_proj, n_ten)
    got_both, proj_blocks = lax.optimization_barrier((got_both, proj_blocks))
    my_owners = owners[where_am]
    slot_both = got_both[my_owners]
    slot_keys = slot_both[..., : prompt_keys.shape[2]]
    slot_values = slot_both[..., prompt_keys.shape[2] :]
    slot_len = prompt_lengths[fork_table[where_am]]

    peer_of = partner // local_rows
    moved_row = peer_of != where_am
    pairing = (peer_of[None, :] == jnp.arange(peer_count, dtype=jnp.int32)[:, None]) & moved_row[
        None, :
    ]
    peer_row = jnp.sum(
        jnp.where(pairing, jnp.arange(local_rows, dtype=jnp.int32)[None, :], 0), axis=1
    )
    has_row = jnp.any(pairing, axis=1)[:, None, None]
    from_peer = jnp.where(moved_row, peer_of, 0)
    keep_mask = moved_row[:, None, None]
    packed = jnp.concatenate([queries, new_keys, new_values], axis=2)
    outgoing = jnp.where(has_row, packed[peer_row], jnp.zeros((), packed.dtype))
    received = lax.all_to_all(outgoing, "replica", split_axis=0, concat_axis=0, tiled=True)
    use_packed = jnp.where(keep_mask, received[from_peer], packed)
    q_width = queries.shape[2]
    kv_width = new_keys.shape[2]
    use_q = use_packed[..., :q_width]
    use_nk = use_packed[..., q_width : q_width + kv_width]
    use_nv = use_packed[..., q_width + kv_width :]

    own_ids = first_id + jnp.arange(local_rows, dtype=jnp.int32)
    slot_of_row = row_slot[own_ids]
    old_len = cache_lengths[own_ids]
    alive = 1 - finished[own_ids]
    cache_side = attend_fused(
        use_q,
        use_nk,
        use_nv,
        slot_keys,
        slot_values,
        slot_of_row,
        slot_len,
        cache_keys,
        cache_values,
        old_len,
        alive,
    )

    back = jnp.where(has_row, cache_side[peer_row], jnp.zeros((), cache_side.dtype))
    returned = lax.all_to_all(back, "replica", split_axis=0, concat_axis=0, tiled=True)
    heads_out = jnp.where(keep_mask, returned[from_peer], cache_side)

    all_heads = lax.all_gather(heads_out, "tensor", axis=0, tiled=False)
    summed = jnp.einsum(
        "tbsh,thd->bsd", all_heads, proj_blocks, preferred_element_type=jnp.float32
    )
    return (residual.astype(jnp.float32) + summed).astype(jnp.bfloat16)


def solution(mesh):
    in_specs = (
        P("replica", None, "tensor"),
        P("replica", None, "tensor"),
        P("replica", None, "tensor"),
        P("replica", None, "tensor"),
        P("replica", None, "tensor"),
        P("replica", None, "tensor"),
        P(),
        P(),
        P("replica"),
        P(),
        P(),
        P("replica", None, "tensor"),
        P("replica", None, "tensor"),
        P(),
        P("tensor", None),
    )
    out_specs = P("replica", None, "tensor")
    return jax.shard_map(body, mesh=mesh, in_specs=in_specs, out_specs=out_specs, check_vma=False)
```

```python
import math

import jax
import jax.numpy as jnp
from jax import lax
import functools

from jax.experimental import pallas as pl
from jax.experimental.pallas import tpu as pltpu
from jax.sharding import PartitionSpec as P

HEAD_DIM = 128
MESH = pl.DeviceIdType.MESH


def attend_local(q, nk, nv, slot_keys, slot_values, slot_of_row, slot_len, old_keys, old_values, old_len):
    rows, steps = q.shape[0], q.shape[1]
    groups = q.shape[2] // HEAD_DIM
    n_slots, pre_len_max = slot_keys.shape[0], slot_keys.shape[1]
    qs = q.reshape(rows, steps * groups, HEAD_DIM)
    scale = 1.0 / math.sqrt(HEAD_DIM)
    flat_pk = slot_keys.reshape(n_slots * pre_len_max, HEAD_DIM)
    flat_pv = slot_values.reshape(n_slots * pre_len_max, HEAD_DIM)
    part_pre = (
        jnp.einsum("bqd,kd->bqk", qs, flat_pk, preferred_element_type=jnp.float32) * scale
    )
    part_old = (
        jnp.einsum("bqd,btd->bqt", qs, old_keys, preferred_element_type=jnp.float32) * scale
    )
    part_new = jnp.einsum("bqd,btd->bqt", qs, nk, preferred_element_type=jnp.float32) * scale
    key_slot = jnp.arange(n_slots * pre_len_max, dtype=jnp.int32) // pre_len_max
    key_pos = jnp.arange(n_slots * pre_len_max, dtype=jnp.int32) % pre_len_max
    mask_pre = (key_slot[None, :] == slot_of_row[:, None]) & (
        key_pos[None, :] < slot_len[key_slot][None, :]
    )
    mask_old = jnp.arange(old_keys.shape[1], dtype=jnp.int32)[None, :] < old_len[:, None]
    q_step = jnp.arange(steps * groups, dtype=jnp.int32) // groups
    mask_new = jnp.arange(steps, dtype=jnp.int32)[None, :] <= q_step[:, None]
    part_pre = jnp.where(mask_pre[:, None, :], part_pre, -jnp.inf)
    part_old = jnp.where(mask_old[:, None, :], part_old, -jnp.inf)
    part_new = jnp.where(mask_new[None, :, :], part_new, -jnp.inf)
    scores = jnp.concatenate([part_pre, part_old, part_new], axis=-1)
    row_top = jnp.max(scores, axis=-1, keepdims=True)
    exp_scores = jnp.exp(scores - row_top)
    weights = (exp_scores / jnp.sum(exp_scores, axis=-1, keepdims=True)).astype(jnp.bfloat16)
    n_pre = n_slots * pre_len_max
    n_old = old_keys.shape[1]
    mixed = jnp.einsum(
        "bqk,kd->bqd", weights[..., :n_pre], flat_pv, preferred_element_type=jnp.float32
    )
    mixed = mixed + jnp.einsum(
        "bqt,btd->bqd",
        weights[..., n_pre : n_pre + n_old],
        old_values,
        preferred_element_type=jnp.float32,
    )
    mixed = mixed + jnp.einsum(
        "bqt,btd->bqd", weights[..., n_pre + n_old :], nv, preferred_element_type=jnp.float32
    )
    return mixed.reshape(rows, steps, groups * HEAD_DIM)


def weight_kernel(n_ten, w_ref, w_recv, s_sem, r_sem, l_sem):
    me = lax.axis_index("replica")
    mt = lax.axis_index("tensor")
    width = w_recv.shape[2]
    barrier = pltpu.get_barrier_semaphore()

    def greet(k, carry):
        t = lax.rem(mt + k, n_ten)
        pl.semaphore_signal(barrier, inc=1, device_id=(me, t), device_id_type=MESH)
        return carry

    lax.fori_loop(1, n_ten, greet, 0)
    pl.semaphore_wait(barrier, n_ten - 1)

    def w_cols(t):
        return w_ref.at[:, pl.ds(pl.multiple_of(t * width, width), width)]

    def w_out(t):
        return pltpu.make_async_remote_copy(
            src_ref=w_cols(t), dst_ref=w_recv.at[mt], send_sem=s_sem.at[t],
            recv_sem=r_sem.at[mt], device_id=(me, t), device_id_type=MESH)

    def w_in(t):
        return pltpu.make_async_remote_copy(
            src_ref=w_cols(t), dst_ref=w_recv.at[t], send_sem=s_sem.at[t],
            recv_sem=r_sem.at[t], device_id=(me, t), device_id_type=MESH)

    own = pltpu.make_async_copy(w_cols(mt), w_recv.at[mt], l_sem.at[0])
    own.start()

    def start(k, carry):
        w_out(lax.rem(mt + k, n_ten)).start()
        return carry

    def wait(k, carry):
        t = lax.rem(mt + k, n_ten)
        w_out(t).wait_send()
        w_in(t).wait_recv()
        return carry

    lax.fori_loop(1, n_ten, start, 0)
    lax.fori_loop(1, n_ten, wait, 0)
    own.wait()


def exchange_weights(w, n_ten):
    any_spec = pl.BlockSpec(memory_space=pl.ANY)
    width = w.shape[1] // n_ten
    return pl.pallas_call(
        functools.partial(weight_kernel, n_ten),
        out_shape=jax.ShapeDtypeStruct((n_ten, w.shape[0], width), w.dtype),
        in_specs=[any_spec],
        out_specs=any_spec,
        scratch_shapes=[
            pltpu.SemaphoreType.DMA((n_ten,)),
            pltpu.SemaphoreType.DMA((n_ten,)),
            pltpu.SemaphoreType.DMA((1,)),
        ],
        compiler_params=pltpu.CompilerParams(collective_id=2, has_side_effects=True),
    )(w)


def project_kernel(n_ten, h_ref, w_ref, o_ref, held, s_sem, r_sem):
    me = lax.axis_index("replica")
    mt = lax.axis_index("tensor")
    barrier = pltpu.get_barrier_semaphore()
    for k in range(1, n_ten):
        t = lax.rem(mt + k, n_ten)
        pl.semaphore_signal(barrier, inc=1, device_id=(me, t), device_id_type=MESH)
    pl.semaphore_wait(barrier, n_ten - 1)

    def send(t):
        return pltpu.make_async_remote_copy(
            src_ref=h_ref, dst_ref=held.at[mt], send_sem=s_sem.at[t],
            recv_sem=r_sem.at[mt], device_id=(me, t), device_id_type=MESH)

    def arrive(t):
        return pltpu.make_async_remote_copy(
            src_ref=h_ref, dst_ref=held.at[t], send_sem=s_sem.at[t],
            recv_sem=r_sem.at[t], device_id=(me, t), device_id_type=MESH)

    for k in range(1, n_ten):
        send(lax.rem(mt + k, n_ten)).start()
    o_ref[...] = jnp.dot(h_ref[...], w_ref[mt], preferred_element_type=jnp.float32)
    for k in range(1, n_ten):
        t = lax.rem(mt + n_ten - k, n_ten)
        arrive(t).wait_recv()
        o_ref[...] += jnp.dot(held[t], w_ref[t], preferred_element_type=jnp.float32)
    for k in range(1, n_ten):
        send(lax.rem(mt + k, n_ten)).wait_send()


def gather_project(h, w_blocks, n_ten):
    vmem = pl.BlockSpec(memory_space=pltpu.VMEM)
    return pl.pallas_call(
        functools.partial(project_kernel, n_ten),
        out_shape=jax.ShapeDtypeStruct((h.shape[0], w_blocks.shape[2]), jnp.float32),
        in_specs=[vmem, vmem],
        out_specs=vmem,
        scratch_shapes=[
            pltpu.VMEM((n_ten,) + h.shape, h.dtype),
            pltpu.SemaphoreType.DMA((n_ten,)),
            pltpu.SemaphoreType.DMA((n_ten,)),
        ],
        compiler_params=pltpu.CompilerParams(collective_id=3, has_side_effects=True),
    )(h, w_blocks)


def attn_kernel(scale, q_ref, meta_ref, pk_ref, pv_ref, ck_ref, cv_ref, nk_ref, nv_ref, o_ref):
    q = q_ref[...]
    meta = meta_ref[...]
    dims = (((1,), (1,)), ((), ()))

    def masked(keys, lo, hi):
        s = lax.dot_general(q, keys, dims, preferred_element_type=jnp.float32) * scale
        k = lax.broadcasted_iota(jnp.int32, s.shape, 1)
        return jnp.where((k >= lo) & (k < hi), s, -jnp.inf)

    s_pre = masked(pk_ref[...], meta[:, 0:1], meta[:, 1:2])
    s_old = masked(ck_ref[...], meta[:, 2:3], meta[:, 3:4])
    s_new = masked(nk_ref[...], meta[:, 4:5], meta[:, 5:6])
    top = jnp.maximum(
        jnp.maximum(jnp.max(s_pre, axis=1, keepdims=True), jnp.max(s_old, axis=1, keepdims=True)),
        jnp.max(s_new, axis=1, keepdims=True),
    )
    e_pre = jnp.exp(s_pre - top)
    e_old = jnp.exp(s_old - top)
    e_new = jnp.exp(s_new - top)
    total = (
        jnp.sum(e_pre, axis=1, keepdims=True)
        + jnp.sum(e_old, axis=1, keepdims=True)
        + jnp.sum(e_new, axis=1, keepdims=True)
    )
    w_pre = (e_pre / total).astype(jnp.bfloat16)
    w_old = (e_old / total).astype(jnp.bfloat16)
    w_new = (e_new / total).astype(jnp.bfloat16)
    out = jnp.dot(w_pre, pv_ref[...], preferred_element_type=jnp.float32)
    out = out + jnp.dot(w_old, cv_ref[...], preferred_element_type=jnp.float32)
    out = out + jnp.dot(w_new, nv_ref[...], preferred_element_type=jnp.float32)
    alive = meta[:, 6:7].astype(jnp.float32)
    o_ref[...] = (out * alive).astype(o_ref.dtype)


def attend_kernel_call(q2, meta, pk, pv, ck2, cv2, nk2, nv2, rows_per_block, q_per_row, old_per_row, new_per_row):
    n_q, width = q2.shape
    qb = rows_per_block * q_per_row
    ob = rows_per_block * old_per_row
    nb = rows_per_block * new_per_row
    full = lambda i: (0, 0)
    return pl.pallas_call(
        functools.partial(attn_kernel, 1.0 / math.sqrt(HEAD_DIM)),
        out_shape=jax.ShapeDtypeStruct((n_q, width), jnp.bfloat16),
        grid=(n_q // qb,),
        in_specs=[
            pl.BlockSpec((qb, width), lambda i: (i, 0)),
            pl.BlockSpec((qb, meta.shape[1]), lambda i: (i, 0)),
            pl.BlockSpec(pk.shape, full),
            pl.BlockSpec(pv.shape, full),
            pl.BlockSpec((ob, width), lambda i: (i, 0)),
            pl.BlockSpec((ob, width), lambda i: (i, 0)),
            pl.BlockSpec((nb, width), lambda i: (i, 0)),
            pl.BlockSpec((nb, width), lambda i: (i, 0)),
        ],
        out_specs=pl.BlockSpec((qb, width), lambda i: (i, 0)),
    )(q2, meta, pk, pv, ck2, cv2, nk2, nv2)


def attend_fused(q, nk, nv, slot_keys, slot_values, slot_of_row, slot_len, old_keys, old_values, old_len, alive, rows_per_block=8):
    rows, steps = q.shape[0], q.shape[1]
    groups = q.shape[2] // HEAD_DIM
    n_slots, pre_max = slot_keys.shape[0], slot_keys.shape[1]
    old_max = old_keys.shape[1]
    local = jnp.arange(rows, dtype=jnp.int32) % rows_per_block
    lo_pre = slot_of_row * pre_max
    hi_pre = lo_pre + slot_len[slot_of_row]
    lo_old = local * old_max
    hi_old = lo_old + old_len
    lo_new = local * steps
    step_id = jnp.arange(steps * groups, dtype=jnp.int32) // groups
    per_row = jnp.stack([lo_pre, hi_pre, lo_old, hi_old, lo_new, alive, alive, alive], axis=1)
    meta = jnp.broadcast_to(per_row[:, None, :], (rows, steps * groups, 8))
    hi_new = lo_new[:, None] + step_id[None, :] + 1
    meta = meta.at[:, :, 5].set(hi_new)
    meta = meta.reshape(rows * steps * groups, 8)
    out = attend_kernel_call(
        q.reshape(rows * steps * groups, HEAD_DIM),
        meta,
        slot_keys.reshape(n_slots * pre_max, HEAD_DIM),
        slot_values.reshape(n_slots * pre_max, HEAD_DIM),
        old_keys.reshape(rows * old_max, HEAD_DIM),
        old_values.reshape(rows * old_max, HEAD_DIM),
        nk.reshape(rows * steps, HEAD_DIM),
        nv.reshape(rows * steps, HEAD_DIM),
        rows_per_block, steps * groups, old_max, steps,
    )
    return out.reshape(rows, steps, groups * HEAD_DIM)


def body(
    residual,
    queries,
    new_keys,
    new_values,
    cache_keys,
    cache_values,
    cache_lengths,
    finished,
    partner,
    row_slot,
    fork_table,
    prompt_keys,
    prompt_values,
    prompt_lengths,
    out_proj,
):
    local_rows = queries.shape[0]
    peer_count = lax.axis_size("replica")
    where_am = lax.axis_index("replica")
    first_id = where_am * local_rows
    held_count = prompt_keys.shape[0]

    owners = fork_table // held_count
    chosen = owners == where_am
    offsets = jnp.sum(jnp.where(chosen, fork_table % held_count, 0), axis=1)
    has_block = jnp.any(chosen, axis=1)[:, None, None]
    zero_value = jnp.zeros((), prompt_keys.dtype)
    both = jnp.concatenate([prompt_keys, prompt_values], axis=2)
    out_both = jnp.where(has_block, both[offsets], zero_value)
    got_both = lax.all_to_all(out_both, "replica", split_axis=0, concat_axis=0, tiled=True)
    n_ten = lax.axis_size("tensor")
    proj_blocks = exchange_weights(out_proj, n_ten)
    got_both, proj_blocks = lax.optimization_barrier((got_both, proj_blocks))
    my_owners = owners[where_am]
    slot_both = got_both[my_owners]
    slot_keys = slot_both[..., : prompt_keys.shape[2]]
    slot_values = slot_both[..., prompt_keys.shape[2] :]
    slot_len = prompt_lengths[fork_table[where_am]]

    peer_of = partner // local_rows
    moved_row = peer_of != where_am
    pairing = (peer_of[None, :] == jnp.arange(peer_count, dtype=jnp.int32)[:, None]) & moved_row[
        None, :
    ]
    peer_row = jnp.sum(
        jnp.where(pairing, jnp.arange(local_rows, dtype=jnp.int32)[None, :], 0), axis=1
    )
    has_row = jnp.any(pairing, axis=1)[:, None, None]
    from_peer = jnp.where(moved_row, peer_of, 0)
    keep_mask = moved_row[:, None, None]
    packed = jnp.concatenate([queries, new_keys, new_values], axis=2)
    outgoing = jnp.where(has_row, packed[peer_row], jnp.zeros((), packed.dtype))
    received = lax.all_to_all(outgoing, "replica", split_axis=0, concat_axis=0, tiled=True)
    use_packed = jnp.where(keep_mask, received[from_peer], packed)
    q_width = queries.shape[2]
    kv_width = new_keys.shape[2]
    use_q = use_packed[..., :q_width]
    use_nk = use_packed[..., q_width : q_width + kv_width]
    use_nv = use_packed[..., q_width + kv_width :]

    own_ids = first_id + jnp.arange(local_rows, dtype=jnp.int32)
    slot_of_row = row_slot[own_ids]
    old_len = cache_lengths[own_ids]
    alive = 1 - finished[own_ids]
    cache_side = attend_fused(
        use_q,
        use_nk,
        use_nv,
        slot_keys,
        slot_values,
        slot_of_row,
        slot_len,
        cache_keys,
        cache_values,
        old_len,
        alive,
    )

    back = jnp.where(has_row, cache_side[peer_row], jnp.zeros((), cache_side.dtype))
    returned = lax.all_to_all(back, "replica", split_axis=0, concat_axis=0, tiled=True)
    heads_out = jnp.where(keep_mask, returned[from_peer], cache_side)

    flat_heads = heads_out.reshape(-1, heads_out.shape[2])
    summed = gather_project(flat_heads, proj_blocks, n_ten).reshape(residual.shape)
    return (residual.astype(jnp.float32) + summed).astype(jnp.bfloat16)


def solution(mesh):
    in_specs = (
        P("replica", None, "tensor"),
        P("replica", None, "tensor"),
        P("replica", None, "tensor"),
        P("replica", None, "tensor"),
        P("replica", None, "tensor"),
        P("replica", None, "tensor"),
        P(),
        P(),
        P("replica"),
        P(),
        P(),
        P("replica", None, "tensor"),
        P("replica", None, "tensor"),
        P(),
        P("tensor", None),
    )
    out_specs = P("replica", None, "tensor")
    return jax.shard_map(body, mesh=mesh, in_specs=in_specs, out_specs=out_specs, check_vma=False)
```

```python
import math

import jax
import jax.numpy as jnp
from jax import lax
import functools

from jax.experimental import pallas as pl
from jax.experimental.pallas import tpu as pltpu
from jax.sharding import PartitionSpec as P

HEAD_DIM = 128
MESH = pl.DeviceIdType.MESH


def attend_local(q, nk, nv, slot_keys, slot_values, slot_of_row, slot_len, old_keys, old_values, old_len):
    rows, steps = q.shape[0], q.shape[1]
    groups = q.shape[2] // HEAD_DIM
    n_slots, pre_len_max = slot_keys.shape[0], slot_keys.shape[1]
    qs = q.reshape(rows, steps * groups, HEAD_DIM)
    scale = 1.0 / math.sqrt(HEAD_DIM)
    flat_pk = slot_keys.reshape(n_slots * pre_len_max, HEAD_DIM)
    flat_pv = slot_values.reshape(n_slots * pre_len_max, HEAD_DIM)
    part_pre = (
        jnp.einsum("bqd,kd->bqk", qs, flat_pk, preferred_element_type=jnp.float32) * scale
    )
    part_old = (
        jnp.einsum("bqd,btd->bqt", qs, old_keys, preferred_element_type=jnp.float32) * scale
    )
    part_new = jnp.einsum("bqd,btd->bqt", qs, nk, preferred_element_type=jnp.float32) * scale
    key_slot = jnp.arange(n_slots * pre_len_max, dtype=jnp.int32) // pre_len_max
    key_pos = jnp.arange(n_slots * pre_len_max, dtype=jnp.int32) % pre_len_max
    mask_pre = (key_slot[None, :] == slot_of_row[:, None]) & (
        key_pos[None, :] < slot_len[key_slot][None, :]
    )
    mask_old = jnp.arange(old_keys.shape[1], dtype=jnp.int32)[None, :] < old_len[:, None]
    q_step = jnp.arange(steps * groups, dtype=jnp.int32) // groups
    mask_new = jnp.arange(steps, dtype=jnp.int32)[None, :] <= q_step[:, None]
    part_pre = jnp.where(mask_pre[:, None, :], part_pre, -jnp.inf)
    part_old = jnp.where(mask_old[:, None, :], part_old, -jnp.inf)
    part_new = jnp.where(mask_new[None, :, :], part_new, -jnp.inf)
    scores = jnp.concatenate([part_pre, part_old, part_new], axis=-1)
    row_top = jnp.max(scores, axis=-1, keepdims=True)
    exp_scores = jnp.exp(scores - row_top)
    weights = (exp_scores / jnp.sum(exp_scores, axis=-1, keepdims=True)).astype(jnp.bfloat16)
    n_pre = n_slots * pre_len_max
    n_old = old_keys.shape[1]
    mixed = jnp.einsum(
        "bqk,kd->bqd", weights[..., :n_pre], flat_pv, preferred_element_type=jnp.float32
    )
    mixed = mixed + jnp.einsum(
        "bqt,btd->bqd",
        weights[..., n_pre : n_pre + n_old],
        old_values,
        preferred_element_type=jnp.float32,
    )
    mixed = mixed + jnp.einsum(
        "bqt,btd->bqd", weights[..., n_pre + n_old :], nv, preferred_element_type=jnp.float32
    )
    return mixed.reshape(rows, steps, groups * HEAD_DIM)


def weight_kernel(n_ten, w_ref, w_recv, s_sem, r_sem, l_sem):
    me = lax.axis_index("replica")
    mt = lax.axis_index("tensor")
    width = w_recv.shape[2]
    barrier = pltpu.get_barrier_semaphore()

    def greet(k, carry):
        t = lax.rem(mt + k, n_ten)
        pl.semaphore_signal(barrier, inc=1, device_id=(me, t), device_id_type=MESH)
        return carry

    lax.fori_loop(1, n_ten, greet, 0)
    pl.semaphore_wait(barrier, n_ten - 1)

    def w_cols(t):
        return w_ref.at[:, pl.ds(pl.multiple_of(t * width, width), width)]

    def w_out(t):
        return pltpu.make_async_remote_copy(
            src_ref=w_cols(t), dst_ref=w_recv.at[mt], send_sem=s_sem.at[t],
            recv_sem=r_sem.at[mt], device_id=(me, t), device_id_type=MESH)

    def w_in(t):
        return pltpu.make_async_remote_copy(
            src_ref=w_cols(t), dst_ref=w_recv.at[t], send_sem=s_sem.at[t],
            recv_sem=r_sem.at[t], device_id=(me, t), device_id_type=MESH)

    own = pltpu.make_async_copy(w_cols(mt), w_recv.at[mt], l_sem.at[0])
    own.start()

    def start(k, carry):
        w_out(lax.rem(mt + k, n_ten)).start()
        return carry

    def wait(k, carry):
        t = lax.rem(mt + k, n_ten)
        w_out(t).wait_send()
        w_in(t).wait_recv()
        return carry

    lax.fori_loop(1, n_ten, start, 0)
    lax.fori_loop(1, n_ten, wait, 0)
    own.wait()


def exchange_weights(w, n_ten):
    any_spec = pl.BlockSpec(memory_space=pl.ANY)
    width = w.shape[1] // n_ten
    return pl.pallas_call(
        functools.partial(weight_kernel, n_ten),
        out_shape=jax.ShapeDtypeStruct((n_ten, w.shape[0], width), w.dtype),
        in_specs=[any_spec],
        out_specs=any_spec,
        scratch_shapes=[
            pltpu.SemaphoreType.DMA((n_ten,)),
            pltpu.SemaphoreType.DMA((n_ten,)),
            pltpu.SemaphoreType.DMA((1,)),
        ],
        compiler_params=pltpu.CompilerParams(collective_id=2, has_side_effects=True),
    )(w)


def project_kernel(n_ten, h_ref, w_ref, o_ref, held, s_sem, r_sem):
    me = lax.axis_index("replica")
    mt = lax.axis_index("tensor")
    barrier = pltpu.get_barrier_semaphore()
    for k in range(1, n_ten):
        t = lax.rem(mt + k, n_ten)
        pl.semaphore_signal(barrier, inc=1, device_id=(me, t), device_id_type=MESH)
    pl.semaphore_wait(barrier, n_ten - 1)

    def send(t):
        return pltpu.make_async_remote_copy(
            src_ref=h_ref, dst_ref=held.at[mt], send_sem=s_sem.at[t],
            recv_sem=r_sem.at[mt], device_id=(me, t), device_id_type=MESH)

    def arrive(t):
        return pltpu.make_async_remote_copy(
            src_ref=h_ref, dst_ref=held.at[t], send_sem=s_sem.at[t],
            recv_sem=r_sem.at[t], device_id=(me, t), device_id_type=MESH)

    for k in range(1, n_ten):
        send(lax.rem(mt + k, n_ten)).start()
    o_ref[...] = jnp.dot(h_ref[...], w_ref[mt], preferred_element_type=jnp.float32)
    for k in range(1, n_ten):
        t = lax.rem(mt + n_ten - k, n_ten)
        arrive(t).wait_recv()
        o_ref[...] += jnp.dot(held[t], w_ref[t], preferred_element_type=jnp.float32)
    for k in range(1, n_ten):
        send(lax.rem(mt + k, n_ten)).wait_send()


def gather_project(h, w_blocks, n_ten, cid):
    vmem = pl.BlockSpec(memory_space=pltpu.VMEM)
    return pl.pallas_call(
        functools.partial(project_kernel, n_ten),
        out_shape=jax.ShapeDtypeStruct((h.shape[0], w_blocks.shape[2]), jnp.float32),
        in_specs=[vmem, vmem],
        out_specs=vmem,
        scratch_shapes=[
            pltpu.VMEM((n_ten,) + h.shape, h.dtype),
            pltpu.SemaphoreType.DMA((n_ten,)),
            pltpu.SemaphoreType.DMA((n_ten,)),
        ],
        compiler_params=pltpu.CompilerParams(collective_id=cid, has_side_effects=True),
    )(h, w_blocks)


def attn_kernel(scale, q_ref, meta_ref, pk_ref, pv_ref, ck_ref, cv_ref, nk_ref, nv_ref, o_ref):
    q = q_ref[...]
    meta = meta_ref[...]
    dims = (((1,), (1,)), ((), ()))

    def masked(keys, lo, hi):
        s = lax.dot_general(q, keys, dims, preferred_element_type=jnp.float32) * scale
        k = lax.broadcasted_iota(jnp.int32, s.shape, 1)
        return jnp.where((k >= lo) & (k < hi), s, -jnp.inf)

    s_pre = masked(pk_ref[...], meta[:, 0:1], meta[:, 1:2])
    s_old = masked(ck_ref[...], meta[:, 2:3], meta[:, 3:4])
    s_new = masked(nk_ref[...], meta[:, 4:5], meta[:, 5:6])
    top = jnp.maximum(
        jnp.maximum(jnp.max(s_pre, axis=1, keepdims=True), jnp.max(s_old, axis=1, keepdims=True)),
        jnp.max(s_new, axis=1, keepdims=True),
    )
    e_pre = jnp.exp(s_pre - top)
    e_old = jnp.exp(s_old - top)
    e_new = jnp.exp(s_new - top)
    total = (
        jnp.sum(e_pre, axis=1, keepdims=True)
        + jnp.sum(e_old, axis=1, keepdims=True)
        + jnp.sum(e_new, axis=1, keepdims=True)
    )
    w_pre = (e_pre / total).astype(jnp.bfloat16)
    w_old = (e_old / total).astype(jnp.bfloat16)
    w_new = (e_new / total).astype(jnp.bfloat16)
    out = jnp.dot(w_pre, pv_ref[...], preferred_element_type=jnp.float32)
    out = out + jnp.dot(w_old, cv_ref[...], preferred_element_type=jnp.float32)
    out = out + jnp.dot(w_new, nv_ref[...], preferred_element_type=jnp.float32)
    alive = meta[:, 6:7].astype(jnp.float32)
    o_ref[...] = (out * alive).astype(o_ref.dtype)


def attend_kernel_call(q2, meta, pk, pv, ck2, cv2, nk2, nv2, rows_per_block, q_per_row, old_per_row, new_per_row):
    n_q, width = q2.shape
    qb = rows_per_block * q_per_row
    ob = rows_per_block * old_per_row
    nb = rows_per_block * new_per_row
    full = lambda i: (0, 0)
    return pl.pallas_call(
        functools.partial(attn_kernel, 1.0 / math.sqrt(HEAD_DIM)),
        out_shape=jax.ShapeDtypeStruct((n_q, width), jnp.bfloat16),
        grid=(n_q // qb,),
        in_specs=[
            pl.BlockSpec((qb, width), lambda i: (i, 0)),
            pl.BlockSpec((qb, meta.shape[1]), lambda i: (i, 0)),
            pl.BlockSpec(pk.shape, full),
            pl.BlockSpec(pv.shape, full),
            pl.BlockSpec((ob, width), lambda i: (i, 0)),
            pl.BlockSpec((ob, width), lambda i: (i, 0)),
            pl.BlockSpec((nb, width), lambda i: (i, 0)),
            pl.BlockSpec((nb, width), lambda i: (i, 0)),
        ],
        out_specs=pl.BlockSpec((qb, width), lambda i: (i, 0)),
    )(q2, meta, pk, pv, ck2, cv2, nk2, nv2)


def attend_fused(q, nk, nv, slot_keys, slot_values, slot_of_row, slot_len, old_keys, old_values, old_len, alive, rows_per_block=8):
    rows, steps = q.shape[0], q.shape[1]
    groups = q.shape[2] // HEAD_DIM
    n_slots, pre_max = slot_keys.shape[0], slot_keys.shape[1]
    old_max = old_keys.shape[1]
    local = jnp.arange(rows, dtype=jnp.int32) % rows_per_block
    lo_pre = slot_of_row * pre_max
    hi_pre = lo_pre + slot_len[slot_of_row]
    lo_old = local * old_max
    hi_old = lo_old + old_len
    lo_new = local * steps
    step_id = jnp.arange(steps * groups, dtype=jnp.int32) // groups
    per_row = jnp.stack([lo_pre, hi_pre, lo_old, hi_old, lo_new, alive, alive, alive], axis=1)
    meta = jnp.broadcast_to(per_row[:, None, :], (rows, steps * groups, 8))
    hi_new = lo_new[:, None] + step_id[None, :] + 1
    meta = meta.at[:, :, 5].set(hi_new)
    meta = meta.reshape(rows * steps * groups, 8)
    out = attend_kernel_call(
        q.reshape(rows * steps * groups, HEAD_DIM),
        meta,
        slot_keys.reshape(n_slots * pre_max, HEAD_DIM),
        slot_values.reshape(n_slots * pre_max, HEAD_DIM),
        old_keys.reshape(rows * old_max, HEAD_DIM),
        old_values.reshape(rows * old_max, HEAD_DIM),
        nk.reshape(rows * steps, HEAD_DIM),
        nv.reshape(rows * steps, HEAD_DIM),
        rows_per_block, steps * groups, old_max, steps,
    )
    return out.reshape(rows, steps, groups * HEAD_DIM)


def body(
    residual,
    queries,
    new_keys,
    new_values,
    cache_keys,
    cache_values,
    cache_lengths,
    finished,
    partner,
    row_slot,
    fork_table,
    prompt_keys,
    prompt_values,
    prompt_lengths,
    out_proj,
):
    local_rows = queries.shape[0]
    peer_count = lax.axis_size("replica")
    where_am = lax.axis_index("replica")
    first_id = where_am * local_rows
    held_count = prompt_keys.shape[0]

    owners = fork_table // held_count
    chosen = owners == where_am
    offsets = jnp.sum(jnp.where(chosen, fork_table % held_count, 0), axis=1)
    has_block = jnp.any(chosen, axis=1)[:, None, None]
    zero_value = jnp.zeros((), prompt_keys.dtype)
    both = jnp.concatenate([prompt_keys, prompt_values], axis=2)
    out_both = jnp.where(has_block, both[offsets], zero_value)
    got_both = lax.all_to_all(out_both, "replica", split_axis=0, concat_axis=0, tiled=True)
    n_ten = lax.axis_size("tensor")
    proj_blocks = exchange_weights(out_proj, n_ten)
    got_both, proj_blocks = lax.optimization_barrier((got_both, proj_blocks))
    my_owners = owners[where_am]
    slot_both = got_both[my_owners]
    slot_keys = slot_both[..., : prompt_keys.shape[2]]
    slot_values = slot_both[..., prompt_keys.shape[2] :]
    slot_len = prompt_lengths[fork_table[where_am]]

    peer_of = partner // local_rows
    moved_row = peer_of != where_am
    pairing = (peer_of[None, :] == jnp.arange(peer_count, dtype=jnp.int32)[:, None]) & moved_row[
        None, :
    ]
    peer_row = jnp.sum(
        jnp.where(pairing, jnp.arange(local_rows, dtype=jnp.int32)[None, :], 0), axis=1
    )
    has_row = jnp.any(pairing, axis=1)[:, None, None]
    from_peer = jnp.where(moved_row, peer_of, 0)
    keep_mask = moved_row[:, None, None]
    packed = jnp.concatenate([queries, new_keys, new_values], axis=2)
    outgoing = jnp.where(has_row, packed[peer_row], jnp.zeros((), packed.dtype))
    received = lax.all_to_all(outgoing, "replica", split_axis=0, concat_axis=0, tiled=True)
    use_packed = jnp.where(keep_mask, received[from_peer], packed)
    q_width = queries.shape[2]
    kv_width = new_keys.shape[2]
    use_q = use_packed[..., :q_width]
    use_nk = use_packed[..., q_width : q_width + kv_width]
    use_nv = use_packed[..., q_width + kv_width :]

    own_ids = first_id + jnp.arange(local_rows, dtype=jnp.int32)
    slot_of_row = row_slot[own_ids]
    old_len = cache_lengths[own_ids]
    alive = 1 - finished[own_ids]
    cache_side = attend_fused(
        use_q,
        use_nk,
        use_nv,
        slot_keys,
        slot_values,
        slot_of_row,
        slot_len,
        cache_keys,
        cache_values,
        old_len,
        alive,
    )

    back = jnp.where(has_row, cache_side[peer_row], jnp.zeros((), cache_side.dtype))
    returned = lax.all_to_all(back, "replica", split_axis=0, concat_axis=0, tiled=True)

    stayed = jnp.where(keep_mask, jnp.zeros((), cache_side.dtype), cache_side)
    summed = gather_project(stayed.reshape(-1, stayed.shape[2]), proj_blocks, n_ten, 3)
    summed = summed.reshape(residual.shape)
    move_count = peer_count // 2
    moved_ids = jnp.nonzero(moved_row, size=move_count, fill_value=0)[0]
    valid = jnp.arange(move_count) < jnp.sum(moved_row)
    moved_heads = returned[peer_of[moved_ids]]
    moved_heads = jnp.where(valid[:, None, None], moved_heads, jnp.zeros((), moved_heads.dtype))
    moved_sum = gather_project(moved_heads.reshape(-1, moved_heads.shape[2]), proj_blocks, n_ten, 4)
    summed = summed.at[moved_ids].add(moved_sum.reshape(moved_heads.shape[:2] + summed.shape[2:]))
    return (residual.astype(jnp.float32) + summed).astype(jnp.bfloat16)


def solution(mesh):
    in_specs = (
        P("replica", None, "tensor"),
        P("replica", None, "tensor"),
        P("replica", None, "tensor"),
        P("replica", None, "tensor"),
        P("replica", None, "tensor"),
        P("replica", None, "tensor"),
        P(),
        P(),
        P("replica"),
        P(),
        P(),
        P("replica", None, "tensor"),
        P("replica", None, "tensor"),
        P(),
        P("tensor", None),
    )
    out_specs = P("replica", None, "tensor")
    return jax.shard_map(body, mesh=mesh, in_specs=in_specs, out_specs=out_specs, check_vma=False)
```

```python
import math

import jax
import jax.numpy as jnp
from jax import lax
import functools

from jax.experimental import pallas as pl
from jax.experimental.pallas import tpu as pltpu
from jax.sharding import PartitionSpec as P

HEAD_DIM = 128
MESH = pl.DeviceIdType.MESH


def attend_local(q, nk, nv, slot_keys, slot_values, slot_of_row, slot_len, old_keys, old_values, old_len):
    rows, steps = q.shape[0], q.shape[1]
    groups = q.shape[2] // HEAD_DIM
    n_slots, pre_len_max = slot_keys.shape[0], slot_keys.shape[1]
    qs = q.reshape(rows, steps * groups, HEAD_DIM)
    scale = 1.0 / math.sqrt(HEAD_DIM)
    flat_pk = slot_keys.reshape(n_slots * pre_len_max, HEAD_DIM)
    flat_pv = slot_values.reshape(n_slots * pre_len_max, HEAD_DIM)
    part_pre = (
        jnp.einsum("bqd,kd->bqk", qs, flat_pk, preferred_element_type=jnp.float32) * scale
    )
    part_old = (
        jnp.einsum("bqd,btd->bqt", qs, old_keys, preferred_element_type=jnp.float32) * scale
    )
    part_new = jnp.einsum("bqd,btd->bqt", qs, nk, preferred_element_type=jnp.float32) * scale
    key_slot = jnp.arange(n_slots * pre_len_max, dtype=jnp.int32) // pre_len_max
    key_pos = jnp.arange(n_slots * pre_len_max, dtype=jnp.int32) % pre_len_max
    mask_pre = (key_slot[None, :] == slot_of_row[:, None]) & (
        key_pos[None, :] < slot_len[key_slot][None, :]
    )
    mask_old = jnp.arange(old_keys.shape[1], dtype=jnp.int32)[None, :] < old_len[:, None]
    q_step = jnp.arange(steps * groups, dtype=jnp.int32) // groups
    mask_new = jnp.arange(steps, dtype=jnp.int32)[None, :] <= q_step[:, None]
    part_pre = jnp.where(mask_pre[:, None, :], part_pre, -jnp.inf)
    part_old = jnp.where(mask_old[:, None, :], part_old, -jnp.inf)
    part_new = jnp.where(mask_new[None, :, :], part_new, -jnp.inf)
    scores = jnp.concatenate([part_pre, part_old, part_new], axis=-1)
    row_top = jnp.max(scores, axis=-1, keepdims=True)
    exp_scores = jnp.exp(scores - row_top)
    weights = (exp_scores / jnp.sum(exp_scores, axis=-1, keepdims=True)).astype(jnp.bfloat16)
    n_pre = n_slots * pre_len_max
    n_old = old_keys.shape[1]
    mixed = jnp.einsum(
        "bqk,kd->bqd", weights[..., :n_pre], flat_pv, preferred_element_type=jnp.float32
    )
    mixed = mixed + jnp.einsum(
        "bqt,btd->bqd",
        weights[..., n_pre : n_pre + n_old],
        old_values,
        preferred_element_type=jnp.float32,
    )
    mixed = mixed + jnp.einsum(
        "bqt,btd->bqd", weights[..., n_pre + n_old :], nv, preferred_element_type=jnp.float32
    )
    return mixed.reshape(rows, steps, groups * HEAD_DIM)


def weight_kernel(n_ten, w_ref, w_recv, s_sem, r_sem, l_sem):
    me = lax.axis_index("replica")
    mt = lax.axis_index("tensor")
    width = w_recv.shape[2]
    barrier = pltpu.get_barrier_semaphore()

    def greet(k, carry):
        t = lax.rem(mt + k, n_ten)
        pl.semaphore_signal(barrier, inc=1, device_id=(me, t), device_id_type=MESH)
        return carry

    lax.fori_loop(1, n_ten, greet, 0)
    pl.semaphore_wait(barrier, n_ten - 1)

    def w_cols(t):
        return w_ref.at[:, pl.ds(pl.multiple_of(t * width, width), width)]

    def w_out(t):
        return pltpu.make_async_remote_copy(
            src_ref=w_cols(t), dst_ref=w_recv.at[mt], send_sem=s_sem.at[t],
            recv_sem=r_sem.at[mt], device_id=(me, t), device_id_type=MESH)

    def w_in(t):
        return pltpu.make_async_remote_copy(
            src_ref=w_cols(t), dst_ref=w_recv.at[t], send_sem=s_sem.at[t],
            recv_sem=r_sem.at[t], device_id=(me, t), device_id_type=MESH)

    own = pltpu.make_async_copy(w_cols(mt), w_recv.at[mt], l_sem.at[0])
    own.start()

    def start(k, carry):
        w_out(lax.rem(mt + k, n_ten)).start()
        return carry

    def wait(k, carry):
        t = lax.rem(mt + k, n_ten)
        w_out(t).wait_send()
        w_in(t).wait_recv()
        return carry

    lax.fori_loop(1, n_ten, start, 0)
    lax.fori_loop(1, n_ten, wait, 0)
    own.wait()


def exchange_weights(w, n_ten):
    any_spec = pl.BlockSpec(memory_space=pl.ANY)
    width = w.shape[1] // n_ten
    return pl.pallas_call(
        functools.partial(weight_kernel, n_ten),
        out_shape=jax.ShapeDtypeStruct((n_ten, w.shape[0], width), w.dtype),
        in_specs=[any_spec],
        out_specs=any_spec,
        scratch_shapes=[
            pltpu.SemaphoreType.DMA((n_ten,)),
            pltpu.SemaphoreType.DMA((n_ten,)),
            pltpu.SemaphoreType.DMA((1,)),
        ],
        compiler_params=pltpu.CompilerParams(collective_id=2, has_side_effects=True),
    )(w)


def project_kernel(n_ten, h_ref, w_ref, o_ref, held, s_sem, r_sem, f_ssem, f_rsem):
    me = lax.axis_index("replica")
    mt = lax.axis_index("tensor")
    right, left = lax.rem(mt + 1, n_ten), lax.rem(mt + n_ten - 1, n_ten)
    far = lax.rem(mt + 2, n_ten)
    half = h_ref.shape[0] // 2
    barrier = pltpu.get_barrier_semaphore()
    for t in (left, right):
        pl.semaphore_signal(barrier, inc=1, device_id=(me, t), device_id_type=MESH)
    pl.semaphore_wait(barrier, 2)

    def send(t, side):
        return pltpu.make_async_remote_copy(
            src_ref=h_ref, dst_ref=held.at[mt], send_sem=s_sem.at[side],
            recv_sem=r_sem.at[1 - side], device_id=(me, t), device_id_type=MESH)

    def arrive(t, side):
        return pltpu.make_async_remote_copy(
            src_ref=h_ref, dst_ref=held.at[t], send_sem=s_sem.at[side],
            recv_sem=r_sem.at[side], device_id=(me, t), device_id_type=MESH)

    to_right, to_left = send(right, 0), send(left, 1)
    to_right.start()
    to_left.start()
    o_ref[...] = jnp.dot(h_ref[...], w_ref[mt], preferred_element_type=jnp.float32)
    from_left = arrive(left, 1)
    from_right = arrive(right, 0)
    from_left.wait_recv()
    fwd_right = pltpu.make_async_remote_copy(
        src_ref=held.at[left, pl.ds(0, half)], dst_ref=held.at[left, pl.ds(0, half)],
        send_sem=f_ssem.at[0], recv_sem=f_rsem.at[0], device_id=(me, right), device_id_type=MESH)
    fwd_right.start()
    from_right.wait_recv()
    fwd_left = pltpu.make_async_remote_copy(
        src_ref=held.at[right, pl.ds(half, half)], dst_ref=held.at[right, pl.ds(half, half)],
        send_sem=f_ssem.at[1], recv_sem=f_rsem.at[1], device_id=(me, left), device_id_type=MESH)
    fwd_left.start()
    o_ref[...] += jnp.dot(held[left], w_ref[left], preferred_element_type=jnp.float32)
    o_ref[...] += jnp.dot(held[right], w_ref[right], preferred_element_type=jnp.float32)
    far_first = pltpu.make_async_remote_copy(
        src_ref=held.at[far, pl.ds(0, half)], dst_ref=held.at[far, pl.ds(0, half)],
        send_sem=f_ssem.at[0], recv_sem=f_rsem.at[0], device_id=(me, right), device_id_type=MESH)
    far_second = pltpu.make_async_remote_copy(
        src_ref=held.at[far, pl.ds(half, half)], dst_ref=held.at[far, pl.ds(half, half)],
        send_sem=f_ssem.at[1], recv_sem=f_rsem.at[1], device_id=(me, left), device_id_type=MESH)
    far_first.wait_recv()
    far_second.wait_recv()
    o_ref[...] += jnp.dot(held[far], w_ref[far], preferred_element_type=jnp.float32)
    to_right.wait_send()
    to_left.wait_send()
    fwd_right.wait_send()
    fwd_left.wait_send()


def gather_project(h, w_blocks, n_ten):
    vmem = pl.BlockSpec(memory_space=pltpu.VMEM)
    return pl.pallas_call(
        functools.partial(project_kernel, n_ten),
        out_shape=jax.ShapeDtypeStruct((h.shape[0], w_blocks.shape[2]), jnp.float32),
        in_specs=[vmem, vmem],
        out_specs=vmem,
        scratch_shapes=[
            pltpu.VMEM((n_ten,) + h.shape, h.dtype),
            pltpu.SemaphoreType.DMA((2,)),
            pltpu.SemaphoreType.DMA((2,)),
            pltpu.SemaphoreType.DMA((2,)),
            pltpu.SemaphoreType.DMA((2,)),
        ],
        compiler_params=pltpu.CompilerParams(collective_id=3, has_side_effects=True),
    )(h, w_blocks)


def attn_kernel(scale, q_ref, meta_ref, pk_ref, pv_ref, ck_ref, cv_ref, nk_ref, nv_ref, o_ref):
    q = q_ref[...]
    meta = meta_ref[...]
    dims = (((1,), (1,)), ((), ()))

    def masked(keys, lo, hi):
        s = lax.dot_general(q, keys, dims, preferred_element_type=jnp.float32) * scale
        k = lax.broadcasted_iota(jnp.int32, s.shape, 1)
        return jnp.where((k >= lo) & (k < hi), s, -jnp.inf)

    s_pre = masked(pk_ref[...], meta[:, 0:1], meta[:, 1:2])
    s_old = masked(ck_ref[...], meta[:, 2:3], meta[:, 3:4])
    s_new = masked(nk_ref[...], meta[:, 4:5], meta[:, 5:6])
    top = jnp.maximum(
        jnp.maximum(jnp.max(s_pre, axis=1, keepdims=True), jnp.max(s_old, axis=1, keepdims=True)),
        jnp.max(s_new, axis=1, keepdims=True),
    )
    e_pre = jnp.exp(s_pre - top)
    e_old = jnp.exp(s_old - top)
    e_new = jnp.exp(s_new - top)
    total = (
        jnp.sum(e_pre, axis=1, keepdims=True)
        + jnp.sum(e_old, axis=1, keepdims=True)
        + jnp.sum(e_new, axis=1, keepdims=True)
    )
    w_pre = (e_pre / total).astype(jnp.bfloat16)
    w_old = (e_old / total).astype(jnp.bfloat16)
    w_new = (e_new / total).astype(jnp.bfloat16)
    out = jnp.dot(w_pre, pv_ref[...], preferred_element_type=jnp.float32)
    out = out + jnp.dot(w_old, cv_ref[...], preferred_element_type=jnp.float32)
    out = out + jnp.dot(w_new, nv_ref[...], preferred_element_type=jnp.float32)
    alive = meta[:, 6:7].astype(jnp.float32)
    o_ref[...] = (out * alive).astype(o_ref.dtype)


def attend_kernel_call(q2, meta, pk, pv, ck2, cv2, nk2, nv2, rows_per_block, q_per_row, old_per_row, new_per_row):
    n_q, width = q2.shape
    qb = rows_per_block * q_per_row
    ob = rows_per_block * old_per_row
    nb = rows_per_block * new_per_row
    full = lambda i: (0, 0)
    return pl.pallas_call(
        functools.partial(attn_kernel, 1.0 / math.sqrt(HEAD_DIM)),
        out_shape=jax.ShapeDtypeStruct((n_q, width), jnp.bfloat16),
        grid=(n_q // qb,),
        in_specs=[
            pl.BlockSpec((qb, width), lambda i: (i, 0)),
            pl.BlockSpec((qb, meta.shape[1]), lambda i: (i, 0)),
            pl.BlockSpec(pk.shape, full),
            pl.BlockSpec(pv.shape, full),
            pl.BlockSpec((ob, width), lambda i: (i, 0)),
            pl.BlockSpec((ob, width), lambda i: (i, 0)),
            pl.BlockSpec((nb, width), lambda i: (i, 0)),
            pl.BlockSpec((nb, width), lambda i: (i, 0)),
        ],
        out_specs=pl.BlockSpec((qb, width), lambda i: (i, 0)),
    )(q2, meta, pk, pv, ck2, cv2, nk2, nv2)


def attend_fused(q, nk, nv, slot_keys, slot_values, slot_of_row, slot_len, old_keys, old_values, old_len, alive, rows_per_block=8):
    rows, steps = q.shape[0], q.shape[1]
    groups = q.shape[2] // HEAD_DIM
    n_slots, pre_max = slot_keys.shape[0], slot_keys.shape[1]
    old_max = old_keys.shape[1]
    local = jnp.arange(rows, dtype=jnp.int32) % rows_per_block
    lo_pre = slot_of_row * pre_max
    hi_pre = lo_pre + slot_len[slot_of_row]
    lo_old = local * old_max
    hi_old = lo_old + old_len
    lo_new = local * steps
    step_id = jnp.arange(steps * groups, dtype=jnp.int32) // groups
    per_row = jnp.stack([lo_pre, hi_pre, lo_old, hi_old, lo_new, alive, alive, alive], axis=1)
    meta = jnp.broadcast_to(per_row[:, None, :], (rows, steps * groups, 8))
    hi_new = lo_new[:, None] + step_id[None, :] + 1
    meta = meta.at[:, :, 5].set(hi_new)
    meta = meta.reshape(rows * steps * groups, 8)
    out = attend_kernel_call(
        q.reshape(rows * steps * groups, HEAD_DIM),
        meta,
        slot_keys.reshape(n_slots * pre_max, HEAD_DIM),
        slot_values.reshape(n_slots * pre_max, HEAD_DIM),
        old_keys.reshape(rows * old_max, HEAD_DIM),
        old_values.reshape(rows * old_max, HEAD_DIM),
        nk.reshape(rows * steps, HEAD_DIM),
        nv.reshape(rows * steps, HEAD_DIM),
        rows_per_block, steps * groups, old_max, steps,
    )
    return out.reshape(rows, steps, groups * HEAD_DIM)


def body(
    residual,
    queries,
    new_keys,
    new_values,
    cache_keys,
    cache_values,
    cache_lengths,
    finished,
    partner,
    row_slot,
    fork_table,
    prompt_keys,
    prompt_values,
    prompt_lengths,
    out_proj,
):
    local_rows = queries.shape[0]
    peer_count = lax.axis_size("replica")
    where_am = lax.axis_index("replica")
    first_id = where_am * local_rows
    held_count = prompt_keys.shape[0]

    owners = fork_table // held_count
    chosen = owners == where_am
    offsets = jnp.sum(jnp.where(chosen, fork_table % held_count, 0), axis=1)
    has_block = jnp.any(chosen, axis=1)[:, None, None]
    zero_value = jnp.zeros((), prompt_keys.dtype)
    both = jnp.concatenate([prompt_keys, prompt_values], axis=2)
    out_both = jnp.where(has_block, both[offsets], zero_value)
    got_both = lax.all_to_all(out_both, "replica", split_axis=0, concat_axis=0, tiled=True)
    n_ten = lax.axis_size("tensor")
    proj_blocks = exchange_weights(out_proj, n_ten)
    got_both, proj_blocks = lax.optimization_barrier((got_both, proj_blocks))
    my_owners = owners[where_am]
    slot_both = got_both[my_owners]
    slot_keys = slot_both[..., : prompt_keys.shape[2]]
    slot_values = slot_both[..., prompt_keys.shape[2] :]
    slot_len = prompt_lengths[fork_table[where_am]]

    peer_of = partner // local_rows
    moved_row = peer_of != where_am
    pairing = (peer_of[None, :] == jnp.arange(peer_count, dtype=jnp.int32)[:, None]) & moved_row[
        None, :
    ]
    peer_row = jnp.sum(
        jnp.where(pairing, jnp.arange(local_rows, dtype=jnp.int32)[None, :], 0), axis=1
    )
    has_row = jnp.any(pairing, axis=1)[:, None, None]
    from_peer = jnp.where(moved_row, peer_of, 0)
    keep_mask = moved_row[:, None, None]
    packed = jnp.concatenate([queries, new_keys, new_values], axis=2)
    outgoing = jnp.where(has_row, packed[peer_row], jnp.zeros((), packed.dtype))
    received = lax.all_to_all(outgoing, "replica", split_axis=0, concat_axis=0, tiled=True)
    use_packed = jnp.where(keep_mask, received[from_peer], packed)
    q_width = queries.shape[2]
    kv_width = new_keys.shape[2]
    use_q = use_packed[..., :q_width]
    use_nk = use_packed[..., q_width : q_width + kv_width]
    use_nv = use_packed[..., q_width + kv_width :]

    own_ids = first_id + jnp.arange(local_rows, dtype=jnp.int32)
    slot_of_row = row_slot[own_ids]
    old_len = cache_lengths[own_ids]
    alive = 1 - finished[own_ids]
    cache_side = attend_fused(
        use_q,
        use_nk,
        use_nv,
        slot_keys,
        slot_values,
        slot_of_row,
        slot_len,
        cache_keys,
        cache_values,
        old_len,
        alive,
    )

    back = jnp.where(has_row, cache_side[peer_row], jnp.zeros((), cache_side.dtype))
    returned = lax.all_to_all(back, "replica", split_axis=0, concat_axis=0, tiled=True)
    heads_out = jnp.where(keep_mask, returned[from_peer], cache_side)

    flat_heads = heads_out.reshape(-1, heads_out.shape[2])
    summed = gather_project(flat_heads, proj_blocks, n_ten).reshape(residual.shape)
    return (residual.astype(jnp.float32) + summed).astype(jnp.bfloat16)


def solution(mesh):
    in_specs = (
        P("replica", None, "tensor"),
        P("replica", None, "tensor"),
        P("replica", None, "tensor"),
        P("replica", None, "tensor"),
        P("replica", None, "tensor"),
        P("replica", None, "tensor"),
        P(),
        P(),
        P("replica"),
        P(),
        P(),
        P("replica", None, "tensor"),
        P("replica", None, "tensor"),
        P(),
        P("tensor", None),
    )
    out_specs = P("replica", None, "tensor")
    return jax.shard_map(body, mesh=mesh, in_specs=in_specs, out_specs=out_specs, check_vma=False)
```

```python
import math

import jax
import jax.numpy as jnp
from jax import lax
import functools

from jax.experimental import pallas as pl
from jax.experimental.pallas import tpu as pltpu
from jax.sharding import PartitionSpec as P

HEAD_DIM = 128
MESH = pl.DeviceIdType.MESH


def attend_local(q, nk, nv, slot_keys, slot_values, slot_of_row, slot_len, old_keys, old_values, old_len):
    rows, steps = q.shape[0], q.shape[1]
    groups = q.shape[2] // HEAD_DIM
    n_slots, pre_len_max = slot_keys.shape[0], slot_keys.shape[1]
    qs = q.reshape(rows, steps * groups, HEAD_DIM)
    scale = 1.0 / math.sqrt(HEAD_DIM)
    flat_pk = slot_keys.reshape(n_slots * pre_len_max, HEAD_DIM)
    flat_pv = slot_values.reshape(n_slots * pre_len_max, HEAD_DIM)
    part_pre = (
        jnp.einsum("bqd,kd->bqk", qs, flat_pk, preferred_element_type=jnp.float32) * scale
    )
    part_old = (
        jnp.einsum("bqd,btd->bqt", qs, old_keys, preferred_element_type=jnp.float32) * scale
    )
    part_new = jnp.einsum("bqd,btd->bqt", qs, nk, preferred_element_type=jnp.float32) * scale
    key_slot = jnp.arange(n_slots * pre_len_max, dtype=jnp.int32) // pre_len_max
    key_pos = jnp.arange(n_slots * pre_len_max, dtype=jnp.int32) % pre_len_max
    mask_pre = (key_slot[None, :] == slot_of_row[:, None]) & (
        key_pos[None, :] < slot_len[key_slot][None, :]
    )
    mask_old = jnp.arange(old_keys.shape[1], dtype=jnp.int32)[None, :] < old_len[:, None]
    q_step = jnp.arange(steps * groups, dtype=jnp.int32) // groups
    mask_new = jnp.arange(steps, dtype=jnp.int32)[None, :] <= q_step[:, None]
    part_pre = jnp.where(mask_pre[:, None, :], part_pre, -jnp.inf)
    part_old = jnp.where(mask_old[:, None, :], part_old, -jnp.inf)
    part_new = jnp.where(mask_new[None, :, :], part_new, -jnp.inf)
    scores = jnp.concatenate([part_pre, part_old, part_new], axis=-1)
    row_top = jnp.max(scores, axis=-1, keepdims=True)
    exp_scores = jnp.exp(scores - row_top)
    weights = (exp_scores / jnp.sum(exp_scores, axis=-1, keepdims=True)).astype(jnp.bfloat16)
    n_pre = n_slots * pre_len_max
    n_old = old_keys.shape[1]
    mixed = jnp.einsum(
        "bqk,kd->bqd", weights[..., :n_pre], flat_pv, preferred_element_type=jnp.float32
    )
    mixed = mixed + jnp.einsum(
        "bqt,btd->bqd",
        weights[..., n_pre : n_pre + n_old],
        old_values,
        preferred_element_type=jnp.float32,
    )
    mixed = mixed + jnp.einsum(
        "bqt,btd->bqd", weights[..., n_pre + n_old :], nv, preferred_element_type=jnp.float32
    )
    return mixed.reshape(rows, steps, groups * HEAD_DIM)


def weight_kernel(n_ten, w_ref, w_recv, s_sem, r_sem, l_sem):
    me = lax.axis_index("replica")
    mt = lax.axis_index("tensor")
    width = w_recv.shape[2]
    barrier = pltpu.get_barrier_semaphore()

    def greet(k, carry):
        t = lax.rem(mt + k, n_ten)
        pl.semaphore_signal(barrier, inc=1, device_id=(me, t), device_id_type=MESH)
        return carry

    lax.fori_loop(1, n_ten, greet, 0)
    pl.semaphore_wait(barrier, n_ten - 1)

    def w_cols(t):
        return w_ref.at[:, pl.ds(pl.multiple_of(t * width, width), width)]

    def w_out(t):
        return pltpu.make_async_remote_copy(
            src_ref=w_cols(t), dst_ref=w_recv.at[mt], send_sem=s_sem.at[t],
            recv_sem=r_sem.at[mt], device_id=(me, t), device_id_type=MESH)

    def w_in(t):
        return pltpu.make_async_remote_copy(
            src_ref=w_cols(t), dst_ref=w_recv.at[t], send_sem=s_sem.at[t],
            recv_sem=r_sem.at[t], device_id=(me, t), device_id_type=MESH)

    own = pltpu.make_async_copy(w_cols(mt), w_recv.at[mt], l_sem.at[0])
    own.start()

    def start(k, carry):
        w_out(lax.rem(mt + k, n_ten)).start()
        return carry

    def wait(k, carry):
        t = lax.rem(mt + k, n_ten)
        w_out(t).wait_send()
        w_in(t).wait_recv()
        return carry

    lax.fori_loop(1, n_ten, start, 0)
    lax.fori_loop(1, n_ten, wait, 0)
    own.wait()


def exchange_weights(w, n_ten):
    any_spec = pl.BlockSpec(memory_space=pl.ANY)
    width = w.shape[1] // n_ten
    return pl.pallas_call(
        functools.partial(weight_kernel, n_ten),
        out_shape=jax.ShapeDtypeStruct((n_ten, w.shape[0], width), w.dtype),
        in_specs=[any_spec],
        out_specs=any_spec,
        scratch_shapes=[
            pltpu.SemaphoreType.DMA((n_ten,)),
            pltpu.SemaphoreType.DMA((n_ten,)),
            pltpu.SemaphoreType.DMA((1,)),
        ],
        compiler_params=pltpu.CompilerParams(collective_id=2, has_side_effects=True),
    )(w)


def project_kernel(n_ten, h_ref, w_ref, o_ref, held, s_sem, r_sem, f_ssem, f_rsem):
    me = lax.axis_index("replica")
    mt = lax.axis_index("tensor")
    right, left = lax.rem(mt + 1, n_ten), lax.rem(mt + n_ten - 1, n_ten)
    far = lax.rem(mt + 2, n_ten)
    half = h_ref.shape[0] // 2
    barrier = pltpu.get_barrier_semaphore()
    for t in (left, right):
        pl.semaphore_signal(barrier, inc=1, device_id=(me, t), device_id_type=MESH)
    pl.semaphore_wait(barrier, 2)

    first, second = pl.ds(0, half), pl.ds(half, half)

    def out_copy(t, rows, sem):
        return pltpu.make_async_remote_copy(
            src_ref=h_ref.at[rows], dst_ref=held.at[mt, rows], send_sem=s_sem.at[sem],
            recv_sem=r_sem.at[sem], device_id=(me, t), device_id_type=MESH)

    def in_copy(t, rows, sem):
        return pltpu.make_async_remote_copy(
            src_ref=h_ref.at[rows], dst_ref=held.at[t, rows], send_sem=s_sem.at[sem],
            recv_sem=r_sem.at[sem], device_id=(me, t), device_id_type=MESH)

    sends = (
        out_copy(right, first, 0),
        out_copy(left, second, 2),
        out_copy(right, second, 1),
        out_copy(left, first, 3),
    )
    for c in sends:
        c.start()
    o_ref[...] = jnp.dot(h_ref[...], w_ref[mt], preferred_element_type=jnp.float32)
    in_copy(left, first, 0).wait_recv()
    fwd_right = pltpu.make_async_remote_copy(
        src_ref=held.at[left, first], dst_ref=held.at[left, first],
        send_sem=f_ssem.at[0], recv_sem=f_rsem.at[0], device_id=(me, right), device_id_type=MESH)
    fwd_right.start()
    in_copy(right, second, 2).wait_recv()
    fwd_left = pltpu.make_async_remote_copy(
        src_ref=held.at[right, second], dst_ref=held.at[right, second],
        send_sem=f_ssem.at[1], recv_sem=f_rsem.at[1], device_id=(me, left), device_id_type=MESH)
    fwd_left.start()
    in_copy(left, second, 1).wait_recv()
    in_copy(right, first, 3).wait_recv()
    o_ref[...] += jnp.dot(held[left], w_ref[left], preferred_element_type=jnp.float32)
    o_ref[...] += jnp.dot(held[right], w_ref[right], preferred_element_type=jnp.float32)
    far_first = pltpu.make_async_remote_copy(
        src_ref=held.at[far, pl.ds(0, half)], dst_ref=held.at[far, pl.ds(0, half)],
        send_sem=f_ssem.at[0], recv_sem=f_rsem.at[0], device_id=(me, right), device_id_type=MESH)
    far_second = pltpu.make_async_remote_copy(
        src_ref=held.at[far, pl.ds(half, half)], dst_ref=held.at[far, pl.ds(half, half)],
        send_sem=f_ssem.at[1], recv_sem=f_rsem.at[1], device_id=(me, left), device_id_type=MESH)
    far_first.wait_recv()
    far_second.wait_recv()
    o_ref[...] += jnp.dot(held[far], w_ref[far], preferred_element_type=jnp.float32)
    for c in sends:
        c.wait_send()
    fwd_right.wait_send()
    fwd_left.wait_send()


def gather_project(h, w_blocks, n_ten):
    vmem = pl.BlockSpec(memory_space=pltpu.VMEM)
    return pl.pallas_call(
        functools.partial(project_kernel, n_ten),
        out_shape=jax.ShapeDtypeStruct((h.shape[0], w_blocks.shape[2]), jnp.float32),
        in_specs=[vmem, vmem],
        out_specs=vmem,
        scratch_shapes=[
            pltpu.VMEM((n_ten,) + h.shape, h.dtype),
            pltpu.SemaphoreType.DMA((4,)),
            pltpu.SemaphoreType.DMA((4,)),
            pltpu.SemaphoreType.DMA((2,)),
            pltpu.SemaphoreType.DMA((2,)),
        ],
        compiler_params=pltpu.CompilerParams(collective_id=3, has_side_effects=True),
    )(h, w_blocks)


def attn_kernel(scale, q_ref, meta_ref, pk_ref, pv_ref, ck_ref, cv_ref, nk_ref, nv_ref, o_ref):
    q = q_ref[...]
    meta = meta_ref[...]
    dims = (((1,), (1,)), ((), ()))

    def masked(keys, lo, hi):
        s = lax.dot_general(q, keys, dims, preferred_element_type=jnp.float32) * scale
        k = lax.broadcasted_iota(jnp.int32, s.shape, 1)
        return jnp.where((k >= lo) & (k < hi), s, -jnp.inf)

    s_pre = masked(pk_ref[...], meta[:, 0:1], meta[:, 1:2])
    s_old = masked(ck_ref[...], meta[:, 2:3], meta[:, 3:4])
    s_new = masked(nk_ref[...], meta[:, 4:5], meta[:, 5:6])
    top = jnp.maximum(
        jnp.maximum(jnp.max(s_pre, axis=1, keepdims=True), jnp.max(s_old, axis=1, keepdims=True)),
        jnp.max(s_new, axis=1, keepdims=True),
    )
    e_pre = jnp.exp(s_pre - top)
    e_old = jnp.exp(s_old - top)
    e_new = jnp.exp(s_new - top)
    total = (
        jnp.sum(e_pre, axis=1, keepdims=True)
        + jnp.sum(e_old, axis=1, keepdims=True)
        + jnp.sum(e_new, axis=1, keepdims=True)
    )
    w_pre = (e_pre / total).astype(jnp.bfloat16)
    w_old = (e_old / total).astype(jnp.bfloat16)
    w_new = (e_new / total).astype(jnp.bfloat16)
    out = jnp.dot(w_pre, pv_ref[...], preferred_element_type=jnp.float32)
    out = out + jnp.dot(w_old, cv_ref[...], preferred_element_type=jnp.float32)
    out = out + jnp.dot(w_new, nv_ref[...], preferred_element_type=jnp.float32)
    alive = meta[:, 6:7].astype(jnp.float32)
    o_ref[...] = (out * alive).astype(o_ref.dtype)


def attend_kernel_call(q2, meta, pk, pv, ck2, cv2, nk2, nv2, rows_per_block, q_per_row, old_per_row, new_per_row):
    n_q, width = q2.shape
    qb = rows_per_block * q_per_row
    ob = rows_per_block * old_per_row
    nb = rows_per_block * new_per_row
    full = lambda i: (0, 0)
    return pl.pallas_call(
        functools.partial(attn_kernel, 1.0 / math.sqrt(HEAD_DIM)),
        out_shape=jax.ShapeDtypeStruct((n_q, width), jnp.bfloat16),
        grid=(n_q // qb,),
        in_specs=[
            pl.BlockSpec((qb, width), lambda i: (i, 0)),
            pl.BlockSpec((qb, meta.shape[1]), lambda i: (i, 0)),
            pl.BlockSpec(pk.shape, full),
            pl.BlockSpec(pv.shape, full),
            pl.BlockSpec((ob, width), lambda i: (i, 0)),
            pl.BlockSpec((ob, width), lambda i: (i, 0)),
            pl.BlockSpec((nb, width), lambda i: (i, 0)),
            pl.BlockSpec((nb, width), lambda i: (i, 0)),
        ],
        out_specs=pl.BlockSpec((qb, width), lambda i: (i, 0)),
    )(q2, meta, pk, pv, ck2, cv2, nk2, nv2)


def attend_fused(q, nk, nv, slot_keys, slot_values, slot_of_row, slot_len, old_keys, old_values, old_len, alive, rows_per_block=8):
    rows, steps = q.shape[0], q.shape[1]
    groups = q.shape[2] // HEAD_DIM
    n_slots, pre_max = slot_keys.shape[0], slot_keys.shape[1]
    old_max = old_keys.shape[1]
    local = jnp.arange(rows, dtype=jnp.int32) % rows_per_block
    lo_pre = slot_of_row * pre_max
    hi_pre = lo_pre + slot_len[slot_of_row]
    lo_old = local * old_max
    hi_old = lo_old + old_len
    lo_new = local * steps
    step_id = jnp.arange(steps * groups, dtype=jnp.int32) // groups
    per_row = jnp.stack([lo_pre, hi_pre, lo_old, hi_old, lo_new, alive, alive, alive], axis=1)
    meta = jnp.broadcast_to(per_row[:, None, :], (rows, steps * groups, 8))
    hi_new = lo_new[:, None] + step_id[None, :] + 1
    meta = meta.at[:, :, 5].set(hi_new)
    meta = meta.reshape(rows * steps * groups, 8)
    out = attend_kernel_call(
        q.reshape(rows * steps * groups, HEAD_DIM),
        meta,
        slot_keys.reshape(n_slots * pre_max, HEAD_DIM),
        slot_values.reshape(n_slots * pre_max, HEAD_DIM),
        old_keys.reshape(rows * old_max, HEAD_DIM),
        old_values.reshape(rows * old_max, HEAD_DIM),
        nk.reshape(rows * steps, HEAD_DIM),
        nv.reshape(rows * steps, HEAD_DIM),
        rows_per_block, steps * groups, old_max, steps,
    )
    return out.reshape(rows, steps, groups * HEAD_DIM)


def body(
    residual,
    queries,
    new_keys,
    new_values,
    cache_keys,
    cache_values,
    cache_lengths,
    finished,
    partner,
    row_slot,
    fork_table,
    prompt_keys,
    prompt_values,
    prompt_lengths,
    out_proj,
):
    local_rows = queries.shape[0]
    peer_count = lax.axis_size("replica")
    where_am = lax.axis_index("replica")
    first_id = where_am * local_rows
    held_count = prompt_keys.shape[0]

    owners = fork_table // held_count
    chosen = owners == where_am
    offsets = jnp.sum(jnp.where(chosen, fork_table % held_count, 0), axis=1)
    has_block = jnp.any(chosen, axis=1)[:, None, None]
    zero_value = jnp.zeros((), prompt_keys.dtype)
    both = jnp.concatenate([prompt_keys, prompt_values], axis=2)
    out_both = jnp.where(has_block, both[offsets], zero_value)
    got_both = lax.all_to_all(out_both, "replica", split_axis=0, concat_axis=0, tiled=True)
    n_ten = lax.axis_size("tensor")
    proj_blocks = exchange_weights(out_proj, n_ten)
    got_both, proj_blocks = lax.optimization_barrier((got_both, proj_blocks))
    my_owners = owners[where_am]
    slot_both = got_both[my_owners]
    slot_keys = slot_both[..., : prompt_keys.shape[2]]
    slot_values = slot_both[..., prompt_keys.shape[2] :]
    slot_len = prompt_lengths[fork_table[where_am]]

    peer_of = partner // local_rows
    moved_row = peer_of != where_am
    pairing = (peer_of[None, :] == jnp.arange(peer_count, dtype=jnp.int32)[:, None]) & moved_row[
        None, :
    ]
    peer_row = jnp.sum(
        jnp.where(pairing, jnp.arange(local_rows, dtype=jnp.int32)[None, :], 0), axis=1
    )
    has_row = jnp.any(pairing, axis=1)[:, None, None]
    from_peer = jnp.where(moved_row, peer_of, 0)
    keep_mask = moved_row[:, None, None]
    packed = jnp.concatenate([queries, new_keys, new_values], axis=2)
    outgoing = jnp.where(has_row, packed[peer_row], jnp.zeros((), packed.dtype))
    received = lax.all_to_all(outgoing, "replica", split_axis=0, concat_axis=0, tiled=True)
    use_packed = jnp.where(keep_mask, received[from_peer], packed)
    q_width = queries.shape[2]
    kv_width = new_keys.shape[2]
    use_q = use_packed[..., :q_width]
    use_nk = use_packed[..., q_width : q_width + kv_width]
    use_nv = use_packed[..., q_width + kv_width :]

    own_ids = first_id + jnp.arange(local_rows, dtype=jnp.int32)
    slot_of_row = row_slot[own_ids]
    old_len = cache_lengths[own_ids]
    alive = 1 - finished[own_ids]
    cache_side = attend_fused(
        use_q,
        use_nk,
        use_nv,
        slot_keys,
        slot_values,
        slot_of_row,
        slot_len,
        cache_keys,
        cache_values,
        old_len,
        alive,
    )

    back = jnp.where(has_row, cache_side[peer_row], jnp.zeros((), cache_side.dtype))
    returned = lax.all_to_all(back, "replica", split_axis=0, concat_axis=0, tiled=True)
    heads_out = jnp.where(keep_mask, returned[from_peer], cache_side)

    flat_heads = heads_out.reshape(-1, heads_out.shape[2])
    summed = gather_project(flat_heads, proj_blocks, n_ten).reshape(residual.shape)
    return (residual.astype(jnp.float32) + summed).astype(jnp.bfloat16)


def solution(mesh):
    in_specs = (
        P("replica", None, "tensor"),
        P("replica", None, "tensor"),
        P("replica", None, "tensor"),
        P("replica", None, "tensor"),
        P("replica", None, "tensor"),
        P("replica", None, "tensor"),
        P(),
        P(),
        P("replica"),
        P(),
        P(),
        P("replica", None, "tensor"),
        P("replica", None, "tensor"),
        P(),
        P("tensor", None),
    )
    out_specs = P("replica", None, "tensor")
    return jax.shard_map(body, mesh=mesh, in_specs=in_specs, out_specs=out_specs, check_vma=False)
```

```python
import math

import jax
import jax.numpy as jnp
from jax import lax
import functools

from jax.experimental import pallas as pl
from jax.experimental.pallas import tpu as pltpu
from jax.sharding import PartitionSpec as P

HEAD_DIM = 128
MESH = pl.DeviceIdType.MESH


def attend_local(q, nk, nv, slot_keys, slot_values, slot_of_row, slot_len, old_keys, old_values, old_len):
    rows, steps = q.shape[0], q.shape[1]
    groups = q.shape[2] // HEAD_DIM
    n_slots, pre_len_max = slot_keys.shape[0], slot_keys.shape[1]
    qs = q.reshape(rows, steps * groups, HEAD_DIM)
    scale = 1.0 / math.sqrt(HEAD_DIM)
    flat_pk = slot_keys.reshape(n_slots * pre_len_max, HEAD_DIM)
    flat_pv = slot_values.reshape(n_slots * pre_len_max, HEAD_DIM)
    part_pre = (
        jnp.einsum("bqd,kd->bqk", qs, flat_pk, preferred_element_type=jnp.float32) * scale
    )
    part_old = (
        jnp.einsum("bqd,btd->bqt", qs, old_keys, preferred_element_type=jnp.float32) * scale
    )
    part_new = jnp.einsum("bqd,btd->bqt", qs, nk, preferred_element_type=jnp.float32) * scale
    key_slot = jnp.arange(n_slots * pre_len_max, dtype=jnp.int32) // pre_len_max
    key_pos = jnp.arange(n_slots * pre_len_max, dtype=jnp.int32) % pre_len_max
    mask_pre = (key_slot[None, :] == slot_of_row[:, None]) & (
        key_pos[None, :] < slot_len[key_slot][None, :]
    )
    mask_old = jnp.arange(old_keys.shape[1], dtype=jnp.int32)[None, :] < old_len[:, None]
    q_step = jnp.arange(steps * groups, dtype=jnp.int32) // groups
    mask_new = jnp.arange(steps, dtype=jnp.int32)[None, :] <= q_step[:, None]
    part_pre = jnp.where(mask_pre[:, None, :], part_pre, -jnp.inf)
    part_old = jnp.where(mask_old[:, None, :], part_old, -jnp.inf)
    part_new = jnp.where(mask_new[None, :, :], part_new, -jnp.inf)
    scores = jnp.concatenate([part_pre, part_old, part_new], axis=-1)
    row_top = jnp.max(scores, axis=-1, keepdims=True)
    exp_scores = jnp.exp(scores - row_top)
    weights = (exp_scores / jnp.sum(exp_scores, axis=-1, keepdims=True)).astype(jnp.bfloat16)
    n_pre = n_slots * pre_len_max
    n_old = old_keys.shape[1]
    mixed = jnp.einsum(
        "bqk,kd->bqd", weights[..., :n_pre], flat_pv, preferred_element_type=jnp.float32
    )
    mixed = mixed + jnp.einsum(
        "bqt,btd->bqd",
        weights[..., n_pre : n_pre + n_old],
        old_values,
        preferred_element_type=jnp.float32,
    )
    mixed = mixed + jnp.einsum(
        "bqt,btd->bqd", weights[..., n_pre + n_old :], nv, preferred_element_type=jnp.float32
    )
    return mixed.reshape(rows, steps, groups * HEAD_DIM)


def weight_kernel(n_ten, w_ref, w_recv, s_sem, r_sem, l_sem):
    me = lax.axis_index("replica")
    mt = lax.axis_index("tensor")
    width = w_recv.shape[2]
    barrier = pltpu.get_barrier_semaphore()

    def greet(k, carry):
        t = lax.rem(mt + k, n_ten)
        pl.semaphore_signal(barrier, inc=1, device_id=(me, t), device_id_type=MESH)
        return carry

    lax.fori_loop(1, n_ten, greet, 0)
    pl.semaphore_wait(barrier, n_ten - 1)

    def w_cols(t):
        return w_ref.at[:, pl.ds(pl.multiple_of(t * width, width), width)]

    def w_out(t):
        return pltpu.make_async_remote_copy(
            src_ref=w_cols(t), dst_ref=w_recv.at[mt], send_sem=s_sem.at[t],
            recv_sem=r_sem.at[mt], device_id=(me, t), device_id_type=MESH)

    def w_in(t):
        return pltpu.make_async_remote_copy(
            src_ref=w_cols(t), dst_ref=w_recv.at[t], send_sem=s_sem.at[t],
            recv_sem=r_sem.at[t], device_id=(me, t), device_id_type=MESH)

    own = pltpu.make_async_copy(w_cols(mt), w_recv.at[mt], l_sem.at[0])
    own.start()

    def start(k, carry):
        w_out(lax.rem(mt + k, n_ten)).start()
        return carry

    def wait(k, carry):
        t = lax.rem(mt + k, n_ten)
        w_out(t).wait_send()
        w_in(t).wait_recv()
        return carry

    lax.fori_loop(1, n_ten, start, 0)
    lax.fori_loop(1, n_ten, wait, 0)
    own.wait()


def exchange_weights(w, n_ten):
    any_spec = pl.BlockSpec(memory_space=pl.ANY)
    width = w.shape[1] // n_ten
    return pl.pallas_call(
        functools.partial(weight_kernel, n_ten),
        out_shape=jax.ShapeDtypeStruct((n_ten, w.shape[0], width), w.dtype),
        in_specs=[any_spec],
        out_specs=any_spec,
        scratch_shapes=[
            pltpu.SemaphoreType.DMA((n_ten,)),
            pltpu.SemaphoreType.DMA((n_ten,)),
            pltpu.SemaphoreType.DMA((1,)),
        ],
        compiler_params=pltpu.CompilerParams(collective_id=2, has_side_effects=True),
    )(w)


def project_kernel(n_ten, h_ref, w_ref, o_ref, held, s_sem, r_sem, f_ssem, f_rsem):
    me = lax.axis_index("replica")
    mt = lax.axis_index("tensor")
    right, left = lax.rem(mt + 1, n_ten), lax.rem(mt + n_ten - 1, n_ten)
    far = lax.rem(mt + 2, n_ten)
    half = h_ref.shape[0] // 2
    barrier = pltpu.get_barrier_semaphore()
    for t in (left, right):
        pl.semaphore_signal(barrier, inc=1, device_id=(me, t), device_id_type=MESH)
    pl.semaphore_wait(barrier, 2)

    first, second = pl.ds(0, half), pl.ds(half, half)

    def out_copy(t, rows, sem):
        return pltpu.make_async_remote_copy(
            src_ref=h_ref.at[rows], dst_ref=held.at[mt, rows], send_sem=s_sem.at[sem],
            recv_sem=r_sem.at[sem], device_id=(me, t), device_id_type=MESH)

    def in_copy(t, rows, sem):
        return pltpu.make_async_remote_copy(
            src_ref=h_ref.at[rows], dst_ref=held.at[t, rows], send_sem=s_sem.at[sem],
            recv_sem=r_sem.at[sem], device_id=(me, t), device_id_type=MESH)

    sends = (
        out_copy(right, first, 0),
        out_copy(left, second, 2),
        out_copy(right, second, 1),
        out_copy(left, first, 3),
    )
    for c in sends:
        c.start()
    o_ref[...] = jnp.dot(h_ref[...], w_ref[mt], preferred_element_type=jnp.float32)
    in_copy(left, first, 0).wait_recv()
    fwd_right = pltpu.make_async_remote_copy(
        src_ref=held.at[left, first], dst_ref=held.at[left, first],
        send_sem=f_ssem.at[0], recv_sem=f_rsem.at[0], device_id=(me, right), device_id_type=MESH)
    fwd_right.start()
    in_copy(right, second, 2).wait_recv()
    fwd_left = pltpu.make_async_remote_copy(
        src_ref=held.at[right, second], dst_ref=held.at[right, second],
        send_sem=f_ssem.at[1], recv_sem=f_rsem.at[1], device_id=(me, left), device_id_type=MESH)
    fwd_left.start()
    in_copy(left, second, 1).wait_recv()
    o_ref[...] += jnp.dot(held[left], w_ref[left], preferred_element_type=jnp.float32)
    in_copy(right, first, 3).wait_recv()
    o_ref[...] += jnp.dot(held[right], w_ref[right], preferred_element_type=jnp.float32)
    far_first = pltpu.make_async_remote_copy(
        src_ref=held.at[far, pl.ds(0, half)], dst_ref=held.at[far, pl.ds(0, half)],
        send_sem=f_ssem.at[0], recv_sem=f_rsem.at[0], device_id=(me, right), device_id_type=MESH)
    far_second = pltpu.make_async_remote_copy(
        src_ref=held.at[far, pl.ds(half, half)], dst_ref=held.at[far, pl.ds(half, half)],
        send_sem=f_ssem.at[1], recv_sem=f_rsem.at[1], device_id=(me, left), device_id_type=MESH)
    far_first.wait_recv()
    o_ref[first] += jnp.dot(held[far, first], w_ref[far], preferred_element_type=jnp.float32)
    far_second.wait_recv()
    o_ref[second] += jnp.dot(held[far, second], w_ref[far], preferred_element_type=jnp.float32)
    for c in sends:
        c.wait_send()
    fwd_right.wait_send()
    fwd_left.wait_send()


def gather_project(h, w_blocks, n_ten):
    vmem = pl.BlockSpec(memory_space=pltpu.VMEM)
    return pl.pallas_call(
        functools.partial(project_kernel, n_ten),
        out_shape=jax.ShapeDtypeStruct((h.shape[0], w_blocks.shape[2]), jnp.float32),
        in_specs=[vmem, vmem],
        out_specs=vmem,
        scratch_shapes=[
            pltpu.VMEM((n_ten,) + h.shape, h.dtype),
            pltpu.SemaphoreType.DMA((4,)),
            pltpu.SemaphoreType.DMA((4,)),
            pltpu.SemaphoreType.DMA((2,)),
            pltpu.SemaphoreType.DMA((2,)),
        ],
        compiler_params=pltpu.CompilerParams(collective_id=3, has_side_effects=True),
    )(h, w_blocks)


def attn_kernel(scale, q_ref, meta_ref, pk_ref, pv_ref, ck_ref, cv_ref, nk_ref, nv_ref, o_ref):
    q = q_ref[...]
    meta = meta_ref[...]
    dims = (((1,), (1,)), ((), ()))

    def masked(keys, lo, hi):
        s = lax.dot_general(q, keys, dims, preferred_element_type=jnp.float32) * scale
        k = lax.broadcasted_iota(jnp.int32, s.shape, 1)
        return jnp.where((k >= lo) & (k < hi), s, -jnp.inf)

    s_pre = masked(pk_ref[...], meta[:, 0:1], meta[:, 1:2])
    s_old = masked(ck_ref[...], meta[:, 2:3], meta[:, 3:4])
    s_new = masked(nk_ref[...], meta[:, 4:5], meta[:, 5:6])
    top = jnp.maximum(
        jnp.maximum(jnp.max(s_pre, axis=1, keepdims=True), jnp.max(s_old, axis=1, keepdims=True)),
        jnp.max(s_new, axis=1, keepdims=True),
    )
    e_pre = jnp.exp(s_pre - top)
    e_old = jnp.exp(s_old - top)
    e_new = jnp.exp(s_new - top)
    total = (
        jnp.sum(e_pre, axis=1, keepdims=True)
        + jnp.sum(e_old, axis=1, keepdims=True)
        + jnp.sum(e_new, axis=1, keepdims=True)
    )
    w_pre = (e_pre / total).astype(jnp.bfloat16)
    w_old = (e_old / total).astype(jnp.bfloat16)
    w_new = (e_new / total).astype(jnp.bfloat16)
    out = jnp.dot(w_pre, pv_ref[...], preferred_element_type=jnp.float32)
    out = out + jnp.dot(w_old, cv_ref[...], preferred_element_type=jnp.float32)
    out = out + jnp.dot(w_new, nv_ref[...], preferred_element_type=jnp.float32)
    alive = meta[:, 6:7].astype(jnp.float32)
    o_ref[...] = (out * alive).astype(o_ref.dtype)


def attend_kernel_call(q2, meta, pk, pv, ck2, cv2, nk2, nv2, rows_per_block, q_per_row, old_per_row, new_per_row):
    n_q, width = q2.shape
    qb = rows_per_block * q_per_row
    ob = rows_per_block * old_per_row
    nb = rows_per_block * new_per_row
    full = lambda i: (0, 0)
    return pl.pallas_call(
        functools.partial(attn_kernel, 1.0 / math.sqrt(HEAD_DIM)),
        out_shape=jax.ShapeDtypeStruct((n_q, width), jnp.bfloat16),
        grid=(n_q // qb,),
        in_specs=[
            pl.BlockSpec((qb, width), lambda i: (i, 0)),
            pl.BlockSpec((qb, meta.shape[1]), lambda i: (i, 0)),
            pl.BlockSpec(pk.shape, full),
            pl.BlockSpec(pv.shape, full),
            pl.BlockSpec((ob, width), lambda i: (i, 0)),
            pl.BlockSpec((ob, width), lambda i: (i, 0)),
            pl.BlockSpec((nb, width), lambda i: (i, 0)),
            pl.BlockSpec((nb, width), lambda i: (i, 0)),
        ],
        out_specs=pl.BlockSpec((qb, width), lambda i: (i, 0)),
    )(q2, meta, pk, pv, ck2, cv2, nk2, nv2)


def attend_fused(q, nk, nv, slot_keys, slot_values, slot_of_row, slot_len, old_keys, old_values, old_len, alive, rows_per_block=8):
    rows, steps = q.shape[0], q.shape[1]
    groups = q.shape[2] // HEAD_DIM
    n_slots, pre_max = slot_keys.shape[0], slot_keys.shape[1]
    old_max = old_keys.shape[1]
    local = jnp.arange(rows, dtype=jnp.int32) % rows_per_block
    lo_pre = slot_of_row * pre_max
    hi_pre = lo_pre + slot_len[slot_of_row]
    lo_old = local * old_max
    hi_old = lo_old + old_len
    lo_new = local * steps
    step_id = jnp.arange(steps * groups, dtype=jnp.int32) // groups
    per_row = jnp.stack([lo_pre, hi_pre, lo_old, hi_old, lo_new, alive, alive, alive], axis=1)
    meta = jnp.broadcast_to(per_row[:, None, :], (rows, steps * groups, 8))
    hi_new = lo_new[:, None] + step_id[None, :] + 1
    meta = meta.at[:, :, 5].set(hi_new)
    meta = meta.reshape(rows * steps * groups, 8)
    out = attend_kernel_call(
        q.reshape(rows * steps * groups, HEAD_DIM),
        meta,
        slot_keys.reshape(n_slots * pre_max, HEAD_DIM),
        slot_values.reshape(n_slots * pre_max, HEAD_DIM),
        old_keys.reshape(rows * old_max, HEAD_DIM),
        old_values.reshape(rows * old_max, HEAD_DIM),
        nk.reshape(rows * steps, HEAD_DIM),
        nv.reshape(rows * steps, HEAD_DIM),
        rows_per_block, steps * groups, old_max, steps,
    )
    return out.reshape(rows, steps, groups * HEAD_DIM)


def body(
    residual,
    queries,
    new_keys,
    new_values,
    cache_keys,
    cache_values,
    cache_lengths,
    finished,
    partner,
    row_slot,
    fork_table,
    prompt_keys,
    prompt_values,
    prompt_lengths,
    out_proj,
):
    local_rows = queries.shape[0]
    peer_count = lax.axis_size("replica")
    where_am = lax.axis_index("replica")
    first_id = where_am * local_rows
    held_count = prompt_keys.shape[0]

    owners = fork_table // held_count
    chosen = owners == where_am
    offsets = jnp.sum(jnp.where(chosen, fork_table % held_count, 0), axis=1)
    has_block = jnp.any(chosen, axis=1)[:, None, None]
    zero_value = jnp.zeros((), prompt_keys.dtype)
    both = jnp.concatenate([prompt_keys, prompt_values], axis=2)
    out_both = jnp.where(has_block, both[offsets], zero_value)
    got_both = lax.all_to_all(out_both, "replica", split_axis=0, concat_axis=0, tiled=True)
    n_ten = lax.axis_size("tensor")
    proj_blocks = exchange_weights(out_proj, n_ten)
    got_both, proj_blocks = lax.optimization_barrier((got_both, proj_blocks))
    my_owners = owners[where_am]
    slot_both = got_both[my_owners]
    slot_keys = slot_both[..., : prompt_keys.shape[2]]
    slot_values = slot_both[..., prompt_keys.shape[2] :]
    slot_len = prompt_lengths[fork_table[where_am]]

    peer_of = partner // local_rows
    moved_row = peer_of != where_am
    pairing = (peer_of[None, :] == jnp.arange(peer_count, dtype=jnp.int32)[:, None]) & moved_row[
        None, :
    ]
    peer_row = jnp.sum(
        jnp.where(pairing, jnp.arange(local_rows, dtype=jnp.int32)[None, :], 0), axis=1
    )
    has_row = jnp.any(pairing, axis=1)[:, None, None]
    from_peer = jnp.where(moved_row, peer_of, 0)
    keep_mask = moved_row[:, None, None]
    packed = jnp.concatenate([queries, new_keys, new_values], axis=2)
    outgoing = jnp.where(has_row, packed[peer_row], jnp.zeros((), packed.dtype))
    received = lax.all_to_all(outgoing, "replica", split_axis=0, concat_axis=0, tiled=True)
    use_packed = jnp.where(keep_mask, received[from_peer], packed)
    q_width = queries.shape[2]
    kv_width = new_keys.shape[2]
    use_q = use_packed[..., :q_width]
    use_nk = use_packed[..., q_width : q_width + kv_width]
    use_nv = use_packed[..., q_width + kv_width :]

    own_ids = first_id + jnp.arange(local_rows, dtype=jnp.int32)
    slot_of_row = row_slot[own_ids]
    old_len = cache_lengths[own_ids]
    alive = 1 - finished[own_ids]
    cache_side = attend_fused(
        use_q,
        use_nk,
        use_nv,
        slot_keys,
        slot_values,
        slot_of_row,
        slot_len,
        cache_keys,
        cache_values,
        old_len,
        alive,
    )

    back = jnp.where(has_row, cache_side[peer_row], jnp.zeros((), cache_side.dtype))
    returned = lax.all_to_all(back, "replica", split_axis=0, concat_axis=0, tiled=True)
    heads_out = jnp.where(keep_mask, returned[from_peer], cache_side)

    flat_heads = heads_out.reshape(-1, heads_out.shape[2])
    summed = gather_project(flat_heads, proj_blocks, n_ten).reshape(residual.shape)
    return (residual.astype(jnp.float32) + summed).astype(jnp.bfloat16)


def solution(mesh):
    in_specs = (
        P("replica", None, "tensor"),
        P("replica", None, "tensor"),
        P("replica", None, "tensor"),
        P("replica", None, "tensor"),
        P("replica", None, "tensor"),
        P("replica", None, "tensor"),
        P(),
        P(),
        P("replica"),
        P(),
        P(),
        P("replica", None, "tensor"),
        P("replica", None, "tensor"),
        P(),
        P("tensor", None),
    )
    out_specs = P("replica", None, "tensor")
    return jax.shard_map(body, mesh=mesh, in_specs=in_specs, out_specs=out_specs, check_vma=False)
```

```python
import math

import jax
import jax.numpy as jnp
from jax import lax
import functools

from jax.experimental import pallas as pl
from jax.experimental.pallas import tpu as pltpu
from jax.sharding import PartitionSpec as P

HEAD_DIM = 128
MESH = pl.DeviceIdType.MESH


def attend_local(q, nk, nv, slot_keys, slot_values, slot_of_row, slot_len, old_keys, old_values, old_len):
    rows, steps = q.shape[0], q.shape[1]
    groups = q.shape[2] // HEAD_DIM
    n_slots, pre_len_max = slot_keys.shape[0], slot_keys.shape[1]
    qs = q.reshape(rows, steps * groups, HEAD_DIM)
    scale = 1.0 / math.sqrt(HEAD_DIM)
    flat_pk = slot_keys.reshape(n_slots * pre_len_max, HEAD_DIM)
    flat_pv = slot_values.reshape(n_slots * pre_len_max, HEAD_DIM)
    part_pre = (
        jnp.einsum("bqd,kd->bqk", qs, flat_pk, preferred_element_type=jnp.float32) * scale
    )
    part_old = (
        jnp.einsum("bqd,btd->bqt", qs, old_keys, preferred_element_type=jnp.float32) * scale
    )
    part_new = jnp.einsum("bqd,btd->bqt", qs, nk, preferred_element_type=jnp.float32) * scale
    key_slot = jnp.arange(n_slots * pre_len_max, dtype=jnp.int32) // pre_len_max
    key_pos = jnp.arange(n_slots * pre_len_max, dtype=jnp.int32) % pre_len_max
    mask_pre = (key_slot[None, :] == slot_of_row[:, None]) & (
        key_pos[None, :] < slot_len[key_slot][None, :]
    )
    mask_old = jnp.arange(old_keys.shape[1], dtype=jnp.int32)[None, :] < old_len[:, None]
    q_step = jnp.arange(steps * groups, dtype=jnp.int32) // groups
    mask_new = jnp.arange(steps, dtype=jnp.int32)[None, :] <= q_step[:, None]
    part_pre = jnp.where(mask_pre[:, None, :], part_pre, -jnp.inf)
    part_old = jnp.where(mask_old[:, None, :], part_old, -jnp.inf)
    part_new = jnp.where(mask_new[None, :, :], part_new, -jnp.inf)
    scores = jnp.concatenate([part_pre, part_old, part_new], axis=-1)
    row_top = jnp.max(scores, axis=-1, keepdims=True)
    exp_scores = jnp.exp(scores - row_top)
    weights = (exp_scores / jnp.sum(exp_scores, axis=-1, keepdims=True)).astype(jnp.bfloat16)
    n_pre = n_slots * pre_len_max
    n_old = old_keys.shape[1]
    mixed = jnp.einsum(
        "bqk,kd->bqd", weights[..., :n_pre], flat_pv, preferred_element_type=jnp.float32
    )
    mixed = mixed + jnp.einsum(
        "bqt,btd->bqd",
        weights[..., n_pre : n_pre + n_old],
        old_values,
        preferred_element_type=jnp.float32,
    )
    mixed = mixed + jnp.einsum(
        "bqt,btd->bqd", weights[..., n_pre + n_old :], nv, preferred_element_type=jnp.float32
    )
    return mixed.reshape(rows, steps, groups * HEAD_DIM)


def weight_kernel(n_ten, w_ref, w_recv, s_sem, r_sem, l_sem):
    me = lax.axis_index("replica")
    mt = lax.axis_index("tensor")
    width = w_recv.shape[2]
    barrier = pltpu.get_barrier_semaphore()

    def greet(k, carry):
        t = lax.rem(mt + k, n_ten)
        pl.semaphore_signal(barrier, inc=1, device_id=(me, t), device_id_type=MESH)
        return carry

    lax.fori_loop(1, n_ten, greet, 0)
    pl.semaphore_wait(barrier, n_ten - 1)

    def w_cols(t):
        return w_ref.at[:, pl.ds(pl.multiple_of(t * width, width), width)]

    def w_out(t):
        return pltpu.make_async_remote_copy(
            src_ref=w_cols(t), dst_ref=w_recv.at[mt], send_sem=s_sem.at[t],
            recv_sem=r_sem.at[mt], device_id=(me, t), device_id_type=MESH)

    def w_in(t):
        return pltpu.make_async_remote_copy(
            src_ref=w_cols(t), dst_ref=w_recv.at[t], send_sem=s_sem.at[t],
            recv_sem=r_sem.at[t], device_id=(me, t), device_id_type=MESH)

    own = pltpu.make_async_copy(w_cols(mt), w_recv.at[mt], l_sem.at[0])
    own.start()

    def start(k, carry):
        w_out(lax.rem(mt + k, n_ten)).start()
        return carry

    def wait(k, carry):
        t = lax.rem(mt + k, n_ten)
        w_out(t).wait_send()
        w_in(t).wait_recv()
        return carry

    lax.fori_loop(1, n_ten, start, 0)
    lax.fori_loop(1, n_ten, wait, 0)
    own.wait()


def exchange_weights(w, n_ten):
    any_spec = pl.BlockSpec(memory_space=pl.ANY)
    width = w.shape[1] // n_ten
    return pl.pallas_call(
        functools.partial(weight_kernel, n_ten),
        out_shape=jax.ShapeDtypeStruct((n_ten, w.shape[0], width), w.dtype),
        in_specs=[any_spec],
        out_specs=any_spec,
        scratch_shapes=[
            pltpu.SemaphoreType.DMA((n_ten,)),
            pltpu.SemaphoreType.DMA((n_ten,)),
            pltpu.SemaphoreType.DMA((1,)),
        ],
        compiler_params=pltpu.CompilerParams(collective_id=2, has_side_effects=True),
    )(w)


def project_kernel(n_ten, h_ref, w_ref, res_ref, out_ref, o_ref, held, s_sem, r_sem, f_ssem, f_rsem):
    me = lax.axis_index("replica")
    mt = lax.axis_index("tensor")
    right, left = lax.rem(mt + 1, n_ten), lax.rem(mt + n_ten - 1, n_ten)
    far = lax.rem(mt + 2, n_ten)
    half = h_ref.shape[0] // 2
    barrier = pltpu.get_barrier_semaphore()
    for t in (left, right):
        pl.semaphore_signal(barrier, inc=1, device_id=(me, t), device_id_type=MESH)
    pl.semaphore_wait(barrier, 2)

    first, second = pl.ds(0, half), pl.ds(half, half)

    def out_copy(t, rows, sem):
        return pltpu.make_async_remote_copy(
            src_ref=h_ref.at[rows], dst_ref=held.at[mt, rows], send_sem=s_sem.at[sem],
            recv_sem=r_sem.at[sem], device_id=(me, t), device_id_type=MESH)

    def in_copy(t, rows, sem):
        return pltpu.make_async_remote_copy(
            src_ref=h_ref.at[rows], dst_ref=held.at[t, rows], send_sem=s_sem.at[sem],
            recv_sem=r_sem.at[sem], device_id=(me, t), device_id_type=MESH)

    sends = (
        out_copy(right, first, 0),
        out_copy(left, second, 2),
        out_copy(right, second, 1),
        out_copy(left, first, 3),
    )
    for c in sends:
        c.start()
    o_ref[...] = jnp.dot(h_ref[...], w_ref[mt], preferred_element_type=jnp.float32)
    in_copy(left, first, 0).wait_recv()
    fwd_right = pltpu.make_async_remote_copy(
        src_ref=held.at[left, first], dst_ref=held.at[left, first],
        send_sem=f_ssem.at[0], recv_sem=f_rsem.at[0], device_id=(me, right), device_id_type=MESH)
    fwd_right.start()
    in_copy(right, second, 2).wait_recv()
    fwd_left = pltpu.make_async_remote_copy(
        src_ref=held.at[right, second], dst_ref=held.at[right, second],
        send_sem=f_ssem.at[1], recv_sem=f_rsem.at[1], device_id=(me, left), device_id_type=MESH)
    fwd_left.start()
    in_copy(left, second, 1).wait_recv()
    in_copy(right, first, 3).wait_recv()
    o_ref[...] += jnp.dot(held[left], w_ref[left], preferred_element_type=jnp.float32)
    o_ref[...] += jnp.dot(held[right], w_ref[right], preferred_element_type=jnp.float32)
    far_first = pltpu.make_async_remote_copy(
        src_ref=held.at[far, pl.ds(0, half)], dst_ref=held.at[far, pl.ds(0, half)],
        send_sem=f_ssem.at[0], recv_sem=f_rsem.at[0], device_id=(me, right), device_id_type=MESH)
    far_second = pltpu.make_async_remote_copy(
        src_ref=held.at[far, pl.ds(half, half)], dst_ref=held.at[far, pl.ds(half, half)],
        send_sem=f_ssem.at[1], recv_sem=f_rsem.at[1], device_id=(me, left), device_id_type=MESH)
    far_first.wait_recv()
    far_second.wait_recv()
    o_ref[...] += jnp.dot(held[far], w_ref[far], preferred_element_type=jnp.float32)
    for c in sends:
        c.wait_send()
    fwd_right.wait_send()
    fwd_left.wait_send()
    out_ref[...] = (o_ref[...] + res_ref[...].astype(jnp.float32)).astype(out_ref.dtype)


def gather_project(h, w_blocks, res, n_ten):
    vmem = pl.BlockSpec(memory_space=pltpu.VMEM)
    return pl.pallas_call(
        functools.partial(project_kernel, n_ten),
        out_shape=jax.ShapeDtypeStruct(res.shape, res.dtype),
        in_specs=[vmem, vmem, vmem],
        out_specs=vmem,
        scratch_shapes=[
            pltpu.VMEM(res.shape, jnp.float32),
            pltpu.VMEM((n_ten,) + h.shape, h.dtype),
            pltpu.SemaphoreType.DMA((4,)),
            pltpu.SemaphoreType.DMA((4,)),
            pltpu.SemaphoreType.DMA((2,)),
            pltpu.SemaphoreType.DMA((2,)),
        ],
        compiler_params=pltpu.CompilerParams(collective_id=3, has_side_effects=True),
    )(h, w_blocks, res)


def attn_kernel(scale, q_ref, meta_ref, pk_ref, pv_ref, ck_ref, cv_ref, nk_ref, nv_ref, o_ref):
    q = q_ref[...]
    meta = meta_ref[...]
    dims = (((1,), (1,)), ((), ()))

    def masked(keys, lo, hi):
        s = lax.dot_general(q, keys, dims, preferred_element_type=jnp.float32) * scale
        k = lax.broadcasted_iota(jnp.int32, s.shape, 1)
        return jnp.where((k >= lo) & (k < hi), s, -jnp.inf)

    s_pre = masked(pk_ref[...], meta[:, 0:1], meta[:, 1:2])
    s_old = masked(ck_ref[...], meta[:, 2:3], meta[:, 3:4])
    s_new = masked(nk_ref[...], meta[:, 4:5], meta[:, 5:6])
    top = jnp.maximum(
        jnp.maximum(jnp.max(s_pre, axis=1, keepdims=True), jnp.max(s_old, axis=1, keepdims=True)),
        jnp.max(s_new, axis=1, keepdims=True),
    )
    e_pre = jnp.exp(s_pre - top)
    e_old = jnp.exp(s_old - top)
    e_new = jnp.exp(s_new - top)
    total = (
        jnp.sum(e_pre, axis=1, keepdims=True)
        + jnp.sum(e_old, axis=1, keepdims=True)
        + jnp.sum(e_new, axis=1, keepdims=True)
    )
    w_pre = (e_pre / total).astype(jnp.bfloat16)
    w_old = (e_old / total).astype(jnp.bfloat16)
    w_new = (e_new / total).astype(jnp.bfloat16)
    out = jnp.dot(w_pre, pv_ref[...], preferred_element_type=jnp.float32)
    out = out + jnp.dot(w_old, cv_ref[...], preferred_element_type=jnp.float32)
    out = out + jnp.dot(w_new, nv_ref[...], preferred_element_type=jnp.float32)
    alive = meta[:, 6:7].astype(jnp.float32)
    o_ref[...] = (out * alive).astype(o_ref.dtype)


def attend_kernel_call(q2, meta, pk, pv, ck2, cv2, nk2, nv2, rows_per_block, q_per_row, old_per_row, new_per_row):
    n_q, width = q2.shape
    qb = rows_per_block * q_per_row
    ob = rows_per_block * old_per_row
    nb = rows_per_block * new_per_row
    full = lambda i: (0, 0)
    return pl.pallas_call(
        functools.partial(attn_kernel, 1.0 / math.sqrt(HEAD_DIM)),
        out_shape=jax.ShapeDtypeStruct((n_q, width), jnp.bfloat16),
        grid=(n_q // qb,),
        in_specs=[
            pl.BlockSpec((qb, width), lambda i: (i, 0)),
            pl.BlockSpec((qb, meta.shape[1]), lambda i: (i, 0)),
            pl.BlockSpec(pk.shape, full),
            pl.BlockSpec(pv.shape, full),
            pl.BlockSpec((ob, width), lambda i: (i, 0)),
            pl.BlockSpec((ob, width), lambda i: (i, 0)),
            pl.BlockSpec((nb, width), lambda i: (i, 0)),
            pl.BlockSpec((nb, width), lambda i: (i, 0)),
        ],
        out_specs=pl.BlockSpec((qb, width), lambda i: (i, 0)),
    )(q2, meta, pk, pv, ck2, cv2, nk2, nv2)


def attend_fused(q, nk, nv, slot_keys, slot_values, slot_of_row, slot_len, old_keys, old_values, old_len, alive, rows_per_block=8):
    rows, steps = q.shape[0], q.shape[1]
    groups = q.shape[2] // HEAD_DIM
    n_slots, pre_max = slot_keys.shape[0], slot_keys.shape[1]
    old_max = old_keys.shape[1]
    local = jnp.arange(rows, dtype=jnp.int32) % rows_per_block
    lo_pre = slot_of_row * pre_max
    hi_pre = lo_pre + slot_len[slot_of_row]
    lo_old = local * old_max
    hi_old = lo_old + old_len
    lo_new = local * steps
    step_id = jnp.arange(steps * groups, dtype=jnp.int32) // groups
    per_row = jnp.stack([lo_pre, hi_pre, lo_old, hi_old, lo_new, alive, alive, alive], axis=1)
    meta = jnp.broadcast_to(per_row[:, None, :], (rows, steps * groups, 8))
    hi_new = lo_new[:, None] + step_id[None, :] + 1
    meta = meta.at[:, :, 5].set(hi_new)
    meta = meta.reshape(rows * steps * groups, 8)
    out = attend_kernel_call(
        q.reshape(rows * steps * groups, HEAD_DIM),
        meta,
        slot_keys.reshape(n_slots * pre_max, HEAD_DIM),
        slot_values.reshape(n_slots * pre_max, HEAD_DIM),
        old_keys.reshape(rows * old_max, HEAD_DIM),
        old_values.reshape(rows * old_max, HEAD_DIM),
        nk.reshape(rows * steps, HEAD_DIM),
        nv.reshape(rows * steps, HEAD_DIM),
        rows_per_block, steps * groups, old_max, steps,
    )
    return out.reshape(rows, steps, groups * HEAD_DIM)


def body(
    residual,
    queries,
    new_keys,
    new_values,
    cache_keys,
    cache_values,
    cache_lengths,
    finished,
    partner,
    row_slot,
    fork_table,
    prompt_keys,
    prompt_values,
    prompt_lengths,
    out_proj,
):
    local_rows = queries.shape[0]
    peer_count = lax.axis_size("replica")
    where_am = lax.axis_index("replica")
    first_id = where_am * local_rows
    held_count = prompt_keys.shape[0]

    owners = fork_table // held_count
    chosen = owners == where_am
    offsets = jnp.sum(jnp.where(chosen, fork_table % held_count, 0), axis=1)
    has_block = jnp.any(chosen, axis=1)[:, None, None]
    zero_value = jnp.zeros((), prompt_keys.dtype)
    both = jnp.concatenate([prompt_keys, prompt_values], axis=2)
    out_both = jnp.where(has_block, both[offsets], zero_value)
    got_both = lax.all_to_all(out_both, "replica", split_axis=0, concat_axis=0, tiled=True)
    n_ten = lax.axis_size("tensor")
    proj_blocks = exchange_weights(out_proj, n_ten)
    got_both, proj_blocks = lax.optimization_barrier((got_both, proj_blocks))
    my_owners = owners[where_am]
    slot_both = got_both[my_owners]
    slot_keys = slot_both[..., : prompt_keys.shape[2]]
    slot_values = slot_both[..., prompt_keys.shape[2] :]
    slot_len = prompt_lengths[fork_table[where_am]]

    peer_of = partner // local_rows
    moved_row = peer_of != where_am
    pairing = (peer_of[None, :] == jnp.arange(peer_count, dtype=jnp.int32)[:, None]) & moved_row[
        None, :
    ]
    peer_row = jnp.sum(
        jnp.where(pairing, jnp.arange(local_rows, dtype=jnp.int32)[None, :], 0), axis=1
    )
    has_row = jnp.any(pairing, axis=1)[:, None, None]
    from_peer = jnp.where(moved_row, peer_of, 0)
    keep_mask = moved_row[:, None, None]
    packed = jnp.concatenate([queries, new_keys, new_values], axis=2)
    outgoing = jnp.where(has_row, packed[peer_row], jnp.zeros((), packed.dtype))
    received = lax.all_to_all(outgoing, "replica", split_axis=0, concat_axis=0, tiled=True)
    use_packed = jnp.where(keep_mask, received[from_peer], packed)
    q_width = queries.shape[2]
    kv_width = new_keys.shape[2]
    use_q = use_packed[..., :q_width]
    use_nk = use_packed[..., q_width : q_width + kv_width]
    use_nv = use_packed[..., q_width + kv_width :]

    own_ids = first_id + jnp.arange(local_rows, dtype=jnp.int32)
    slot_of_row = row_slot[own_ids]
    old_len = cache_lengths[own_ids]
    alive = 1 - finished[own_ids]
    cache_side = attend_fused(
        use_q,
        use_nk,
        use_nv,
        slot_keys,
        slot_values,
        slot_of_row,
        slot_len,
        cache_keys,
        cache_values,
        old_len,
        alive,
    )

    back = jnp.where(has_row, cache_side[peer_row], jnp.zeros((), cache_side.dtype))
    returned = lax.all_to_all(back, "replica", split_axis=0, concat_axis=0, tiled=True)
    heads_out = jnp.where(keep_mask, returned[from_peer], cache_side)

    flat_heads = heads_out.reshape(-1, heads_out.shape[2])
    flat_res = residual.reshape(-1, residual.shape[2])
    return gather_project(flat_heads, proj_blocks, flat_res, n_ten).reshape(residual.shape)


def solution(mesh):
    in_specs = (
        P("replica", None, "tensor"),
        P("replica", None, "tensor"),
        P("replica", None, "tensor"),
        P("replica", None, "tensor"),
        P("replica", None, "tensor"),
        P("replica", None, "tensor"),
        P(),
        P(),
        P("replica"),
        P(),
        P(),
        P("replica", None, "tensor"),
        P("replica", None, "tensor"),
        P(),
        P("tensor", None),
    )
    out_specs = P("replica", None, "tensor")
    return jax.shard_map(body, mesh=mesh, in_specs=in_specs, out_specs=out_specs, check_vma=False)
```
